32 devices in a mesh: key: 4 (over x, core), head: 4 (over z), query: 2 (over y).
Axes of the slice: x: 2, y: 2, z: 4, core: 2. Of those that a mesh axis runs over, the one named last changes fastest.
Arguments:
- main_query: bfloat16 [4, 256, 24576], P(None, 'query', 'head'), may hold values from -64 to 64
- key_nope: bfloat16 [2048, 16384], P('key', 'head'), may hold values from -4 to 4
- key_rope: bfloat16 [2048, 64], P('key'), may hold values from -4 to 4
- query_pos: int32 [4, 256], P(None, 'query'), may hold values from 0 to 131071, as said below
- key_pos: int32 [2048], P('key'), may hold values from 0 to 131071, as said below
- key_count: int32 [64], P('key'), may hold values from 1 to 32, as said below
- index_query: bfloat16 [1024, 8192], P(('head', 'query')), may hold values from -16 to 16
- index_key: bfloat16 [2048, 128], P('key'), may hold values from -4 to 4
- index_weight: bfloat16 [1024, 64], P(('head', 'query')), may hold values from -0.5 to 0.5
- row_cotangent: float32 [1024], P(('head', 'query')), may hold values from 512 to 4096
Outputs:
- kl_rows: float32 [1024], P(('head', 'query'))
- grad_index_query: float32 [1024, 8192], P(('head', 'query'), 'key')
- grad_index_key: float32 [2048, 128], P('key')
The draws below stay inside these ranges and needn't reach their ends.
Inputs may be any that keep to these rules, and one draw needn't show every extreme that they name: `query_pos`: increasing along the flattened order, distinct; the first query is at position 0 and the last at position 131071. `key_pos`: increasing, distinct; the first key is at position 0. `key_count`: some block is full and some block holds one live key.
All inputs are finite; a program needn't handle non-finite values.
Results may differ from the reference program's by a relative error of at most 0.002.
Values sent between devices are 32-bit elements; how exact they have to be, the bound alone decides.
No kernel may reach another device: no remote copies, remote signals or barrier semaphores. Data moves between devices by JAX's collectives and lax.ppermute only.
A program may use at most 128 MiB of HBM per device.

```python
import math
import jax
import jax.numpy as jnp
from jax import lax

H = 128
DNOPE = 128
DROPE = 64
IH = 64
ID = 128
QROWS_DEV = 128
KBLOCK = 32
CONTEXT = 131072
DQK = 192
TQ = 1024
TK = 2048
QGROUPS = 4
KB = 64


weight_spread = 0.125


def drawn_normal(key, code, shape, spread):
    return jnp.clip(jax.random.normal(jax.random.fold_in(key, code), shape, jnp.float32), -4.0, 4.0) * spread


def draw_main_query(key, part):
    values = drawn_normal(key, 11, (TQ, H * DQK), 1.0)
    return values.reshape(QGROUPS, TQ // QGROUPS, H * DQK).astype(jnp.bfloat16)


def draw_key_nope(key, part):
    values = drawn_normal(key, 12, (TK, H * DNOPE), 1.0)
    return values.astype(jnp.bfloat16)


def draw_key_rope(key, part):
    values = drawn_normal(key, 13, (TK, DROPE), 1.0)
    return values.astype(jnp.bfloat16)


def draw_index_query(key, part):
    values = drawn_normal(key, 14, (TQ, IH * ID), 1.0)
    return values.astype(jnp.bfloat16)


def draw_index_key(key, part):
    values = drawn_normal(key, 15, (TK, ID), 1.0)
    return values.astype(jnp.bfloat16)


def draw_index_weight(key, part):
    values = drawn_normal(key, 16, (TQ, IH), weight_spread)
    return values.astype(jnp.bfloat16)


def draw_query_pos(key, part):
    picks = jax.random.permutation(jax.random.fold_in(key, 21), CONTEXT - 2)[:TQ - 2] + 1
    ordered = jnp.sort(picks).astype(jnp.int32)
    full = jnp.concatenate([jnp.array([0], jnp.int32), ordered, jnp.array([CONTEXT - 1], jnp.int32)])
    return full.reshape(QGROUPS, TQ // QGROUPS)


def draw_key_pos(key, part):
    picks = jax.random.permutation(jax.random.fold_in(key, 22), CONTEXT - 1)[:TK - 1] + 1
    ordered = jnp.sort(picks).astype(jnp.int32)
    return jnp.concatenate([jnp.array([0], jnp.int32), ordered])


def draw_key_count(key, part):
    base = jax.random.fold_in(key, 23)
    counts = jax.random.randint(jax.random.fold_in(base, 1), (KB,), 1, KBLOCK + 1).astype(jnp.int32)
    full_at = jax.random.randint(jax.random.fold_in(base, 2), (), 0, KB)
    single_at = (full_at + 1 + jax.random.randint(jax.random.fold_in(base, 3), (), 0, KB - 1)) % KB
    counts = counts.at[full_at].set(KBLOCK).at[single_at].set(1)
    return counts.astype(jnp.int32)


def steps_of(stream_key, dims, shards, least, top_value):
    loudness, own = 1.0, jax.random.fold_in(stream_key, 6)
    for axis_at, parts in shards:
        heights = jnp.exp(jax.random.uniform(jax.random.fold_in(own, axis_at), (parts,), jnp.float32, least / len(shards), top_value / len(shards)))
        loudness = loudness * jnp.repeat(heights, dims[axis_at] // parts).reshape([-1 if axis == axis_at else 1 for axis in range(len(dims))])
    return loudness


def setup_inputs(seed: int = 0) -> dict:
    seeds = jax.random.split(jax.random.key(seed), 11)
    return {
        "main_query": draw_main_query(jax.random.fold_in(seeds[10], 71), 0),
        "key_nope": draw_key_nope(jax.random.fold_in(seeds[10], 71), 0),
        "key_rope": draw_key_rope(jax.random.fold_in(seeds[10], 71), 0),
        "query_pos": draw_query_pos(jax.random.fold_in(seeds[10], 71), 0),
        "key_pos": draw_key_pos(jax.random.fold_in(seeds[10], 71), 0),
        "key_count": draw_key_count(jax.random.fold_in(seeds[10], 71), 0),
        "index_query": draw_index_query(jax.random.fold_in(seeds[10], 71), 0),
        "index_key": draw_index_key(jax.random.fold_in(seeds[10], 71), 0),
        "index_weight": draw_index_weight(jax.random.fold_in(seeds[10], 71), 0),
        "row_cotangent": jnp.clip(jnp.exp(math.log(4096.0) - 2.0794415 * jax.random.uniform(seeds[9], (TQ,), jnp.float32) ** steps_of(seeds[9], (TQ,), ((0, 8),), -0.2, 0.2)), 512.0, 4096.0),
    }


neg_big = -1.0e30


def reference(main_query, key_nope, key_rope, query_pos, key_pos, key_count, index_query, index_key, index_weight, row_cotangent):
    f32 = jnp.float32
    q_all = main_query.reshape(TQ, H, DQK).astype(f32)
    k_nope = key_nope.reshape(TK, H, DNOPE).astype(f32)
    k_rope = key_rope.astype(f32)
    positions = query_pos.reshape(TQ)
    slots = jnp.arange(TK, dtype=jnp.int32) % KBLOCK
    counts = jnp.repeat(key_count, KBLOCK, total_repeat_length=TK)
    key_live = slots < counts
    iq_all = index_query.reshape(TQ, IH, ID).astype(f32)
    ik_all = index_key.astype(f32)
    weights = index_weight.astype(f32)
    scale_main = DQK ** -0.5
    scale_index = ID ** -0.5
    blocks = TQ // QROWS_DEV

    def step(grad_key, block):
        start = (block * QROWS_DEV).astype(jnp.int32)
        q_rows = lax.dynamic_slice_in_dim(q_all, start, QROWS_DEV, 0)
        pos_rows = lax.dynamic_slice_in_dim(positions, start, QROWS_DEV, 0)
        iq_rows = lax.dynamic_slice_in_dim(iq_all, start, QROWS_DEV, 0)
        w_rows = lax.dynamic_slice_in_dim(weights, start, QROWS_DEV, 0)
        cot_rows = lax.dynamic_slice_in_dim(row_cotangent, start, QROWS_DEV, 0)
        valid = (key_pos[None, :] <= pos_rows[:, None]) & key_live[None, :]
        scores = (jnp.einsum('thd,khd->htk', q_rows[:, :, :DNOPE], k_nope)
                  + jnp.einsum('thd,kd->htk', q_rows[:, :, DNOPE:], k_rope)) * scale_main
        top = jnp.max(jnp.where(valid[None], scores, neg_big), axis=-1)
        expo = jnp.where(valid[None], jnp.exp(scores - top[..., None]), 0.0)
        total = jnp.sum(expo, axis=-1)
        probs = expo / total[..., None]
        target = jnp.sum(probs, axis=0) / H
        z_vals = jnp.einsum('tjd,kd->tjk', iq_rows, ik_all)
        logits = scale_index * jnp.sum(jnp.maximum(z_vals, 0.0) * w_rows[:, :, None], axis=1)
        lmax = jnp.max(jnp.where(valid, logits, neg_big), axis=-1)
        lsum = jnp.sum(jnp.where(valid, jnp.exp(logits - lmax[:, None]), 0.0), axis=-1)
        lse = lmax + jnp.log(lsum)
        qprob = jnp.where(valid, jnp.exp(logits - lse[:, None]), 0.0)
        safe = jnp.where(target > 0, target, 1.0)
        entropy = jnp.sum(jnp.where(target > 0, target * jnp.log(safe), 0.0), axis=-1)
        cross = jnp.sum(jnp.where(valid, target * logits, 0.0), axis=-1)
        kl = entropy - cross + lse
        grad_logits = cot_rows[:, None] * (qprob - target)
        positive = (z_vals > 0).astype(f32)
        dz_vals = ((scale_index * grad_logits)[:, None, :] * w_rows[:, :, None] * positive).astype(jnp.bfloat16).astype(f32)
        grad_rows = jnp.einsum('tjk,kd->tjd', dz_vals, ik_all).reshape(QROWS_DEV, IH * ID)
        grad_key = grad_key + jnp.einsum('tjk,tjd->kd', dz_vals, iq_rows)
        return grad_key, (kl, grad_rows)

    grad_key, outs = lax.scan(step, jnp.zeros((TK, ID), f32), jnp.arange(blocks, dtype=jnp.int32))
    kl_rows = outs[0].reshape(TQ)
    grad_query = outs[1].reshape(TQ, IH * ID)
    return kl_rows, grad_query, grad_key
```

```python
import functools
import math
import jax
import jax.numpy as jnp
from jax import lax
from jax.experimental import pallas as pl
from jax.experimental.pallas import tpu as pltpu
from jax.sharding import PartitionSpec as P

H = 128
DNOPE = 128
DROPE = 64
IH = 64
ID = 128
KBLOCK = 32
DQK = 192
LANES = 128
PAIR = 2 * DQK
NEG = -1e30
BIG = 2**30
LOG2E = math.log2(math.e)
SCALE_MAIN = DQK ** (-0.5) * LOG2E
SCALE_INDEX = ID ** (-0.5)
VMEM_LIMIT = 60 * 1024 * 1024

f32 = jnp.float32
bf16 = jnp.bfloat16


def dot_nt(a, b):
    return lax.dot_general(a, b, (((1,), (1,)), ((), ())), preferred_element_type=f32)


def dot_nn(a, b):
    return lax.dot_general(a, b, (((1,), (0,)), ((), ())), preferred_element_type=f32)


def params(*semantics):
    return pltpu.CompilerParams(
        dimension_semantics=semantics, vmem_limit_bytes=VMEM_LIMIT
    )


def cost(flops, bytes_accessed, transcendentals=0):
    return pl.CostEstimate(
        flops=int(flops), bytes_accessed=int(bytes_accessed), transcendentals=int(transcendentals)
    )


def key_limit_column(count_ref, pos_ref, keys):
    blocks = keys // KBLOCK
    lane = lax.broadcasted_iota(jnp.int32, (1, keys), 1)
    block = lane // KBLOCK
    limit = jnp.zeros((1, keys), jnp.int32)
    for b in range(blocks):
        limit = jnp.where(block == b, count_ref[b], limit)
    live = (lane % KBLOCK) < limit
    row = jnp.where(live, pos_ref[...], BIG)
    return jnp.transpose(jnp.broadcast_to(row, (8, keys)))[:, :1]


def main_keys(kn_ref, rope, parity):
    keys = rope.shape[0]
    zero = jnp.zeros((keys, DROPE), bf16)
    if parity == 0:
        return jnp.concatenate([kn_ref[:, :DNOPE], rope, zero], axis=1)
    return jnp.concatenate([zero, kn_ref[:, DNOPE:], rope], axis=1)


def stats_kernel(count_ref, q_ref, kn_ref, rope_ref, qpos_ref, kpos_ref, lse_ref, bias_ref):
    step = pl.program_id(0)
    keys = kn_ref.shape[0]
    groups, rows = q_ref.shape[0], q_ref.shape[1]

    @pl.when(step == 0)
    def _():
        column = key_limit_column(count_ref, kpos_ref, keys)
        for g in range(groups):
            valid = column <= qpos_ref[g : g + 1, :]
            bias_ref[:, g * rows : (g + 1) * rows] = jnp.where(valid, 0.0, NEG)

    rope = rope_ref[...]
    for parity in range(2):
        kk = main_keys(kn_ref, rope, parity)
        head = 2 * step + parity
        for c in range(groups // 2):
            q = q_ref[2 * c : 2 * c + 2, :, parity * LANES : parity * LANES + 2 * LANES]
            q = q.reshape(2 * rows, 2 * LANES)
            cols = slice(2 * c * rows, (2 * c + 2) * rows)
            s = dot_nt(kk, q) * SCALE_MAIN + bias_ref[:, cols]
            top = jnp.max(s, axis=0, keepdims=True)
            total = jnp.sum(jnp.exp2(s - top), axis=0, keepdims=True)
            lse_ref[pl.ds(head, 1), cols] = top + jnp.log2(total)


def main_stats(main_query, key_nope, key_rope, query_pos, key_pos, key_count):
    groups, rows, width = main_query.shape
    heads = width // DQK
    keys = key_nope.shape[0]
    total = groups * rows
    return pl.pallas_call(
        stats_kernel,
        grid_spec=pltpu.PrefetchScalarGridSpec(
            num_scalar_prefetch=1,
            grid=(heads // 2,),
            in_specs=[
                pl.BlockSpec((groups, rows, PAIR), lambda i, c: (0, 0, i)),
                pl.BlockSpec((keys, 2 * DNOPE), lambda i, c: (0, i)),
                pl.BlockSpec((keys, DROPE), lambda i, c: (0, 0)),
                pl.BlockSpec((groups, rows), lambda i, c: (0, 0)),
                pl.BlockSpec((1, keys), lambda i, c: (0, 0)),
            ],
            out_specs=pl.BlockSpec((heads, total), lambda i, c: (0, 0)),
            scratch_shapes=[pltpu.VMEM((keys, total), f32)],
        ),
        out_shape=jax.ShapeDtypeStruct((heads, total), f32),
        compiler_params=params("arbitrary"),
        cost_estimate=cost(
            heads * total * keys * 512, main_query.size * 2 + key_nope.size * 2, heads * total * keys
        ),
        name="main_stats",
    )(key_count, main_query, key_nope, key_rope, query_pos, key_pos.reshape(1, keys))


def target_kernel(n_lse, n_groups, count_ref, grp_ref, *refs):
    q_refs = refs[:n_groups]
    kn_ref, rope_ref, qpos_ref, kpos_ref = refs[n_groups : n_groups + 4]
    lse_refs = refs[n_groups + 4 : n_groups + 4 + n_lse * n_groups]
    out_refs = refs[n_groups + 4 + n_lse * n_groups : -1]
    glob_ref = refs[-1]
    step = pl.program_id(0)
    keys = kn_ref.shape[0]
    rows = q_refs[0].shape[1]

    @pl.when(step == 0)
    def _():
        for g in range(n_groups):
            parts = [r[...] for r in lse_refs[g * n_lse : (g + 1) * n_lse]]
            top = functools.reduce(jnp.maximum, parts)
            total = functools.reduce(jnp.add, [jnp.exp2(p - top) for p in parts])
            glob_ref[:, g * rows : (g + 1) * rows] = top + jnp.log2(total)
            out_refs[g][...] = jnp.zeros_like(out_refs[g])

    rope = rope_ref[...]
    acc = None
    for parity in range(2):
        kk = main_keys(kn_ref, rope, parity)
        lanes = slice(parity * LANES, parity * LANES + 2 * LANES)
        qs = [r[0, :, lanes] for r in q_refs]
        q = qs[0] if n_groups == 1 else jnp.concatenate(qs, axis=0)
        lse = glob_ref[pl.ds(2 * step + parity, 1), :]
        e = jnp.exp2(dot_nt(kk, q) * SCALE_MAIN - lse)
        acc = e if acc is None else acc + e
    for g in range(n_groups):
        out_refs[g][...] += acc[:, g * rows : (g + 1) * rows]

    @pl.when(step == pl.num_programs(0) - 1)
    def _():
        column = key_limit_column(count_ref, kpos_ref, keys)
        for g in range(n_groups):
            valid = column <= qpos_ref[pl.ds(grp_ref[g], 1), :]
            out_refs[g][...] = jnp.where(valid, out_refs[g][...], 0.0)


def head_sums(group_ids, main_query, key_nope, key_rope, query_pos, key_pos, key_count, lses):
    groups, rows, width = main_query.shape
    heads = width // DQK
    keys = key_nope.shape[0]
    n = len(group_ids)

    def group_q(g):
        return pl.BlockSpec((1, rows, PAIR), lambda i, c, grp: (grp[g], 0, i))

    def group_lse(g):
        return pl.BlockSpec((heads, rows), lambda i, c, grp: (0, grp[g]))

    return pl.pallas_call(
        functools.partial(target_kernel, len(lses), n),
        grid_spec=pltpu.PrefetchScalarGridSpec(
            num_scalar_prefetch=2,
            grid=(heads // 2,),
            in_specs=[group_q(g) for g in range(n)]
            + [
                pl.BlockSpec((keys, 2 * DNOPE), lambda i, c, grp: (0, i)),
                pl.BlockSpec((keys, DROPE), lambda i, c, grp: (0, 0)),
                pl.BlockSpec((groups, rows), lambda i, c, grp: (0, 0)),
                pl.BlockSpec((1, keys), lambda i, c, grp: (0, 0)),
            ]
            + [group_lse(g) for g in range(n) for _ in lses],
            out_specs=[pl.BlockSpec((keys, rows), lambda i, c, grp: (0, 0))] * n,
            scratch_shapes=[pltpu.VMEM((heads, n * rows), f32)],
        ),
        out_shape=[jax.ShapeDtypeStruct((keys, rows), f32)] * n,
        compiler_params=params("arbitrary"),
        cost_estimate=cost(
            heads * n * rows * keys * 512, main_query.size * n // 2 + key_nope.size * 2,
            heads * n * rows * keys,
        ),
        name="head_sums",
    )(
        key_count,
        jnp.stack(group_ids),
        *([main_query] * n),
        key_nope,
        key_rope,
        query_pos,
        key_pos.reshape(1, keys),
        *(list(lses) * n),
    )


def logits_kernel(count_ref, grp_ref, iq_ref, ik_ref, w_ref, qpos_ref, kpos_ref,
                  logits_ref, lse_ref, wm_ref, wt_ref):
    step = pl.program_id(0)
    keys = ik_ref.shape[0]
    rows = iq_ref.shape[0]
    per = iq_ref.shape[1] // ID

    @pl.when(step == 0)
    def _():
        wt_ref[...] = jnp.transpose(w_ref[...].astype(f32))
        logits_ref[...] = jnp.zeros_like(logits_ref)

    ik = ik_ref[...]
    total = None
    for p in range(per // 2):
        cols = [slice((2 * p + a) * ID, (2 * p + a + 1) * ID) for a in range(2)]
        q = jnp.concatenate([iq_ref[:, c] for c in cols], axis=0)
        z = dot_nt(ik, q)
        w = jnp.concatenate(
            [wt_ref[pl.ds(step * per + 2 * p + a, 1), :] for a in range(2)], axis=1
        )
        positive = z > 0
        masked = jnp.where(positive, w, 0.0)
        wm_ref[:, 2 * p * rows : (2 * p + 2) * rows] = masked.astype(bf16)
        r = z * masked
        r = r[:, :rows] + r[:, rows:]
        total = r if total is None else total + r
    logits_ref[...] += total

    @pl.when(step == pl.num_programs(0) - 1)
    def _():
        logits = logits_ref[...] * SCALE_INDEX
        logits_ref[...] = logits
        column = key_limit_column(count_ref, kpos_ref, keys)
        valid = column <= qpos_ref[pl.ds(grp_ref[0], 1), :]
        s = jnp.where(valid, logits * LOG2E, NEG)
        top = jnp.max(s, axis=0, keepdims=True)
        lse_ref[...] = top + jnp.log2(jnp.sum(jnp.exp2(s - top), axis=0, keepdims=True))


def index_logits(group_id, index_query, index_key, index_weight, query_pos, key_pos, key_count):
    rows, width = index_query.shape
    keys = index_key.shape[0]
    groups = query_pos.shape[0]
    per = 8
    steps = width // (per * ID)
    return pl.pallas_call(
        logits_kernel,
        grid_spec=pltpu.PrefetchScalarGridSpec(
            num_scalar_prefetch=2,
            grid=(steps,),
            in_specs=[
                pl.BlockSpec((rows, per * ID), lambda i, c, grp: (0, i)),
                pl.BlockSpec((keys, ID), lambda i, c, grp: (0, 0)),
                pl.BlockSpec((rows, width // ID), lambda i, c, grp: (0, 0)),
                pl.BlockSpec((groups, rows), lambda i, c, grp: (0, 0)),
                pl.BlockSpec((1, keys), lambda i, c, grp: (0, 0)),
            ],
            out_specs=[
                pl.BlockSpec((keys, rows), lambda i, c, grp: (0, 0)),
                pl.BlockSpec((1, rows), lambda i, c, grp: (0, 0)),
                pl.BlockSpec((keys, per * rows), lambda i, c, grp: (0, i)),
            ],
            scratch_shapes=[pltpu.VMEM((width // ID, rows), f32)],
        ),
        out_shape=[
            jax.ShapeDtypeStruct((keys, rows), f32),
            jax.ShapeDtypeStruct((1, rows), f32),
            jax.ShapeDtypeStruct((keys, (width // ID) * rows), bf16),
        ],
        compiler_params=params("arbitrary"),
        cost_estimate=cost(2 * keys * rows * width, rows * width * 2 + keys * rows * width // ID * 2),
        name="index_logits",
    )(key_count, group_id.reshape(1), index_query, index_key, index_weight, query_pos,
      key_pos.reshape(1, keys))


def combine_lse(parts):
    top = functools.reduce(jnp.maximum, parts)
    return top + jnp.log2(functools.reduce(jnp.add, [jnp.exp2(p - top) for p in parts]))


def grad_key_kernel(n_parts, n_lse, count_ref, grp_ref, *refs):
    parts = refs[:n_parts]
    lses = refs[n_parts : n_parts + n_lse]
    (logits_ref, cot_ref, qpos_ref, kpos_ref, wm_ref, iq_ref,
     sg_ref, gk_ref) = refs[n_parts + n_lse :]
    step = pl.program_id(0)
    keys, rows = logits_ref.shape
    per = iq_ref.shape[1] // ID

    @pl.when(step == 0)
    def _():
        column = key_limit_column(count_ref, kpos_ref, keys)
        valid = column <= qpos_ref[pl.ds(grp_ref[0], 1), :]
        target = functools.reduce(jnp.add, [p[...] for p in parts]) * (1.0 / H)
        logits = logits_ref[...]
        lse2 = combine_lse([r[...] for r in lses])
        qprob = jnp.where(valid, jnp.exp2(logits * LOG2E - lse2), 0.0)
        sg_ref[:keys, :] = SCALE_INDEX * (cot_ref[...] * (qprob - target))
        live = target > 0
        terms = jnp.where(live, target * (jnp.log(jnp.where(live, target, 1.0)) - logits), 0.0)
        kl = jnp.sum(terms, axis=0, keepdims=True)
        sg_ref[keys:, :] = jnp.broadcast_to(kl, (8, rows))
        gk_ref[...] = jnp.zeros_like(gk_ref)

    sg = sg_ref[:keys, :]
    total = None
    for p in range(per // 2):
        dz = []
        qs = []
        for a in range(2):
            j = 2 * p + a
            dz.append((sg * wm_ref[:, j * rows : (j + 1) * rows].astype(f32)).astype(bf16))
            qs.append(iq_ref[:, j * ID : (j + 1) * ID])
        t = dot_nn(jnp.concatenate(dz, axis=1), jnp.concatenate(qs, axis=0))
        total = t if total is None else total + t
    gk_ref[...] += total


def index_grad_key(group_id, parts, lses, logits, cotangent, wm, index_query,
                   query_pos, key_pos, key_count):
    rows, width = index_query.shape
    keys = logits.shape[0]
    groups = query_pos.shape[0]
    per = 8
    steps = width // (per * ID)
    whole = lambda i, c, grp: (0, 0)
    return pl.pallas_call(
        functools.partial(grad_key_kernel, len(parts), len(lses)),
        grid_spec=pltpu.PrefetchScalarGridSpec(
            num_scalar_prefetch=2,
            grid=(steps,),
            in_specs=[pl.BlockSpec((keys, rows), whole) for _ in parts]
            + [pl.BlockSpec((1, rows), whole) for _ in lses]
            + [
                pl.BlockSpec((keys, rows), whole),
                pl.BlockSpec((1, rows), whole),
                pl.BlockSpec((groups, rows), whole),
                pl.BlockSpec((1, keys), whole),
                pl.BlockSpec((keys, per * rows), lambda i, c, grp: (0, i)),
                pl.BlockSpec((rows, per * ID), lambda i, c, grp: (0, i)),
            ],
            out_specs=[
                pl.BlockSpec((keys + 8, rows), whole),
                pl.BlockSpec((keys, ID), whole),
            ],
        ),
        out_shape=[
            jax.ShapeDtypeStruct((keys + 8, rows), f32),
            jax.ShapeDtypeStruct((keys, ID), f32),
        ],
        compiler_params=params("arbitrary"),
        cost_estimate=cost(2 * keys * rows * width, rows * width * 2 + keys * rows * width // ID * 2),
        name="index_grad_key",
    )(key_count, group_id.reshape(1), *parts, *lses, logits, cotangent.reshape(1, rows),
      query_pos, key_pos.reshape(1, keys), wm, index_query)


def grad_query_kernel(n_shards, first, slot_ref, *refs):
    sgs = refs[:n_shards]
    iks = refs[n_shards : 2 * n_shards]
    iq_ref, w_ref = refs[2 * n_shards : 2 * n_shards + 2]
    rest = refs[2 * n_shards + 2 :]
    if first:
        gq_ref, kl_ref = rest
    else:
        gq_in_ref, kl_in_ref, gq_ref, kl_ref = rest
    rows = iq_ref.shape[0]
    heads = iq_ref.shape[1] // ID
    keys = iks[0].shape[0]
    weights = w_ref[...].astype(f32)
    col = lax.broadcasted_iota(jnp.int32, weights.shape, 1)
    base = slot_ref[0] * heads
    iq = jnp.concatenate([iq_ref[:, j * ID : (j + 1) * ID] for j in range(heads)], axis=0)
    ws = [
        jnp.sum(jnp.where(col == base + j, weights, 0.0), axis=1, keepdims=True)
        for j in range(heads)
    ]
    kl = functools.reduce(jnp.add, [s[keys : keys + 1, :] for s in sgs])
    kl_ref[...] = kl if first else kl_in_ref[...] + kl
    out = None
    for s_ref, ik_ref in zip(sgs, iks):
        ik = ik_ref[...].astype(bf16)
        sgt = jnp.transpose(s_ref[:keys, :])
        z = dot_nt(iq, ik)
        dz = jnp.concatenate(
            [
                jnp.where(z[j * rows : (j + 1) * rows] > 0, sgt * ws[j], 0.0).astype(bf16)
                for j in range(heads)
            ],
            axis=0,
        )
        g = dot_nn(dz, ik)
        out = g if out is None else out + g
    for j in range(heads):
        cols = slice(j * ID, (j + 1) * ID)
        g = out[j * rows : (j + 1) * rows]
        gq_ref[:, cols] = g if first else gq_in_ref[:, cols] + g


def index_grad_query(slot, n_slots, sgs, iks, index_query, index_weight, carry):
    rows, width = index_query.shape
    heads = width // ID
    mine = width // n_slots
    keys = iks[0].shape[0]
    whole = lambda i, s: (0, 0)
    first = carry is None
    carried = [] if first else list(carry)
    n = len(sgs)
    return pl.pallas_call(
        functools.partial(grad_query_kernel, n, first),
        grid_spec=pltpu.PrefetchScalarGridSpec(
            num_scalar_prefetch=1,
            grid=(1,),
            in_specs=[pl.BlockSpec((keys + 8, rows), whole) for _ in sgs]
            + [pl.BlockSpec((keys, ID), whole) for _ in iks]
            + [
                pl.BlockSpec((rows, mine), lambda i, s: (0, s[0])),
                pl.BlockSpec((rows, heads), whole),
            ]
            + ([] if first else [pl.BlockSpec((rows, mine), whole), pl.BlockSpec((1, rows), whole)]),
            out_specs=[pl.BlockSpec((rows, mine), whole), pl.BlockSpec((1, rows), whole)],
        ),
        out_shape=[
            jax.ShapeDtypeStruct((rows, mine), f32),
            jax.ShapeDtypeStruct((1, rows), f32),
        ],
        compiler_params=params("arbitrary"),
        cost_estimate=cost(4 * n * keys * rows * mine, n * (keys * ID * 8) + rows * mine * 8),
        name="index_grad_query",
    )(slot.reshape(1), *sgs, *iks, index_query, index_weight, *carried)


def swap(value, axis, mask, size):
    return lax.ppermute(value, axis, [(i, i ^ mask) for i in range(size)])


def rotate(value, axis, by, size):
    return lax.ppermute(value, axis, [(i, (i + by) % size) for i in range(size)])


def summed_copies(value, n_head, n_query):
    steps = [("query", m, n_query) for m in (1 << b for b in range(n_query.bit_length() - 1))]
    steps += [("head", (2 << b) - 1, n_head) for b in range(n_head.bit_length() - 1)]
    count = len(steps)
    if count == 0:
        return value
    rows = value.shape[0]
    unit = -(-rows // (8 * count)) * 8
    pieces = [value[i * unit : min((i + 1) * unit, rows)] for i in range(count)]
    pieces = [p for p in pieces if p.shape[0]]
    for s in range(count):
        moved = [swap(p, *steps[(i + s) % count]) for i, p in enumerate(pieces)]
        pieces = [p + m for p, m in zip(pieces, moved)]
    return jnp.concatenate(pieces, axis=0)


def body(n_key, n_head, n_query, main_query, key_nope, key_rope, query_pos, key_pos, key_count,
         index_query, index_key, index_weight, row_cotangent):
    groups, rows, _ = main_query.shape
    keys = key_nope.shape[0]
    z = lax.axis_index("head")
    slot = lax.axis_index("key")
    main = (main_query, key_nope, key_rope, query_pos, key_pos, key_count)

    lse = main_stats(*main)
    if n_key == 4:
        near = swap(lse, "key", 1, n_key)
        far = swap(lse, "key", 2, n_key)
        lses = [lse, near, far, swap(lse, "key", 3, n_key)]
    else:
        lses = [combine_lse(list(lax.all_gather(lse, "key")))]

    logits, index_lse, wm = index_logits(
        z, index_query, index_key, index_weight, query_pos, key_pos, key_count
    )
    index_lses = list(lax.all_gather(index_lse, "key")) if n_key != 4 else [index_lse] + [
        swap(index_lse, "key", m, n_key) for m in (1, 2, 3)
    ]
    if len(index_lses) > 4:
        index_lses = [combine_lse(index_lses)]

    if n_head == 4 and groups == 4:
        across = head_sums([(z + 2) % 4], *main, lses)[0]
        half = keys // 2
        low = rotate(across[:half], "head", 1, 4)
        high = rotate(across[half:], "head", 3, 4)
        up, down = head_sums([(z + 1) % 4, (z + 3) % 4], *main, lses)
        up = jnp.concatenate([up[:half] + low, up[half:]], axis=0)
        down = jnp.concatenate([down[:half], down[half:] + high], axis=0)
        from_below = rotate(up, "head", 1, 4)
        from_above = rotate(down, "head", 3, 4)
        own = head_sums([z], *main, lses)[0]
        parts = [own, from_below, from_above]
    else:
        tiles = jnp.stack([head_sums([jnp.int32(g)], *main, lses)[0] for g in range(groups)])
        parts = [lax.psum_scatter(tiles, "head", scatter_dimension=0, tiled=True)[0]]

    sg, grad_key = index_grad_key(
        z, parts, index_lses, logits, row_cotangent, wm, index_query, query_pos, key_pos, key_count
    )
    grad_key = summed_copies(grad_key, n_head, n_query)

    wide = index_key.astype(f32)
    if n_key == 4:
        ik_far = swap(wide, "key", 2, n_key)
        iks = [wide, swap(wide, "key", 1, n_key), ik_far, swap(ik_far, "key", 1, n_key)]
        sg_far = swap(sg, "key", 2, n_key)
        sgs = [sg, swap(sg, "key", 1, n_key), sg_far, swap(sg_far, "key", 1, n_key)]
        carry = None
        for lo in (0, 2):
            carry = index_grad_query(
                slot, n_key, sgs[lo : lo + 2], iks[lo : lo + 2], index_query, index_weight, carry
            )
    else:
        iks = list(lax.all_gather(wide, "key"))
        sgs = list(lax.all_gather(sg, "key"))
        carry = None
        for lo in range(0, n_key, 2):
            carry = index_grad_query(
                slot, n_key, sgs[lo : lo + 2], iks[lo : lo + 2], index_query, index_weight, carry
            )
    grad_query, kl = carry
    kl_rows = (kl + combine_lse(index_lses) * (1.0 / LOG2E)).reshape(rows)
    return kl_rows, grad_query, grad_key


def solution(mesh):
    return jax.shard_map(
        functools.partial(body, mesh.shape["key"], mesh.shape["head"], mesh.shape["query"]),
        mesh=mesh,
        in_specs=(
            P(None, "query", "head"),
            P("key", "head"),
            P("key", None),
            P(None, "query"),
            P("key"),
            P("key"),
            P(("head", "query"), None),
            P("key", None),
            P(("head", "query"), None),
            P(("head", "query")),
        ),
        out_specs=(P(("head", "query")), P(("head", "query"), "key"), P("key", None)),
        check_vma=False,
    )
```

```python
import functools
import math
import jax
import jax.numpy as jnp
from jax import lax
from jax.experimental import pallas as pl
from jax.experimental.pallas import tpu as pltpu
from jax.sharding import PartitionSpec as P

H = 128
DNOPE = 128
DROPE = 64
IH = 64
ID = 128
KBLOCK = 32
DQK = 192
LANES = 128
PAIR = 2 * DQK
NEG = -1e30
BIG = 2**30
LOG2E = math.log2(math.e)
SCALE_MAIN = DQK ** (-0.5) * LOG2E
SCALE_INDEX = ID ** (-0.5)
VMEM_LIMIT = 32 * 1024 * 1024

f32 = jnp.float32
bf16 = jnp.bfloat16
IN_VMEM = pl.BlockSpec(memory_space=pltpu.VMEM)


def dot_nt(a, b):
    return lax.dot_general(a, b, (((1,), (1,)), ((), ())), preferred_element_type=f32)


def dot_nn(a, b):
    return lax.dot_general(a, b, (((1,), (0,)), ((), ())), preferred_element_type=f32)


def params():
    return pltpu.CompilerParams(
        dimension_semantics=("arbitrary",), vmem_limit_bytes=VMEM_LIMIT
    )


def cost(flops, bytes_accessed, transcendentals=0):
    return pl.CostEstimate(
        flops=int(flops), bytes_accessed=int(bytes_accessed), transcendentals=int(transcendentals)
    )


def combine_lse(parts):
    if len(parts) == 1:
        return parts[0]
    top = functools.reduce(jnp.maximum, parts)
    return top + jnp.log2(functools.reduce(jnp.add, [jnp.exp2(p - top) for p in parts]))


def key_limit_column(count_ref, pos_ref, keys):
    blocks = keys // KBLOCK
    lane = lax.broadcasted_iota(jnp.int32, (1, keys), 1)
    block = lane // KBLOCK
    limit = jnp.zeros((1, keys), jnp.int32)
    for b in range(blocks):
        limit = jnp.where(block == b, count_ref[b], limit)
    live = (lane % KBLOCK) < limit
    row = jnp.where(live, pos_ref[...], BIG)
    return jnp.transpose(jnp.broadcast_to(row, (8, keys)))[:, :1]


def rope_setup(rope_t_ref, even_ref, odd_ref):
    rope = jnp.transpose(rope_t_ref[...].astype(f32)).astype(bf16)
    zero = jnp.zeros_like(rope)
    even_ref[...] = jnp.concatenate([rope, zero], axis=1)
    odd_ref[...] = jnp.concatenate([zero, rope], axis=1)


def main_keys(nope, parity, even_ref, odd_ref):
    if parity == 0:
        return jnp.concatenate([nope, even_ref[...]], axis=1)
    turned = jnp.concatenate([nope[:, DROPE:], nope[:, :DROPE]], axis=1)
    low = lax.broadcasted_iota(jnp.int32, turned.shape, 1) < DROPE
    first = jnp.where(low, jnp.zeros_like(turned), turned)
    second = jnp.where(low, turned, odd_ref[...])
    return jnp.concatenate([first, second], axis=1)


def stats_kernel(per, count_ref, q_ref, kn_ref, rope_ref, qpos_ref, kpos_ref, lse_ref,
                 bias_ref, even_ref, odd_ref, s0_ref, s1_ref):
    step = pl.program_id(0)
    keys = kn_ref.shape[0]
    groups, rows = q_ref.shape[0], q_ref.shape[1]

    @pl.when(step == 0)
    def _():
        rope_setup(rope_ref, even_ref, odd_ref)
        column = key_limit_column(count_ref, kpos_ref, keys)
        for g in range(groups):
            valid = column <= qpos_ref[g : g + 1, :]
            bias_ref[:, g * rows : (g + 1) * rows] = jnp.where(valid, 0.0, NEG)

    bufs = (s0_ref, s1_ref)
    units = [(p, a, c) for p in range(per) for a in range(2) for c in range(groups // 2)]
    tops = {}
    kept = {}

    def forward(u):
        p, a, c = units[u]
        if c == 0:
            lanes = slice((2 * p + a) * DNOPE, (2 * p + a + 1) * DNOPE)
            kept[0] = main_keys(kn_ref[:, lanes], a, even_ref, odd_ref)
        start = p * PAIR + a * LANES
        q = q_ref[2 * c : 2 * c + 2, :, start : start + 2 * LANES].reshape(2 * rows, 2 * LANES)
        cols = slice(2 * c * rows, (2 * c + 2) * rows)
        s = dot_nt(kept[0], q) * SCALE_MAIN + bias_ref[:, cols]
        bufs[u % 2][...] = s
        tops[u] = jnp.max(s, axis=0, keepdims=True)

    def finish(u):
        p, a, c = units[u]
        cols = slice(2 * c * rows, (2 * c + 2) * rows)
        total = jnp.sum(jnp.exp2(bufs[u % 2][...] - tops[u]), axis=0, keepdims=True)
        lse_ref[pl.ds(2 * per * step + 2 * p + a, 1), cols] = tops[u] + jnp.log2(total)

    forward(0)
    for u in range(1, len(units)):
        forward(u)
        finish(u - 1)
    finish(len(units) - 1)


def main_stats(main_query, key_nope, rope_t, query_pos, key_pos, key_count):
    groups, rows, width = main_query.shape
    heads = width // DQK
    keys = key_nope.shape[0]
    total = groups * rows
    per = 2
    return pl.pallas_call(
        functools.partial(stats_kernel, per),
        grid_spec=pltpu.PrefetchScalarGridSpec(
            num_scalar_prefetch=1,
            grid=(heads // (2 * per),),
            in_specs=[
                pl.BlockSpec((groups, rows, per * PAIR), lambda i, c: (0, 0, i)),
                pl.BlockSpec((keys, per * 2 * DNOPE), lambda i, c: (0, i)),
                IN_VMEM,
                IN_VMEM,
                IN_VMEM,
            ],
            out_specs=IN_VMEM,
            scratch_shapes=[
                pltpu.VMEM((keys, total), f32),
                pltpu.VMEM((keys, LANES), bf16),
                pltpu.VMEM((keys, LANES), bf16),
                pltpu.VMEM((keys, 2 * rows), f32),
                pltpu.VMEM((keys, 2 * rows), f32),
            ],
        ),
        out_shape=jax.ShapeDtypeStruct((heads, total), f32),
        compiler_params=params(),
        cost_estimate=cost(
            heads * total * keys * 512, main_query.size * 2 + key_nope.size * 2, heads * total * keys
        ),
        name="main_stats",
    )(key_count, main_query, key_nope, rope_t, query_pos, key_pos)


def target_kernel(n_lse, n_groups, per, count_ref, grp_ref, *refs):
    q_refs = refs[:n_groups]
    kn_ref, rope_ref, qpos_ref, kpos_ref = refs[n_groups : n_groups + 4]
    lse_refs = refs[n_groups + 4 : n_groups + 4 + n_lse]
    out_refs = refs[n_groups + 4 + n_lse : -3]
    glob_ref, even_ref, odd_ref = refs[-3:]
    step = pl.program_id(0)
    keys = kn_ref.shape[0]
    rows = q_refs[0].shape[1]

    @pl.when(step == 0)
    def _():
        rope_setup(rope_ref, even_ref, odd_ref)
        for g in range(n_groups):
            at = pl.ds(pl.multiple_of(grp_ref[g] * rows, rows), rows)
            glob_ref[:, g * rows : (g + 1) * rows] = combine_lse([r[:, at] for r in lse_refs])
            out_refs[g][...] = jnp.zeros_like(out_refs[g])

    for p in range(per):
        acc = None
        for a in range(2):
            lanes = slice((2 * p + a) * DNOPE, (2 * p + a + 1) * DNOPE)
            kk = main_keys(kn_ref[:, lanes], a, even_ref, odd_ref)
            start = p * PAIR + a * LANES
            qs = [r[0, :, start : start + 2 * LANES] for r in q_refs]
            q = qs[0] if n_groups == 1 else jnp.concatenate(qs, axis=0)
            lse = glob_ref[pl.ds(2 * per * step + 2 * p + a, 1), :]
            e = jnp.exp2(dot_nt(kk, q) * SCALE_MAIN - lse)
            acc = e if acc is None else acc + e
        for g in range(n_groups):
            out_refs[g][...] += acc[:, g * rows : (g + 1) * rows]

    @pl.when(step == pl.num_programs(0) - 1)
    def _():
        column = key_limit_column(count_ref, kpos_ref, keys)
        for g in range(n_groups):
            valid = column <= qpos_ref[pl.ds(grp_ref[g], 1), :]
            out_refs[g][...] = jnp.where(valid, out_refs[g][...], 0.0)


def head_sums(group_ids, main_query, key_nope, rope_t, query_pos, key_pos, key_count, lses):
    groups, rows, width = main_query.shape
    heads = width // DQK
    keys = key_nope.shape[0]
    n = len(group_ids)
    per = 4 // n

    def group_q(g):
        return pl.BlockSpec((1, rows, per * PAIR), lambda i, c, grp: (grp[g], 0, i))

    return pl.pallas_call(
        functools.partial(target_kernel, len(lses), n, per),
        grid_spec=pltpu.PrefetchScalarGridSpec(
            num_scalar_prefetch=2,
            grid=(heads // (2 * per),),
            in_specs=[group_q(g) for g in range(n)]
            + [pl.BlockSpec((keys, per * 2 * DNOPE), lambda i, c, grp: (0, i))]
            + [IN_VMEM] * (3 + len(lses)),
            out_specs=[IN_VMEM] * n,
            scratch_shapes=[
                pltpu.VMEM((heads, n * rows), f32),
                pltpu.VMEM((keys, LANES), bf16),
                pltpu.VMEM((keys, LANES), bf16),
            ],
        ),
        out_shape=[jax.ShapeDtypeStruct((keys, rows), f32)] * n,
        compiler_params=params(),
        cost_estimate=cost(
            heads * n * rows * keys * 512, main_query.size * n // 2 + key_nope.size * 2,
            heads * n * rows * keys,
        ),
        name="head_sums",
    )(
        key_count, jnp.stack(group_ids), *([main_query] * n), key_nope, rope_t, query_pos,
        key_pos, *lses,
    )


def logits_kernel(count_ref, grp_ref, iq_ref, ik_ref, wt_ref, qpos_ref, kpos_ref,
                  logits_ref, lse_ref, wm_ref, w_ref):
    step = pl.program_id(0)
    keys = ik_ref.shape[0]
    rows = iq_ref.shape[0]
    per = iq_ref.shape[1] // ID

    @pl.when(step == 0)
    def _():
        w_ref[...] = wt_ref[...].astype(f32)
        logits_ref[...] = jnp.zeros_like(logits_ref)

    for p in range(per // 2):
        q = jnp.concatenate(
            [iq_ref[:, (2 * p + a) * ID : (2 * p + a + 1) * ID] for a in range(2)], axis=0
        )
        z = dot_nt(ik_ref[...], q)
        w = jnp.concatenate(
            [w_ref[pl.ds(step * per + 2 * p + a, 1), :] for a in range(2)], axis=1
        )
        masked = jnp.where(z > 0, w, 0.0)
        wm_ref[:, 2 * p * rows : (2 * p + 2) * rows] = masked.astype(bf16)
        r = z * masked
        logits_ref[...] += r[:, :rows] + r[:, rows:]

    @pl.when(step == pl.num_programs(0) - 1)
    def _():
        logits = logits_ref[...] * SCALE_INDEX
        logits_ref[...] = logits
        column = key_limit_column(count_ref, kpos_ref, keys)
        valid = column <= qpos_ref[pl.ds(grp_ref[0], 1), :]
        s = jnp.where(valid, logits * LOG2E, NEG)
        top = jnp.max(s, axis=0, keepdims=True)
        lse_ref[...] = top + jnp.log2(jnp.sum(jnp.exp2(s - top), axis=0, keepdims=True))


def index_logits(group_id, index_query, index_key, weight_t, query_pos, key_pos, key_count):
    rows, width = index_query.shape
    keys = index_key.shape[0]
    per = 16
    steps = width // (per * ID)
    return pl.pallas_call(
        logits_kernel,
        grid_spec=pltpu.PrefetchScalarGridSpec(
            num_scalar_prefetch=2,
            grid=(steps,),
            in_specs=[
                pl.BlockSpec((rows, per * ID), lambda i, c, grp: (0, i)),
                IN_VMEM,
                IN_VMEM,
                IN_VMEM,
                IN_VMEM,
            ],
            out_specs=[
                IN_VMEM,
                IN_VMEM,
                pl.BlockSpec((keys, per * rows), lambda i, c, grp: (0, i)),
            ],
            scratch_shapes=[pltpu.VMEM((width // ID, rows), f32)],
        ),
        out_shape=[
            jax.ShapeDtypeStruct((keys, rows), f32),
            jax.ShapeDtypeStruct((1, rows), f32),
            jax.ShapeDtypeStruct((keys, (width // ID) * rows), bf16),
        ],
        compiler_params=params(),
        cost_estimate=cost(2 * keys * rows * width, rows * width * 2 + keys * rows * width // ID * 2),
        name="index_logits",
    )(key_count, group_id.reshape(1), index_query, index_key, weight_t, query_pos, key_pos)


def grad_key_kernel(n_parts, n_lse, count_ref, grp_ref, *refs):
    parts = refs[:n_parts]
    lses = refs[n_parts : n_parts + n_lse]
    (logits_ref, cot_ref, qpos_ref, kpos_ref, wm_ref, iq_ref,
     sg_ref, gk_ref) = refs[n_parts + n_lse :]
    step = pl.program_id(0)
    keys, rows = logits_ref.shape
    per = iq_ref.shape[1] // ID

    @pl.when(step == 0)
    def _():
        column = key_limit_column(count_ref, kpos_ref, keys)
        valid = column <= qpos_ref[pl.ds(grp_ref[0], 1), :]
        target = functools.reduce(jnp.add, [p[...] for p in parts]) * (1.0 / H)
        logits = logits_ref[...]
        lse2 = combine_lse([r[...] for r in lses])
        qprob = jnp.where(valid, jnp.exp2(logits * LOG2E - lse2), 0.0)
        sg_ref[:keys, :] = SCALE_INDEX * (cot_ref[...] * (qprob - target))
        live = target > 0
        terms = jnp.where(live, target * (jnp.log(jnp.where(live, target, 1.0)) - logits), 0.0)
        kl = jnp.sum(terms, axis=0, keepdims=True)
        sg_ref[keys:, :] = jnp.broadcast_to(kl, (8, rows))
        gk_ref[...] = jnp.zeros_like(gk_ref)

    for p in range(per // 2):
        dz = []
        qs = []
        for a in range(2):
            j = 2 * p + a
            wm = wm_ref[:, j * rows : (j + 1) * rows].astype(f32)
            dz.append((sg_ref[:keys, :] * wm).astype(bf16))
            qs.append(iq_ref[:, j * ID : (j + 1) * ID])
        gk_ref[...] += dot_nn(jnp.concatenate(dz, axis=1), jnp.concatenate(qs, axis=0))


def index_grad_key(group_id, parts, lses, logits, cotangent, wm, index_query,
                   query_pos, key_pos, key_count):
    rows, width = index_query.shape
    keys = logits.shape[0]
    per = 16
    steps = width // (per * ID)
    return pl.pallas_call(
        functools.partial(grad_key_kernel, len(parts), len(lses)),
        grid_spec=pltpu.PrefetchScalarGridSpec(
            num_scalar_prefetch=2,
            grid=(steps,),
            in_specs=[IN_VMEM] * (len(parts) + len(lses) + 4)
            + [
                pl.BlockSpec((keys, per * rows), lambda i, c, grp: (0, i)),
                pl.BlockSpec((rows, per * ID), lambda i, c, grp: (0, i)),
            ],
            out_specs=[IN_VMEM, IN_VMEM],
        ),
        out_shape=[
            jax.ShapeDtypeStruct((keys + 8, rows), f32),
            jax.ShapeDtypeStruct((keys, ID), f32),
        ],
        compiler_params=params(),
        cost_estimate=cost(2 * keys * rows * width, rows * width * 2 + keys * rows * width // ID * 2),
        name="index_grad_key",
    )(key_count, group_id.reshape(1), *parts, *lses, logits, cotangent, query_pos, key_pos, wm,
      index_query)


def grad_query_kernel(n_shards, first, n_lse, slot_ref, *refs):
    sgs = refs[:n_shards]
    iks = refs[n_shards : 2 * n_shards]
    iq_ref, w_ref = refs[2 * n_shards : 2 * n_shards + 2]
    rest = refs[2 * n_shards + 2 :]
    lses = rest[:n_lse]
    rest = rest[n_lse:]
    if first:
        gq_ref, kl_ref, ws_ref = rest
    else:
        gq_in_ref, kl_in_ref, gq_ref, kl_ref, ws_ref = rest
    rows = iq_ref.shape[0]
    heads = iq_ref.shape[1] // ID
    keys = iks[0].shape[0]
    ws_ref[...] = w_ref[...].astype(f32)
    mine = ws_ref[pl.ds(slot_ref[0] * heads, heads), :]
    ws = jnp.transpose(jnp.concatenate([mine, jnp.zeros((LANES - heads, rows), f32)], axis=0))
    kl = functools.reduce(jnp.add, [s[keys : keys + 1, :] for s in sgs])
    kl = kl if first else kl_in_ref[...] + kl
    if n_lse:
        kl = kl + combine_lse([r[...] for r in lses]) * (1.0 / LOG2E)
    kl_ref[...] = kl
    unit = min(heads, 4)
    iks = [ref[...].astype(bf16) for ref in iks]
    sgts = [jnp.transpose(ref[:keys, :]) for ref in sgs]
    for start in range(0, heads, unit):
        js = range(start, start + unit)
        iq = jnp.concatenate([iq_ref[:, j * ID : (j + 1) * ID] for j in js], axis=0)
        out = None
        for ik, sgt in zip(iks, sgts):
            z = dot_nt(iq, ik)
            dz = jnp.concatenate(
                [
                    jnp.where(z[i * rows : (i + 1) * rows] > 0, sgt * ws[:, j : j + 1], 0.0).astype(bf16)
                    for i, j in enumerate(js)
                ],
                axis=0,
            )
            g = dot_nn(dz, ik)
            out = g if out is None else out + g
        for i, j in enumerate(js):
            cols = slice(j * ID, (j + 1) * ID)
            g = out[i * rows : (i + 1) * rows]
            gq_ref[:, cols] = g if first else gq_in_ref[:, cols] + g


def index_grad_query(slot, n_slots, sgs, iks, index_query, weight_t, lses, carry):
    rows, width = index_query.shape
    heads = width // ID
    mine = width // n_slots
    keys = iks[0].shape[0]
    first = carry is None
    carried = [] if first else list(carry)
    n = len(sgs)
    return pl.pallas_call(
        functools.partial(grad_query_kernel, n, first, len(lses)),
        grid_spec=pltpu.PrefetchScalarGridSpec(
            num_scalar_prefetch=1,
            grid=(1,),
            in_specs=[IN_VMEM] * (2 * n)
            + [pl.BlockSpec((rows, mine), lambda i, s: (0, s[0]))]
            + [IN_VMEM] * (1 + len(lses) + len(carried)),
            out_specs=[IN_VMEM, IN_VMEM],
            scratch_shapes=[pltpu.VMEM((heads, rows), f32)],
        ),
        out_shape=[
            jax.ShapeDtypeStruct((rows, mine), f32),
            jax.ShapeDtypeStruct((1, rows), f32),
        ],
        compiler_params=params(),
        cost_estimate=cost(4 * n * keys * rows * mine, n * (keys * ID * 8) + rows * mine * 8),
        name="index_grad_query",
    )(slot.reshape(1), *sgs, *iks, index_query, weight_t, *lses, *carried)


def swap(value, axis, mask, size):
    return lax.ppermute(value, axis, [(i, i ^ mask) for i in range(size)])


def rotate(value, axis, by, size):
    return lax.ppermute(value, axis, [(i, (i + by) % size) for i in range(size)])


def summed_copies(value, n_head, n_query):
    steps = [("query", m, n_query) for m in (1 << b for b in range(n_query.bit_length() - 1))]
    steps += [("head", (2 << b) - 1, n_head) for b in range(n_head.bit_length() - 1)]
    count = len(steps)
    if count == 0:
        return value
    rows = value.shape[0]
    unit = -(-rows // (8 * count)) * 8
    pieces = [value[i * unit : min((i + 1) * unit, rows)] for i in range(count)]
    pieces = [p for p in pieces if p.shape[0]]
    for s in range(count):
        moved = [swap(p, *steps[(i + s) % count]) for i, p in enumerate(pieces)]
        pieces = [p + m for p, m in zip(pieces, moved)]
    return jnp.concatenate(pieces, axis=0)


def body(n_key, n_head, n_query, main_query, key_nope, key_rope, query_pos, key_pos, key_count,
         index_query, index_key, index_weight, row_cotangent):
    groups, rows, _ = main_query.shape
    keys = key_nope.shape[0]
    z = lax.axis_index("head")
    slot = lax.axis_index("key")
    key_row = key_pos.reshape(1, keys)
    main = (main_query, key_nope, key_rope.T, query_pos, key_row, key_count)
    weight_t = index_weight.T
    cotangent = row_cotangent.reshape(1, rows)

    def gathered(value):
        if n_key == 4:
            far = swap(value, "key", 2, n_key)
            return [value, swap(value, "key", 1, n_key), far, swap(far, "key", 1, n_key)]
        return list(lax.all_gather(value, "key"))

    iks = gathered(index_key.astype(f32))
    lse = main_stats(*main)
    lses = [lse] + [swap(lse, "key", m, n_key) for m in (1, 2, 3)] if n_key == 4 else [
        combine_lse(gathered(lse))
    ]
    logits, index_lse, wm = index_logits(
        z, index_query, index_key, weight_t, query_pos, key_row, key_count
    )
    index_lses = gathered(index_lse) if n_key == 4 else [combine_lse(gathered(index_lse))]

    if n_head == 4 and groups == 4:
        across = head_sums([(z + 2) % 4], *main, lses)[0]
        half = keys // 2
        low = rotate(across[:half], "head", 1, 4)
        high = rotate(across[half:], "head", 3, 4)
        up, down = head_sums([(z + 1) % 4, (z + 3) % 4], *main, lses)
        up = jnp.concatenate([up[:half] + low, up[half:]], axis=0)
        down = jnp.concatenate([down[:half], down[half:] + high], axis=0)
        from_below = rotate(up, "head", 1, 4)
        from_above = rotate(down, "head", 3, 4)
        own = head_sums([z], *main, lses)[0]
        parts = [own, from_below, from_above]
    else:
        tiles = jnp.stack([head_sums([jnp.int32(g)], *main, lses)[0] for g in range(groups)])
        parts = [lax.psum_scatter(tiles, "head", scatter_dimension=0, tiled=True)[0]]

    sg, grad_key = index_grad_key(
        z, parts, index_lses, logits, cotangent, wm, index_query, query_pos, key_row, key_count
    )
    grad_key = summed_copies(grad_key, n_head, n_query)
    sgs = gathered(sg)
    carry = None
    for lo in range(0, n_key, 2):
        last = lo + 2 >= n_key
        carry = index_grad_query(
            slot, n_key, sgs[lo : lo + 2], iks[lo : lo + 2], index_query, weight_t,
            index_lses if last else [], carry,
        )
    grad_query, kl = carry
    return kl.reshape(rows), grad_query, grad_key


def solution(mesh):
    return jax.shard_map(
        functools.partial(body, mesh.shape["key"], mesh.shape["head"], mesh.shape["query"]),
        mesh=mesh,
        in_specs=(
            P(None, "query", "head"),
            P("key", "head"),
            P("key", None),
            P(None, "query"),
            P("key"),
            P("key"),
            P(("head", "query"), None),
            P("key", None),
            P(("head", "query"), None),
            P(("head", "query")),
        ),
        out_specs=(P(("head", "query")), P(("head", "query"), "key"), P("key", None)),
        check_vma=False,
    )
```

```python
import functools
import math
import jax
import jax.numpy as jnp
from jax import lax
from jax.experimental import pallas as pl
from jax.experimental.pallas import tpu as pltpu
from jax.sharding import PartitionSpec as P


H = 128
DNOPE = 128
DROPE = 64
ID = 128
KBLOCK = 32
DQK = 192
LANES = 128
PAIR = 2 * DQK
NEG = -1e30
SMALL = 2.0**-90
LARGE = 2.0**100
BIG = 2**30
LOG2E = math.log2(math.e)
SCALE_MAIN = DQK ** (-0.5) * LOG2E
SCALE_INDEX = ID ** (-0.5)
VMEM_LIMIT = 32 * 1024 * 1024

f32 = jnp.float32
bf16 = jnp.bfloat16
IN_VMEM = pl.BlockSpec(memory_space=pltpu.VMEM)


def dot_nt(a, b):
    return lax.dot_general(a, b, (((1,), (1,)), ((), ())), preferred_element_type=f32)


def dot_nn(a, b):
    return lax.dot_general(a, b, (((1,), (0,)), ((), ())), preferred_element_type=f32)


def params():
    return pltpu.CompilerParams(
        dimension_semantics=("arbitrary",), vmem_limit_bytes=VMEM_LIMIT
    )


def cost(flops, bytes_accessed, transcendentals=0):
    return pl.CostEstimate(
        flops=int(flops), bytes_accessed=int(bytes_accessed), transcendentals=int(transcendentals)
    )


def combine_lse(parts):
    if len(parts) == 1:
        return parts[0]
    top = functools.reduce(jnp.maximum, parts)
    return top + jnp.log2(functools.reduce(jnp.add, [jnp.exp2(p - top) for p in parts]))


def key_limit_column(count_ref, pos_ref, keys):
    blocks = keys // KBLOCK
    lane = lax.broadcasted_iota(jnp.int32, (1, keys), 1)
    block = lane // KBLOCK
    limit = jnp.zeros((1, keys), jnp.int32)
    for b in range(blocks):
        limit = jnp.where(block == b, count_ref[b], limit)
    live = (lane % KBLOCK) < limit
    row = jnp.where(live, pos_ref[...], BIG)
    return jnp.transpose(jnp.broadcast_to(row, (8, keys)))[:, :1]


def rope_setup(rope_t_ref, even_ref, odd_ref):
    rope = jnp.transpose(rope_t_ref[...].astype(f32)).astype(bf16)
    zero = jnp.zeros_like(rope)
    even_ref[...] = jnp.concatenate([rope, zero], axis=1)
    odd_ref[...] = jnp.concatenate([zero, rope], axis=1)


def main_keys(nope, parity, even_ref, odd_ref):
    if parity == 0:
        return jnp.concatenate([nope, even_ref[...]], axis=1)
    turned = jnp.concatenate([nope[:, DROPE:], nope[:, :DROPE]], axis=1)
    low = lax.broadcasted_iota(jnp.int32, turned.shape, 1) < DROPE
    first = jnp.where(low, jnp.zeros_like(turned), turned)
    second = jnp.where(low, turned, odd_ref[...])
    return jnp.concatenate([first, second], axis=1)


def stats_kernel(per, count_ref, q_ref, kn_ref, rope_ref, qpos_ref, kpos_ref, q_hbm, kn_hbm,
                 lse_ref, bias_ref, even_ref, odd_ref, none_ref, bad_ref, q_buf, kn_buf, sem):
    step = pl.program_id(0)
    keys = kn_ref.shape[0]
    groups, rows = q_ref.shape[0], q_ref.shape[1]
    halves = [slice(2 * c * rows, (2 * c + 2) * rows) for c in range(groups // 2)]

    @pl.when(step == 0)
    def _():
        rope_setup(rope_ref, even_ref, odd_ref)
        column = key_limit_column(count_ref, kpos_ref, keys)
        for g in range(groups):
            valid = column <= qpos_ref[g : g + 1, :]
            bias_ref[:, g * rows : (g + 1) * rows] = jnp.where(valid, 0.0, NEG)
        none_ref[...] = jnp.where(jnp.max(bias_ref[...], axis=0, keepdims=True) < 0, 1.0, 0.0)
        bad_ref[...] = jnp.zeros_like(bad_ref)

    def scores(kk, q3, c):
        q = q3.reshape(2 * rows, 2 * LANES)
        return dot_nt(kk, q) * SCALE_MAIN + bias_ref[:, halves[c]]

    for p in range(per):
        for a in range(2):
            lanes = slice((2 * p + a) * DNOPE, (2 * p + a + 1) * DNOPE)
            kk = main_keys(kn_ref[:, lanes], a, even_ref, odd_ref)
            start = p * PAIR + a * LANES
            for c, cols in enumerate(halves):
                q3 = q_ref[2 * c : 2 * c + 2, :, start : start + 2 * LANES]
                total = jnp.sum(jnp.exp2(scores(kk, q3, c)), axis=0, keepdims=True)
                fine = (total >= SMALL) & (total <= LARGE)
                skip = none_ref[:, cols] > 0
                bad_ref[:, cols] += jnp.where(fine | skip, 0.0, 1.0)
                lse_ref[pl.ds(2 * per * step + 2 * p + a, 1), cols] = jnp.where(
                    skip, NEG, jnp.log2(total)
                )

    last = step == pl.num_programs(0) - 1

    @pl.when(last & (jnp.max(bad_ref[...]) > 0))
    def _():
        def again(i, carry):
            q_at = pl.ds(pl.multiple_of(i * PAIR, LANES), PAIR)
            k_at = pl.ds(pl.multiple_of(i * 2 * DNOPE, LANES), 2 * DNOPE)
            q_copy = pltpu.make_async_copy(q_hbm.at[:, :, q_at], q_buf, sem.at[0])
            k_copy = pltpu.make_async_copy(kn_hbm.at[:, k_at], kn_buf, sem.at[1])
            q_copy.start()
            k_copy.start()
            q_copy.wait()
            k_copy.wait()
            for a in range(2):
                kk = main_keys(kn_buf[:, a * DNOPE : (a + 1) * DNOPE], a, even_ref, odd_ref)
                for c, cols in enumerate(halves):
                    q3 = q_buf[2 * c : 2 * c + 2, :, a * LANES : a * LANES + 2 * LANES]
                    s = scores(kk, q3, c)
                    top = jnp.max(s, axis=0, keepdims=True)
                    total = jnp.sum(jnp.exp2(s - top), axis=0, keepdims=True)
                    lse_ref[pl.ds(2 * i + a, 1), cols] = top + jnp.log2(total)
            return carry

        lax.fori_loop(0, lse_ref.shape[0] // 2, again, 0)


def main_stats(main_query, key_nope, rope_t, query_pos, key_pos, key_count):
    groups, rows, width = main_query.shape
    heads = width // DQK
    keys = key_nope.shape[0]
    total = groups * rows
    per = 2
    return pl.pallas_call(
        functools.partial(stats_kernel, per),
        grid_spec=pltpu.PrefetchScalarGridSpec(
            num_scalar_prefetch=1,
            grid=(heads // (2 * per),),
            in_specs=[
                pl.BlockSpec((groups, rows, per * PAIR), lambda i, c: (0, 0, i)),
                pl.BlockSpec((keys, per * 2 * DNOPE), lambda i, c: (0, i)),
                pl.BlockSpec((DROPE, keys), lambda i, c: (0, 0)),
                pl.BlockSpec((groups, rows), lambda i, c: (0, 0)),
                pl.BlockSpec((1, keys), lambda i, c: (0, 0)),
                pl.BlockSpec(memory_space=pltpu.HBM),
                pl.BlockSpec(memory_space=pltpu.HBM),
            ],
            out_specs=IN_VMEM,
            scratch_shapes=[
                pltpu.VMEM((keys, total), f32),
                pltpu.VMEM((keys, LANES), bf16),
                pltpu.VMEM((keys, LANES), bf16),
                pltpu.VMEM((1, total), f32),
                pltpu.VMEM((1, total), f32),
                pltpu.VMEM((groups, rows, PAIR), bf16),
                pltpu.VMEM((keys, 2 * DNOPE), bf16),
                pltpu.SemaphoreType.DMA((2,)),
            ],
        ),
        out_shape=jax.ShapeDtypeStruct((heads, total), f32),
        compiler_params=params(),
        cost_estimate=cost(
            heads * total * keys * 512, main_query.size * 2 + key_nope.size * 2, heads * total * keys
        ),
        name="main_stats",
    )(key_count, main_query, key_nope, rope_t, query_pos, key_pos, main_query, key_nope)


def target_kernel(n_lse, n_groups, per, parts, count_ref, grp_ref, *refs):
    q_refs = refs[:n_groups]
    kn_ref, rope_ref, qpos_ref, kpos_ref = refs[n_groups : n_groups + 4]
    lse_refs = refs[n_groups + 4 : n_groups + 4 + n_lse]
    out_refs = refs[n_groups + 4 + n_lse : -3]
    glob_ref, even_ref, odd_ref = refs[-3:]
    step = pl.program_id(0)
    keys = kn_ref.shape[0]
    rows = q_refs[0].shape[1]
    size = keys // parts
    tiles = [
        (g, slice(i * size, (i + 1) * size), out_refs[g * parts + i])
        for g in range(n_groups)
        for i in range(parts)
    ]

    @pl.when(step == 0)
    def _():
        rope_setup(rope_ref, even_ref, odd_ref)
        for g in range(n_groups):
            at = pl.ds(pl.multiple_of(grp_ref[g] * rows, rows), rows)
            glob_ref[:, g * rows : (g + 1) * rows] = combine_lse([r[:, at] for r in lse_refs])
        for ref in out_refs:
            ref[...] = jnp.zeros_like(ref)

    for p in range(per):
        acc = None
        for a in range(2):
            lanes = slice((2 * p + a) * DNOPE, (2 * p + a + 1) * DNOPE)
            kk = main_keys(kn_ref[:, lanes], a, even_ref, odd_ref)
            start = p * PAIR + a * LANES
            qs = [r[0, :, start : start + 2 * LANES] for r in q_refs]
            q = qs[0] if n_groups == 1 else jnp.concatenate(qs, axis=0)
            lse = glob_ref[pl.ds(2 * per * step + 2 * p + a, 1), :]
            e = jnp.exp2(dot_nt(kk, q) * SCALE_MAIN - lse)
            acc = e if acc is None else acc + e
        for g, at, ref in tiles:
            ref[...] += acc[at, g * rows : (g + 1) * rows]

    @pl.when(step == pl.num_programs(0) - 1)
    def _():
        column = key_limit_column(count_ref, kpos_ref, keys)
        for g, at, ref in tiles:
            valid = column[at] <= qpos_ref[pl.ds(grp_ref[g], 1), :]
            ref[...] = jnp.where(valid, ref[...], 0.0)


def head_sums(group_ids, main_query, key_nope, rope_t, query_pos, key_pos, key_count, lses, parts=1):
    groups, rows, width = main_query.shape
    heads = width // DQK
    keys = key_nope.shape[0]
    n = len(group_ids)
    per = 4 // n

    def group_q(g):
        return pl.BlockSpec((1, rows, per * PAIR), lambda i, c, grp: (grp[g], 0, i))

    return pl.pallas_call(
        functools.partial(target_kernel, len(lses), n, per, parts),
        grid_spec=pltpu.PrefetchScalarGridSpec(
            num_scalar_prefetch=2,
            grid=(heads // (2 * per),),
            in_specs=[group_q(g) for g in range(n)]
            + [pl.BlockSpec((keys, per * 2 * DNOPE), lambda i, c, grp: (0, i))]
            + [
                pl.BlockSpec((DROPE, keys), lambda i, c, grp: (0, 0)),
                pl.BlockSpec((groups, rows), lambda i, c, grp: (0, 0)),
                pl.BlockSpec((1, keys), lambda i, c, grp: (0, 0)),
            ]
            + [IN_VMEM] * len(lses),
            out_specs=[IN_VMEM] * (n * parts),
            scratch_shapes=[
                pltpu.VMEM((heads, n * rows), f32),
                pltpu.VMEM((keys, LANES), bf16),
                pltpu.VMEM((keys, LANES), bf16),
            ],
        ),
        out_shape=[jax.ShapeDtypeStruct((keys // parts, rows), f32)] * (n * parts),
        compiler_params=params(),
        cost_estimate=cost(
            heads * n * rows * keys * 512, main_query.size * n // 2 + key_nope.size * 2,
            heads * n * rows * keys,
        ),
        name="head_sums",
    )(
        key_count, jnp.stack(group_ids), *([main_query] * n), key_nope, rope_t, query_pos,
        key_pos, *lses,
    )


def logits_kernel(count_ref, grp_ref, iq_ref, ik_ref, wt_ref, qpos_ref, kpos_ref,
                  logits_ref, lse_ref, wm_ref, w_ref):
    step = pl.program_id(0)
    keys = ik_ref.shape[0]
    rows = iq_ref.shape[0]
    per = iq_ref.shape[1] // ID

    @pl.when(step == 0)
    def _():
        w_ref[...] = wt_ref[...].astype(f32)
        logits_ref[...] = jnp.zeros_like(logits_ref)

    for p in range(per // 2):
        q = jnp.concatenate(
            [iq_ref[:, (2 * p + a) * ID : (2 * p + a + 1) * ID] for a in range(2)], axis=0
        )
        z = dot_nt(ik_ref[...], q)
        w = jnp.concatenate(
            [w_ref[pl.ds(step * per + 2 * p + a, 1), :] for a in range(2)], axis=1
        )
        masked = jnp.where(z > 0, w, 0.0)
        wm_ref[:, 2 * p * rows : (2 * p + 2) * rows] = masked.astype(bf16)
        r = z * masked
        logits_ref[...] += r[:, :rows] + r[:, rows:]

    @pl.when(step == pl.num_programs(0) - 1)
    def _():
        logits = logits_ref[...] * SCALE_INDEX
        logits_ref[...] = logits
        column = key_limit_column(count_ref, kpos_ref, keys)
        valid = column <= qpos_ref[pl.ds(grp_ref[0], 1), :]
        s = jnp.where(valid, logits * LOG2E, NEG)
        top = jnp.max(s, axis=0, keepdims=True)
        lse_ref[...] = top + jnp.log2(jnp.sum(jnp.exp2(s - top), axis=0, keepdims=True))


def index_logits(group_id, index_query, index_key, weight_t, query_pos, key_pos, key_count):
    rows, width = index_query.shape
    keys = index_key.shape[0]
    per = 16
    steps = width // (per * ID)
    return pl.pallas_call(
        logits_kernel,
        grid_spec=pltpu.PrefetchScalarGridSpec(
            num_scalar_prefetch=2,
            grid=(steps,),
            in_specs=[
                pl.BlockSpec((rows, per * ID), lambda i, c, grp: (0, i)),
                pl.BlockSpec((keys, ID), lambda i, c, grp: (0, 0)),
                pl.BlockSpec((width // ID, rows), lambda i, c, grp: (0, 0)),
                pl.BlockSpec(query_pos.shape, lambda i, c, grp: (0, 0)),
                pl.BlockSpec((1, keys), lambda i, c, grp: (0, 0)),
            ],
            out_specs=[
                IN_VMEM,
                IN_VMEM,
                pl.BlockSpec((keys, per * rows), lambda i, c, grp: (0, i)),
            ],
            scratch_shapes=[pltpu.VMEM((width // ID, rows), f32)],
        ),
        out_shape=[
            jax.ShapeDtypeStruct((keys, rows), f32),
            jax.ShapeDtypeStruct((1, rows), f32),
            pltpu.HBM((keys, (width // ID) * rows), bf16),
        ],
        compiler_params=params(),
        cost_estimate=cost(2 * keys * rows * width, rows * width * 2 + keys * rows * width // ID * 2),
        name="index_logits",
    )(key_count, group_id.reshape(1), index_query, index_key, weight_t, query_pos, key_pos)


def grad_key_kernel(n_parts, n_lse, count_ref, grp_ref, *refs):
    parts = refs[:n_parts]
    lses = refs[n_parts : n_parts + n_lse]
    (logits_ref, cot_ref, qpos_ref, kpos_ref, wm_ref, iq_ref,
     sg_ref, gk_ref) = refs[n_parts + n_lse :]
    step = pl.program_id(0)
    keys, rows = logits_ref.shape
    per = iq_ref.shape[1] // ID

    @pl.when(step == 0)
    def _():
        column = key_limit_column(count_ref, kpos_ref, keys)
        valid = column <= qpos_ref[pl.ds(grp_ref[0], 1), :]
        target = functools.reduce(jnp.add, [p[...] for p in parts]) * (1.0 / H)
        logits = logits_ref[...]
        lse2 = combine_lse([r[...] for r in lses])
        qprob = jnp.where(valid, jnp.exp2(logits * LOG2E - lse2), 0.0)
        sg_ref[:keys, :] = SCALE_INDEX * (cot_ref[...] * (qprob - target))
        live = target > 0
        terms = jnp.where(live, target * (jnp.log(jnp.where(live, target, 1.0)) - logits), 0.0)
        kl = jnp.sum(terms, axis=0, keepdims=True)
        sg_ref[keys:, :] = jnp.broadcast_to(kl, (8, rows))
        gk_ref[...] = jnp.zeros_like(gk_ref)

    for p in range(per // 2):
        dz = []
        qs = []
        for a in range(2):
            j = 2 * p + a
            wm = wm_ref[:, j * rows : (j + 1) * rows].astype(f32)
            dz.append((sg_ref[:keys, :] * wm).astype(bf16))
            qs.append(iq_ref[:, j * ID : (j + 1) * ID])
        gk_ref[...] += dot_nn(jnp.concatenate(dz, axis=1), jnp.concatenate(qs, axis=0))


def index_grad_key(group_id, parts, lses, logits, cotangent, wm, index_query,
                   query_pos, key_pos, key_count):
    rows, width = index_query.shape
    keys = logits.shape[0]
    per = 16
    steps = width // (per * ID)
    return pl.pallas_call(
        functools.partial(grad_key_kernel, len(parts), len(lses)),
        grid_spec=pltpu.PrefetchScalarGridSpec(
            num_scalar_prefetch=2,
            grid=(steps,),
            in_specs=[IN_VMEM] * (len(parts) + len(lses) + 1)
            + [
                pl.BlockSpec((1, rows), lambda i, c, grp: (0, 0)),
                pl.BlockSpec(query_pos.shape, lambda i, c, grp: (0, 0)),
                pl.BlockSpec((1, keys), lambda i, c, grp: (0, 0)),
                pl.BlockSpec((keys, per * rows), lambda i, c, grp: (0, i)),
                pl.BlockSpec((rows, per * ID), lambda i, c, grp: (0, i)),
            ],
            out_specs=[IN_VMEM, IN_VMEM],
        ),
        out_shape=[
            jax.ShapeDtypeStruct((keys + 8, rows), f32),
            jax.ShapeDtypeStruct((keys, ID), f32),
        ],
        compiler_params=params(),
        cost_estimate=cost(2 * keys * rows * width, rows * width * 2 + keys * rows * width // ID * 2),
        name="index_grad_key",
    )(key_count, group_id.reshape(1), *parts, *lses, logits, cotangent, query_pos, key_pos, wm,
      index_query)


def grad_query_kernel(n_shards, first, n_lse, slot_ref, *refs):
    sgs = refs[:n_shards]
    iks = refs[n_shards : 2 * n_shards]
    iq_ref, w_ref = refs[2 * n_shards : 2 * n_shards + 2]
    rest = refs[2 * n_shards + 2 :]
    lses = rest[:n_lse]
    rest = rest[n_lse:]
    if first:
        gq_ref, kl_ref, ws_ref = rest
    else:
        gq_in_ref, kl_in_ref, gq_ref, kl_ref, ws_ref = rest
    rows = iq_ref.shape[0]
    heads = iq_ref.shape[1] // ID
    keys = iks[0].shape[0]
    ws_ref[...] = w_ref[...].astype(f32)
    mine = ws_ref[pl.ds(slot_ref[0] * heads, heads), :]
    ws = jnp.transpose(jnp.concatenate([mine, jnp.zeros((LANES - heads, rows), f32)], axis=0))
    kl = functools.reduce(jnp.add, [s[keys : keys + 1, :] for s in sgs])
    kl = kl if first else kl_in_ref[...] + kl
    if n_lse:
        kl = kl + combine_lse([r[...] for r in lses]) * (1.0 / LOG2E)
    kl_ref[...] = kl
    unit = min(heads, 4)
    iks = [ref[...].astype(bf16) for ref in iks]
    sgts = [jnp.transpose(ref[:keys, :]) for ref in sgs]
    for start in range(0, heads, unit):
        js = range(start, start + unit)
        iq = jnp.concatenate([iq_ref[:, j * ID : (j + 1) * ID] for j in js], axis=0)
        out = None
        for ik, sgt in zip(iks, sgts):
            z = dot_nt(iq, ik)
            dz = jnp.concatenate(
                [
                    jnp.where(z[i * rows : (i + 1) * rows] > 0, sgt * ws[:, j : j + 1], 0.0).astype(bf16)
                    for i, j in enumerate(js)
                ],
                axis=0,
            )
            g = dot_nn(dz, ik)
            out = g if out is None else out + g
        for i, j in enumerate(js):
            cols = slice(j * ID, (j + 1) * ID)
            g = out[i * rows : (i + 1) * rows]
            gq_ref[:, cols] = g if first else gq_in_ref[:, cols] + g


def index_grad_query(slot, n_slots, sgs, iks, index_query, weight_t, lses, carry):
    rows, width = index_query.shape
    heads = width // ID
    mine = width // n_slots
    keys = iks[0].shape[0]
    first = carry is None
    carried = [] if first else list(carry)
    n = len(sgs)
    return pl.pallas_call(
        functools.partial(grad_query_kernel, n, first, len(lses)),
        grid_spec=pltpu.PrefetchScalarGridSpec(
            num_scalar_prefetch=1,
            grid=(1,),
            in_specs=[IN_VMEM] * (2 * n)
            + [
                pl.BlockSpec((rows, mine), lambda i, s: (0, s[0])),
                pl.BlockSpec(weight_t.shape, lambda i, s: (0, 0)),
            ]
            + [IN_VMEM] * (len(lses) + len(carried)),
            out_specs=[IN_VMEM, IN_VMEM],
            scratch_shapes=[pltpu.VMEM((heads, rows), f32)],
        ),
        out_shape=[
            jax.ShapeDtypeStruct((rows, mine), f32),
            jax.ShapeDtypeStruct((1, rows), f32),
        ],
        compiler_params=params(),
        cost_estimate=cost(4 * n * keys * rows * mine, n * (keys * ID * 8) + rows * mine * 8),
        name="index_grad_query",
    )(slot.reshape(1), *sgs, *iks, index_query, weight_t, *lses, *carried)


def swap(value, axis, mask, size):
    return lax.ppermute(value, axis, [(i, i ^ mask) for i in range(size)])


def rotate(value, axis, by, size):
    return lax.ppermute(value, axis, [(i, (i + by) % size) for i in range(size)])


def butterfly_lse(value, size):
    pair = [value]
    for bit in reversed(range(size.bit_length() - 1)):
        here = combine_lse(pair)
        pair = [here, swap(here, "key", 1 << bit, size)]
    return pair


def summed_copies(value, n_head, n_query):
    steps = [("query", 1 << b, n_query) for b in range(n_query.bit_length() - 1)]
    steps += [("head", (2 << b) - 1, n_head) for b in range(n_head.bit_length() - 1)]
    for axis, mask, size in steps:
        value = value + swap(value, axis, mask, size)
    return value


def in_hbm(*values):
    return tuple(pltpu.with_memory_space_constraint(v, pltpu.HBM) for v in values)


def body(n_key, n_head, n_query, main_query, key_nope, key_rope, query_pos, key_pos, key_count,
         index_query, index_key, index_weight, row_cotangent):
    groups, rows, _ = main_query.shape
    keys = key_nope.shape[0]
    z = lax.axis_index("head")
    slot = lax.axis_index("key")
    (main_query, key_nope, rope_t, query_pos, key_row, key_count, index_query, weight_t, cotangent,
     narrow_key) = in_hbm(
        main_query, key_nope, key_rope.T, query_pos, key_pos.reshape(1, keys), key_count,
        index_query, index_weight.T, row_cotangent.reshape(1, rows), index_key,
    )
    main = (main_query, key_nope, rope_t, query_pos, key_row, key_count)

    def gathered(value):
        if n_key == 4:
            near = swap(value, "key", 1, n_key)
            far = swap(value, "key", 2, n_key)
            across = swap(far, "key", 1, n_key)
            return [value, near, far, across]
        return list(lax.all_gather(value, "key"))

    lse = main_stats(*main)
    lses = butterfly_lse(lse, n_key)
    logits, index_lse, wm = index_logits(
        z, index_query, narrow_key, weight_t, query_pos, key_row, key_count
    )
    wm = in_hbm(wm)[0]
    index_lses = butterfly_lse(index_lse, n_key)
    iks = gathered(index_key.astype(f32))

    if n_head == 4 and groups == 4:
        low, high = head_sums([(z + 2) % 4], *main, lses, parts=2)
        half = keys // 2
        low = rotate(low, "head", 1, 4)
        high = rotate(high, "head", 3, 4)
        up, down = head_sums([(z + 1) % 4, (z + 3) % 4], *main, lses)
        up = up + jnp.pad(low, ((0, half), (0, 0)))
        down = down + jnp.pad(high, ((half, 0), (0, 0)))
        from_below = rotate(up, "head", 1, 4)
        from_above = rotate(down, "head", 3, 4)
        own = head_sums([z], *main, lses)[0]
        parts = [own, from_below, from_above]
    else:
        tiles = jnp.stack([head_sums([jnp.int32(g)], *main, lses)[0] for g in range(groups)])
        parts = [lax.psum_scatter(tiles, "head", scatter_dimension=0, tiled=True)[0]]

    sg, grad_key = index_grad_key(
        z, parts, index_lses, logits, cotangent, wm, index_query, query_pos, key_row, key_count
    )
    grad_key = summed_copies(grad_key, n_head, n_query)
    sgs = gathered(sg)
    carry = None
    for lo in range(0, n_key, 2):
        last = lo + 2 >= n_key
        carry = index_grad_query(
            slot, n_key, sgs[lo : lo + 2], iks[lo : lo + 2], index_query, weight_t,
            index_lses if last else [], carry,
        )
    grad_query, kl = carry
    return kl.reshape(rows), grad_query, grad_key


def solution(mesh):
    sizes = (mesh.shape["key"], mesh.shape["head"], mesh.shape["query"])

    def step(*args):
        return body(*sizes, *args)

    return jax.shard_map(
        step,
        mesh=mesh,
        in_specs=(
            P(None, "query", "head"),
            P("key", "head"),
            P("key", None),
            P(None, "query"),
            P("key"),
            P("key"),
            P(("head", "query"), None),
            P("key", None),
            P(("head", "query"), None),
            P(("head", "query")),
        ),
        out_specs=(P(("head", "query")), P(("head", "query"), "key"), P("key", None)),
        check_vma=False,
    )
```

```python
import functools
import math
import jax
import jax.numpy as jnp
from jax import lax
from jax.experimental import pallas as pl
from jax.experimental.pallas import tpu as pltpu
from jax.sharding import PartitionSpec as P


H = 128
DNOPE = 128
DROPE = 64
ID = 128
KBLOCK = 32
DQK = 192
LANES = 128
PAIR = 2 * DQK
NEG = -1e30
SMALL = 2.0**-90
LARGE = 2.0**100
BIG = 2**30
LOG2E = math.log2(math.e)
SCALE_MAIN = DQK ** (-0.5) * LOG2E
SCALE_INDEX = ID ** (-0.5)

f32 = jnp.float32
bf16 = jnp.bfloat16
IN_VMEM = pl.BlockSpec(memory_space=pltpu.VMEM)


def dot_nt(a, b):
    return lax.dot_general(a, b, (((1,), (1,)), ((), ())), preferred_element_type=f32)


def dot_nn(a, b):
    return lax.dot_general(a, b, (((1,), (0,)), ((), ())), preferred_element_type=f32)


def cost(flops, bytes_accessed, transcendentals=0):
    return pl.CostEstimate(
        flops=int(flops), bytes_accessed=int(bytes_accessed), transcendentals=int(transcendentals)
    )


def combine_lse(parts):
    if len(parts) == 1:
        return parts[0]
    top = functools.reduce(jnp.maximum, parts)
    return top + jnp.log2(functools.reduce(jnp.add, [jnp.exp2(p - top) for p in parts]))


def key_limit_column(count_ref, row, keys):
    lane = lax.broadcasted_iota(jnp.int32, (1, keys), 1)
    block = lane // KBLOCK
    limit = jnp.zeros((1, keys), jnp.int32)
    for b in range(keys // KBLOCK):
        limit = jnp.where(block == b, count_ref[b], limit)
    live = (lane % KBLOCK) < limit
    row = jnp.where(live, row, BIG)
    return jnp.transpose(jnp.broadcast_to(row, (8, keys)))[:, :1]


def main_keys(nope, parity, even_ref, odd_ref):
    if parity == 0:
        return jnp.concatenate([nope, even_ref[...]], axis=1)
    turned = jnp.concatenate([nope[:, DROPE:], nope[:, :DROPE]], axis=1)
    low = lax.broadcasted_iota(jnp.int32, turned.shape, 1) < DROPE
    first = jnp.where(low, jnp.zeros_like(turned), turned)
    second = jnp.where(low, turned, odd_ref[...])
    return jnp.concatenate([first, second], axis=1)


def lanes_at(index, width):
    return pl.ds(pl.multiple_of(index * width, LANES), width)


def stats_kernel(per, count_hbm, q_hbm, kn_hbm, rope_hbm, qpos_hbm, kpos_hbm,
                 lse_ref, q_ref, kk_ref, bias_ref,
                 kn_ref, rope_ref, qpos_ref, kpos_ref, even_ref, odd_ref, none_ref, bad_ref,
                 count_ref, small_sem, q_sem, kn_sem):
    keys = kn_ref.shape[0]
    groups, rows = q_ref.shape[0], q_ref.shape[1]
    pairs = q_ref.shape[2] // PAIR
    halves = [slice(2 * c * rows, (2 * c + 2) * rows) for c in range(groups // 2)]

    small = [
        pltpu.make_async_copy(src, dst, small_sem.at[i])
        for i, (src, dst) in enumerate(
            ((count_hbm, count_ref), (kpos_hbm, kpos_ref), (qpos_hbm, qpos_ref), (rope_hbm, rope_ref))
        )
    ]

    def large(i):
        q_at, k_at = lanes_at(i, PAIR), lanes_at(i, 2 * DNOPE)
        return (
            pltpu.make_async_copy(kn_hbm.at[:, k_at], kn_ref.at[:, k_at], kn_sem.at[i]),
            pltpu.make_async_copy(q_hbm.at[:, :, q_at], q_ref.at[:, :, q_at], q_sem.at[i]),
        )

    for copy in small:
        copy.start()
    for i in range(pairs):
        for copy in large(i):
            copy.start()
    for copy in small:
        copy.wait()

    rope = jnp.transpose(rope_ref[...].astype(f32)).astype(bf16)
    zero = jnp.zeros_like(rope)
    even_ref[...] = jnp.concatenate([rope, zero], axis=1)
    odd_ref[...] = jnp.concatenate([zero, rope], axis=1)
    column = key_limit_column(count_ref, kpos_ref[...], keys)
    for g in range(groups):
        valid = column <= qpos_ref[g : g + 1, :]
        bias = jnp.where(valid, 0.0, NEG)
        bias_ref[:, g * rows : (g + 1) * rows] = bias
        none_ref[:, g * rows : (g + 1) * rows] = jnp.where(
            jnp.max(bias, axis=0, keepdims=True) < 0, 1.0, 0.0
        )
    bad_ref[...] = jnp.zeros_like(bad_ref)

    def scores(kk, q3, c):
        q = q3.reshape(2 * rows, 2 * LANES)
        return dot_nt(kk, q) * SCALE_MAIN + bias_ref[:, halves[c]]

    def query(pair, a, c):
        at = pl.ds(pl.multiple_of(pair * PAIR + a * LANES, LANES), 2 * LANES)
        return q_ref[2 * c : 2 * c + 2, :, at]

    def step(i, carry):
        for p in range(per):
            pair = i * per + p
            for copy in large(pair):
                copy.wait()
        for p in range(per):
            pair = i * per + p
            for a in range(2):
                kk = main_keys(kn_ref[:, lanes_at(2 * pair + a, DNOPE)], a, even_ref, odd_ref)
                kk_ref[:, lanes_at(2 * pair + a, 2 * LANES)] = kk
                for c, cols in enumerate(halves):
                    s = scores(kk, query(pair, a, c), c)
                    total = jnp.sum(jnp.exp2(s), axis=0, keepdims=True)
                    fine = (total >= SMALL) & (total <= LARGE)
                    skip = none_ref[:, cols] > 0
                    bad_ref[:, cols] += jnp.where(fine | skip, 0.0, 1.0)
                    lse_ref[pl.ds(2 * pair + a, 1), cols] = jnp.where(skip, NEG, jnp.log2(total))
        return carry

    lax.fori_loop(0, pairs // per, step, 0)

    @pl.when(jnp.max(bad_ref[...]) > 0)
    def _():
        def again(pair, carry):
            for a in range(2):
                kk = kk_ref[:, lanes_at(2 * pair + a, 2 * LANES)]
                for c, cols in enumerate(halves):
                    s = scores(kk, query(pair, a, c), c)
                    top = jnp.max(s, axis=0, keepdims=True)
                    total = jnp.sum(jnp.exp2(s - top), axis=0, keepdims=True)
                    lse_ref[pl.ds(2 * pair + a, 1), cols] = top + jnp.log2(total)
            return carry

        lax.fori_loop(0, pairs, again, 0)


def main_stats(main_query, key_nope, rope_t, query_pos, key_pos, key_count):
    groups, rows, width = main_query.shape
    heads = width // DQK
    keys = key_nope.shape[0]
    total = groups * rows
    return pl.pallas_call(
        functools.partial(stats_kernel, 2),
        in_specs=[pl.BlockSpec(memory_space=pltpu.HBM)] * 6,
        out_specs=[IN_VMEM] * 4,
        out_shape=[
            jax.ShapeDtypeStruct((heads, total), f32),
            jax.ShapeDtypeStruct(main_query.shape, bf16),
            jax.ShapeDtypeStruct((keys, heads * 2 * LANES), bf16),
            jax.ShapeDtypeStruct((keys, total), f32),
        ],
        scratch_shapes=[
            pltpu.VMEM(key_nope.shape, bf16),
            pltpu.VMEM(rope_t.shape, bf16),
            pltpu.VMEM(query_pos.shape, jnp.int32),
            pltpu.VMEM(key_pos.shape, jnp.int32),
            pltpu.VMEM((keys, LANES), bf16),
            pltpu.VMEM((keys, LANES), bf16),
            pltpu.VMEM((1, total), f32),
            pltpu.VMEM((1, total), f32),
            pltpu.SMEM(key_count.shape, jnp.int32),
            pltpu.SemaphoreType.DMA((4,)),
            pltpu.SemaphoreType.DMA((heads // 2,)),
            pltpu.SemaphoreType.DMA((heads // 2,)),
        ],
        compiler_params=pltpu.CompilerParams(vmem_limit_bytes=16 * 1024 * 1024),
        cost_estimate=cost(
            heads * total * keys * 512, main_query.size * 2 + key_nope.size * 2, heads * total * keys
        ),
        name="main_stats",
    )(key_count, main_query, key_nope, rope_t, query_pos, key_pos)


def target_kernel(n_lse, shifts, per, parts, axis_size, q_ref, kk_ref, bias_ref, *refs):
    lse_refs = refs[:n_lse]
    out_refs = refs[n_lse:-1]
    glob_ref = refs[-1]
    n_groups = len(shifts)
    keys = kk_ref.shape[0]
    rows = q_ref.shape[1]
    pairs = q_ref.shape[2] // PAIR
    size = keys // parts
    me = lax.axis_index("head")
    ids = [lax.rem(me + shift, axis_size) for shift in shifts]
    tiles = [
        (g, slice(i * size, (i + 1) * size), out_refs[g * parts + i])
        for g in range(n_groups)
        for i in range(parts)
    ]
    for g in range(n_groups):
        at = lanes_at(ids[g], rows)
        glob_ref[:, g * rows : (g + 1) * rows] = combine_lse([r[:, at] for r in lse_refs])
    for ref in out_refs:
        ref[...] = jnp.zeros_like(ref)

    def step(i, carry):
        for p in range(per):
            pair = i * per + p
            acc = None
            for a in range(2):
                kk = kk_ref[:, lanes_at(2 * pair + a, 2 * LANES)]
                at = pl.ds(pl.multiple_of(pair * PAIR + a * LANES, LANES), 2 * LANES)
                qs = [q_ref[g, :, at] for g in ids]
                q = qs[0] if n_groups == 1 else jnp.concatenate(qs, axis=0)
                lse = glob_ref[pl.ds(2 * pair + a, 1), :]
                e = jnp.exp2(dot_nt(kk, q) * SCALE_MAIN - lse)
                acc = e if acc is None else acc + e
            for g, at, ref in tiles:
                ref[...] += acc[at, g * rows : (g + 1) * rows]
        return carry

    lax.fori_loop(0, pairs // per, step, 0)
    for g, at, ref in tiles:
        ref[...] = jnp.where(bias_ref[at, lanes_at(ids[g], rows)] < 0, 0.0, ref[...])


def head_sums(shifts, axis_size, q, kk, bias, lses, parts=1):
    _, rows, width = q.shape
    heads = width // DQK
    keys = kk.shape[0]
    n = len(shifts)
    return pl.pallas_call(
        functools.partial(target_kernel, len(lses), shifts, 4 // n, parts, axis_size),
        in_specs=[IN_VMEM] * (3 + len(lses)),
        out_specs=[IN_VMEM] * (n * parts),
        out_shape=[jax.ShapeDtypeStruct((keys // parts, rows), f32)] * (n * parts),
        scratch_shapes=[pltpu.VMEM((heads, n * rows), f32)],
        compiler_params=pltpu.CompilerParams(vmem_limit_bytes=16 * 1024 * 1024),
        cost_estimate=cost(
            heads * n * rows * keys * 512, heads * n * rows * keys // 16, heads * n * rows * keys
        ),
        name="head_sums",
    )(q, kk, bias, *lses)


def logits_kernel(per, iq_ref, ik_ref, wt_ref, bias_ref, logits_ref, lse_ref, wm_ref, w_ref):
    rows, width = iq_ref.shape
    w_ref[...] = wt_ref[...].astype(f32)
    logits_ref[...] = jnp.zeros_like(logits_ref)

    def step(i, carry):
        for p in range(per):
            first = 2 * (i * per + p)
            q = jnp.concatenate([iq_ref[:, lanes_at(first + a, ID)] for a in range(2)], axis=0)
            z = dot_nt(ik_ref[...], q)
            w = jnp.concatenate([w_ref[pl.ds(first + a, 1), :] for a in range(2)], axis=1)
            masked = jnp.where(z > 0, w, 0.0)
            wm_ref[:, lanes_at(i * per + p, 2 * rows)] = masked.astype(bf16)
            r = z * masked
            logits_ref[...] += r[:, :rows] + r[:, rows:]
        return carry

    lax.fori_loop(0, width // (2 * ID * per), step, 0)
    logits = logits_ref[...] * SCALE_INDEX
    logits_ref[...] = logits
    valid = bias_ref[:, lanes_at(lax.axis_index("head"), rows)] == 0
    s = jnp.where(valid, logits * LOG2E, NEG)
    top = jnp.max(s, axis=0, keepdims=True)
    lse_ref[...] = top + jnp.log2(jnp.sum(jnp.exp2(s - top), axis=0, keepdims=True))


def index_logits(index_query, index_key, weight_t, bias):
    rows, width = index_query.shape
    keys = index_key.shape[0]
    whole = lambda i: (0, 0)
    return pl.pallas_call(
        functools.partial(logits_kernel, 4),
        grid=(1,),
        in_specs=[
            IN_VMEM,
            pl.BlockSpec(index_key.shape, whole),
            pl.BlockSpec(weight_t.shape, whole),
            IN_VMEM,
        ],
        out_specs=[IN_VMEM] * 3,
        out_shape=[
            jax.ShapeDtypeStruct((keys, rows), f32),
            jax.ShapeDtypeStruct((1, rows), f32),
            jax.ShapeDtypeStruct((keys, (width // ID) * rows), bf16),
        ],
        scratch_shapes=[pltpu.VMEM((width // ID, rows), f32)],
        compiler_params=pltpu.CompilerParams(vmem_limit_bytes=16 * 1024 * 1024),
        cost_estimate=cost(2 * keys * rows * width, rows * width * 2 + keys * rows * width // ID * 2),
        name="index_logits",
    )(index_query, index_key, weight_t, bias)


def grad_key_kernel(n_parts, n_lse, per, *refs):
    parts = refs[:n_parts]
    lses = refs[n_parts : n_parts + n_lse]
    logits_ref, wm_ref, iq_ref, bias_ref, cot_ref, sg_ref, gk_ref = refs[n_parts + n_lse :]
    keys, rows = logits_ref.shape
    width = iq_ref.shape[1]

    valid = bias_ref[:, lanes_at(lax.axis_index("head"), rows)] == 0
    target = functools.reduce(jnp.add, [p[...] for p in parts]) * (1.0 / H)
    logits = logits_ref[...]
    lse2 = combine_lse([r[...] for r in lses])
    qprob = jnp.where(valid, jnp.exp2(logits * LOG2E - lse2), 0.0)
    sg_ref[:keys, :] = SCALE_INDEX * (cot_ref[...] * (qprob - target))
    live = target > 0
    terms = jnp.where(live, target * (jnp.log(jnp.where(live, target, 1.0)) - logits), 0.0)
    kl = jnp.sum(terms, axis=0, keepdims=True)
    sg_ref[keys:, :] = jnp.broadcast_to(kl, (8, rows))
    gk_ref[...] = jnp.zeros_like(gk_ref)

    def step(i, carry):
        for p in range(per):
            dz = []
            qs = []
            for a in range(2):
                j = 2 * (i * per + p) + a
                wm = wm_ref[:, lanes_at(j, rows)].astype(f32)
                dz.append((sg_ref[:keys, :] * wm).astype(bf16))
                qs.append(iq_ref[:, lanes_at(j, ID)])
            gk_ref[...] += dot_nn(jnp.concatenate(dz, axis=1), jnp.concatenate(qs, axis=0))
        return carry

    lax.fori_loop(0, width // (2 * ID * per), step, 0)


def index_grad_key(parts, lses, logits, wm, index_query, bias, cotangent):
    rows, width = index_query.shape
    keys = logits.shape[0]
    return pl.pallas_call(
        functools.partial(grad_key_kernel, len(parts), len(lses), 8),
        grid=(1,),
        in_specs=[IN_VMEM] * (len(parts) + len(lses) + 4)
        + [pl.BlockSpec((1, rows), lambda i: (0, 0))],
        out_specs=[IN_VMEM, IN_VMEM],
        out_shape=[
            jax.ShapeDtypeStruct((keys + 8, rows), f32),
            jax.ShapeDtypeStruct((keys, ID), f32),
        ],
        compiler_params=pltpu.CompilerParams(vmem_limit_bytes=16 * 1024 * 1024),
        cost_estimate=cost(2 * keys * rows * width, rows * width * 2 + keys * rows * width // ID * 2),
        name="index_grad_key",
    )(*parts, *lses, logits, wm, index_query, bias, cotangent)


def grad_query_kernel(n_shards, first, n_lse, *refs):
    sgs = refs[:n_shards]
    iks = refs[n_shards : 2 * n_shards]
    iq_ref, w_ref = refs[2 * n_shards : 2 * n_shards + 2]
    rest = refs[2 * n_shards + 2 :]
    lses = rest[:n_lse]
    rest = rest[n_lse:]
    if first:
        gq_ref, kl_ref, ws_ref = rest
    else:
        gq_in_ref, kl_in_ref, gq_ref, kl_ref, ws_ref = rest
    rows = iq_ref.shape[0]
    heads = gq_ref.shape[1] // ID
    keys = iks[0].shape[0]
    base = lax.axis_index("key") * heads
    ws_ref[...] = w_ref[...].astype(f32)
    mine = ws_ref[pl.ds(base, heads), :]
    ws = jnp.transpose(jnp.concatenate([mine, jnp.zeros((LANES - heads, rows), f32)], axis=0))
    kl = functools.reduce(jnp.add, [s[keys : keys + 1, :] for s in sgs])
    kl = kl if first else kl_in_ref[...] + kl
    if n_lse:
        kl = kl + combine_lse([r[...] for r in lses]) * (1.0 / LOG2E)
    kl_ref[...] = kl
    unit = min(heads, 4)
    iks = [ref[...].astype(bf16) for ref in iks]
    sgts = [jnp.transpose(ref[:keys, :]) for ref in sgs]
    for start in range(0, heads, unit):
        js = range(start, start + unit)
        iq = jnp.concatenate([iq_ref[:, lanes_at(base + j, ID)] for j in js], axis=0)
        out = None
        for ik, sgt in zip(iks, sgts):
            z = dot_nt(iq, ik)
            dz = jnp.concatenate(
                [
                    jnp.where(z[i * rows : (i + 1) * rows] > 0, sgt * ws[:, j : j + 1], 0.0).astype(bf16)
                    for i, j in enumerate(js)
                ],
                axis=0,
            )
            g = dot_nn(dz, ik)
            out = g if out is None else out + g
        for i, j in enumerate(js):
            cols = slice(j * ID, (j + 1) * ID)
            g = out[i * rows : (i + 1) * rows]
            gq_ref[:, cols] = g if first else gq_in_ref[:, cols] + g


def index_grad_query(n_slots, sgs, iks, index_query, weight_t, lses, carry):
    rows, width = index_query.shape
    heads = width // ID
    mine = width // n_slots
    keys = iks[0].shape[0]
    first = carry is None
    carried = [] if first else list(carry)
    n = len(sgs)
    return pl.pallas_call(
        functools.partial(grad_query_kernel, n, first, len(lses)),
        grid=(1,),
        in_specs=[IN_VMEM] * (2 * n + 1)
        + [pl.BlockSpec(weight_t.shape, lambda i: (0, 0))]
        + [IN_VMEM] * (len(lses) + len(carried)),
        out_specs=[IN_VMEM, IN_VMEM],
        out_shape=[
            jax.ShapeDtypeStruct((rows, mine), f32),
            jax.ShapeDtypeStruct((1, rows), f32),
        ],
        scratch_shapes=[pltpu.VMEM((heads, rows), f32)],
        compiler_params=pltpu.CompilerParams(vmem_limit_bytes=20 * 1024 * 1024),
        cost_estimate=cost(4 * n * keys * rows * mine, n * (keys * ID * 8) + rows * mine * 8),
        name="index_grad_query",
    )(*sgs, *iks, index_query, weight_t, *lses, *carried)


def swap(value, axis, mask, size):
    return lax.ppermute(value, axis, [(i, i ^ mask) for i in range(size)])


def rotate(value, axis, by, size):
    return lax.ppermute(value, axis, [(i, (i + by) % size) for i in range(size)])


def butterfly_lse(value, size):
    pair = [value]
    for bit in reversed(range(size.bit_length() - 1)):
        here = combine_lse(pair)
        pair = [here, swap(here, "key", 1 << bit, size)]
    return pair


def summed_copies(value, n_head, n_query):
    steps = [("query", 1 << b, n_query) for b in range(n_query.bit_length() - 1)]
    steps += [("head", (2 << b) - 1, n_head) for b in range(n_head.bit_length() - 1)]
    for axis, mask, size in steps:
        value = value + swap(value, axis, mask, size)
    return value


def in_hbm(*values):
    return tuple(pltpu.with_memory_space_constraint(v, pltpu.HBM) for v in values)


def body(n_key, n_head, n_query, main_query, key_nope, key_rope, query_pos, key_pos, key_count,
         index_query, index_key, index_weight, row_cotangent):
    groups, rows, _ = main_query.shape
    keys = key_nope.shape[0]
    main_query, key_nope, rope_t, query_pos, key_row, key_count, weight_t, cotangent, narrow = in_hbm(
        main_query, key_nope, key_rope.T, query_pos, key_pos.reshape(1, keys), key_count,
        index_weight.T, row_cotangent.reshape(1, rows), index_key,
    )

    def gathered(value):
        if n_key == 4:
            near = swap(value, "key", 1, n_key)
            far = swap(value, "key", 2, n_key)
            across = swap(far, "key", 1, n_key)
            return [value, near, far, across]
        return list(lax.all_gather(value, "key"))

    lse, q, kk, bias = main_stats(main_query, key_nope, rope_t, query_pos, key_row, key_count)
    lses = butterfly_lse(lse, n_key)
    logits, index_lse, wm = index_logits(index_query, narrow, weight_t, bias)
    index_lses = butterfly_lse(index_lse, n_key)
    iks = gathered(index_key.astype(f32))

    if n_head == 4 and groups == 4:
        low, high = head_sums([2], 4, q, kk, bias, lses, parts=2)
        half = keys // 2
        low = rotate(low, "head", 1, 4)
        high = rotate(high, "head", 3, 4)
        up, down = head_sums([1, 3], 4, q, kk, bias, lses)
        up = up + jnp.pad(low, ((0, half), (0, 0)))
        down = down + jnp.pad(high, ((half, 0), (0, 0)))
        from_below = rotate(up, "head", 1, 4)
        from_above = rotate(down, "head", 3, 4)
        own = head_sums([0], 4, q, kk, bias, lses)[0]
        parts = [own, from_below, from_above]
    else:
        tiles = jnp.stack([head_sums([g], groups, q, kk, bias, lses)[0] for g in range(groups)])
        tiles = jnp.roll(tiles, lax.axis_index("head"), axis=0)
        parts = [lax.psum_scatter(tiles, "head", scatter_dimension=0, tiled=True)[0]]

    sg, grad_key = index_grad_key(parts, index_lses, logits, wm, index_query, bias, cotangent)
    grad_key = summed_copies(grad_key, n_head, n_query)
    sgs = gathered(sg)
    carry = None
    for lo in range(0, n_key, 2):
        last = lo + 2 >= n_key
        carry = index_grad_query(
            n_key, sgs[lo : lo + 2], iks[lo : lo + 2], index_query, weight_t,
            index_lses if last else [], carry,
        )
    grad_query, kl = carry
    return kl.reshape(rows), grad_query, grad_key


def solution(mesh):
    sizes = (mesh.shape["key"], mesh.shape["head"], mesh.shape["query"])

    def step(*args):
        return body(*sizes, *args)

    return jax.shard_map(
        step,
        mesh=mesh,
        in_specs=(
            P(None, "query", "head"),
            P("key", "head"),
            P("key", None),
            P(None, "query"),
            P("key"),
            P("key"),
            P(("head", "query"), None),
            P("key", None),
            P(("head", "query"), None),
            P(("head", "query")),
        ),
        out_specs=(P(("head", "query")), P(("head", "query"), "key"), P("key", None)),
        check_vma=False,
    )
```

```python
import functools
import math
import jax
import jax.numpy as jnp
from jax import lax
from jax.experimental import pallas as pl
from jax.experimental.pallas import tpu as pltpu
from jax.sharding import PartitionSpec as P


H = 128
DNOPE = 128
DROPE = 64
ID = 128
KBLOCK = 32
DQK = 192
LANES = 128
PAIR = 2 * DQK
NEG = -1e30
SMALL = 2.0**-90
LARGE = 2.0**100
BIG = 2**30
LOG2E = math.log2(math.e)
SCALE_MAIN = DQK ** (-0.5) * LOG2E
SCALE_INDEX = ID ** (-0.5)

f32 = jnp.float32
bf16 = jnp.bfloat16
IN_VMEM = pl.BlockSpec(memory_space=pltpu.VMEM)


def dot_nt(a, b):
    return lax.dot_general(a, b, (((1,), (1,)), ((), ())), preferred_element_type=f32)


def dot_nn(a, b):
    return lax.dot_general(a, b, (((1,), (0,)), ((), ())), preferred_element_type=f32)


def cost(flops, bytes_accessed, transcendentals=0):
    return pl.CostEstimate(
        flops=int(flops), bytes_accessed=int(bytes_accessed), transcendentals=int(transcendentals)
    )


def combine_lse(parts):
    if len(parts) == 1:
        return parts[0]
    top = functools.reduce(jnp.maximum, parts)
    return top + jnp.log2(functools.reduce(jnp.add, [jnp.exp2(p - top) for p in parts]))


def key_limit_column(count_ref, row, keys):
    lane = lax.broadcasted_iota(jnp.int32, (1, keys), 1)
    block = lane // KBLOCK
    limit = jnp.zeros((1, keys), jnp.int32)
    for b in range(keys // KBLOCK):
        limit = jnp.where(block == b, count_ref[b], limit)
    live = (lane % KBLOCK) < limit
    row = jnp.where(live, row, BIG)
    return jnp.transpose(jnp.broadcast_to(row, (8, keys)))[:, :1]


def main_keys(nope, parity, even_ref, odd_ref):
    if parity == 0:
        return jnp.concatenate([nope, even_ref[...]], axis=1)
    turned = jnp.concatenate([nope[:, DROPE:], nope[:, :DROPE]], axis=1)
    low = lax.broadcasted_iota(jnp.int32, turned.shape, 1) < DROPE
    first = jnp.where(low, jnp.zeros_like(turned), turned)
    second = jnp.where(low, turned, odd_ref[...])
    return jnp.concatenate([first, second], axis=1)


def lanes_at(index, width):
    return pl.ds(pl.multiple_of(index * width, LANES), width)


def stats_kernel(per, count_hbm, q_hbm, kn_hbm, rope_hbm, qpos_hbm, kpos_hbm,
                 lse_ref, q_ref, kk_ref, bias_ref,
                 kn_ref, rope_ref, qpos_ref, kpos_ref, even_ref, odd_ref, none_ref, bad_ref,
                 count_ref, small_sem, q_sem, kn_sem):
    keys = kn_ref.shape[0]
    groups, rows = q_ref.shape[0], q_ref.shape[1]
    pairs = q_ref.shape[2] // PAIR
    halves = [slice(2 * c * rows, (2 * c + 2) * rows) for c in range(groups // 2)]

    small = [
        pltpu.make_async_copy(src, dst, small_sem.at[i])
        for i, (src, dst) in enumerate(
            ((count_hbm, count_ref), (kpos_hbm, kpos_ref), (qpos_hbm, qpos_ref), (rope_hbm, rope_ref))
        )
    ]

    def large(i):
        q_at, k_at = lanes_at(i, PAIR), lanes_at(i, 2 * DNOPE)
        return (
            pltpu.make_async_copy(kn_hbm.at[:, k_at], kn_ref.at[:, k_at], kn_sem.at[i]),
            pltpu.make_async_copy(q_hbm.at[:, :, q_at], q_ref.at[:, :, q_at], q_sem.at[i]),
        )

    for copy in small:
        copy.start()
    for i in range(pairs):
        for copy in large(i):
            copy.start()
    for copy in small:
        copy.wait()

    rope = jnp.transpose(rope_ref[...].astype(f32)).astype(bf16)
    zero = jnp.zeros_like(rope)
    even_ref[...] = jnp.concatenate([rope, zero], axis=1)
    odd_ref[...] = jnp.concatenate([zero, rope], axis=1)
    column = key_limit_column(count_ref, kpos_ref[...], keys)
    for g in range(groups):
        valid = column <= qpos_ref[g : g + 1, :]
        bias = jnp.where(valid, 0.0, NEG)
        bias_ref[:, g * rows : (g + 1) * rows] = bias
        none_ref[:, g * rows : (g + 1) * rows] = jnp.where(
            jnp.max(bias, axis=0, keepdims=True) < 0, 1.0, 0.0
        )
    bad_ref[...] = jnp.zeros_like(bad_ref)

    def scores(kk, q3, c):
        q = q3.reshape(2 * rows, 2 * LANES)
        return dot_nt(kk, q) * SCALE_MAIN + bias_ref[:, halves[c]]

    def query(pair, a, c):
        at = pl.ds(pl.multiple_of(pair * PAIR + a * LANES, LANES), 2 * LANES)
        return q_ref[2 * c : 2 * c + 2, :, at]

    def step(i, carry):
        for p in range(per):
            pair = i * per + p
            for copy in large(pair):
                copy.wait()
        for p in range(per):
            pair = i * per + p
            for a in range(2):
                kk = main_keys(kn_ref[:, lanes_at(2 * pair + a, DNOPE)], a, even_ref, odd_ref)
                kk_ref[:, lanes_at(2 * pair + a, 2 * LANES)] = kk
                for c, cols in enumerate(halves):
                    s = scores(kk, query(pair, a, c), c)
                    total = jnp.sum(jnp.exp2(s), axis=0, keepdims=True)
                    fine = (total >= SMALL) & (total <= LARGE)
                    skip = none_ref[:, cols] > 0
                    bad_ref[:, cols] += jnp.where(fine | skip, 0.0, 1.0)
                    lse_ref[pl.ds(2 * pair + a, 1), cols] = jnp.where(skip, NEG, jnp.log2(total))
        return carry

    lax.fori_loop(0, pairs // per, step, 0)

    @pl.when(jnp.max(bad_ref[...]) > 0)
    def _():
        def again(pair, carry):
            for a in range(2):
                kk = kk_ref[:, lanes_at(2 * pair + a, 2 * LANES)]
                for c, cols in enumerate(halves):
                    s = scores(kk, query(pair, a, c), c)
                    top = jnp.max(s, axis=0, keepdims=True)
                    total = jnp.sum(jnp.exp2(s - top), axis=0, keepdims=True)
                    lse_ref[pl.ds(2 * pair + a, 1), cols] = top + jnp.log2(total)
            return carry

        lax.fori_loop(0, pairs, again, 0)


def main_stats(main_query, key_nope, rope_t, query_pos, key_pos, key_count):
    groups, rows, width = main_query.shape
    heads = width // DQK
    keys = key_nope.shape[0]
    total = groups * rows
    return pl.pallas_call(
        functools.partial(stats_kernel, 2),
        in_specs=[pl.BlockSpec(memory_space=pltpu.HBM)] * 6,
        out_specs=[IN_VMEM] * 4,
        out_shape=[
            jax.ShapeDtypeStruct((heads, total), f32),
            jax.ShapeDtypeStruct(main_query.shape, bf16),
            jax.ShapeDtypeStruct((keys, heads * 2 * LANES), bf16),
            jax.ShapeDtypeStruct((keys, total), f32),
        ],
        scratch_shapes=[
            pltpu.VMEM(key_nope.shape, bf16),
            pltpu.VMEM(rope_t.shape, bf16),
            pltpu.VMEM(query_pos.shape, jnp.int32),
            pltpu.VMEM(key_pos.shape, jnp.int32),
            pltpu.VMEM((keys, LANES), bf16),
            pltpu.VMEM((keys, LANES), bf16),
            pltpu.VMEM((1, total), f32),
            pltpu.VMEM((1, total), f32),
            pltpu.SMEM(key_count.shape, jnp.int32),
            pltpu.SemaphoreType.DMA((4,)),
            pltpu.SemaphoreType.DMA((heads // 2,)),
            pltpu.SemaphoreType.DMA((heads // 2,)),
        ],
        compiler_params=pltpu.CompilerParams(vmem_limit_bytes=16 * 1024 * 1024),
        cost_estimate=cost(
            heads * total * keys * 512, main_query.size * 2 + key_nope.size * 2, heads * total * keys
        ),
        name="main_stats",
    )(key_count, main_query, key_nope, rope_t, query_pos, key_pos)


def target_kernel(n_lse, masks, per, parts, q_ref, kk_ref, bias_ref, *refs):
    lse_refs = refs[:n_lse]
    out_refs = refs[n_lse:-1]
    glob_ref = refs[-1]
    n_groups = len(masks)
    keys = kk_ref.shape[0]
    rows = q_ref.shape[1]
    pairs = q_ref.shape[2] // PAIR
    size = keys // parts
    me = lax.axis_index("head")
    ids = [lax.bitwise_xor(me, mask) for mask in masks]
    tiles = [
        (g, slice(i * size, (i + 1) * size), out_refs[g * parts + i])
        for g in range(n_groups)
        for i in range(parts)
    ]
    for g in range(n_groups):
        at = lanes_at(ids[g], rows)
        glob_ref[:, g * rows : (g + 1) * rows] = combine_lse([r[:, at] for r in lse_refs])
    for ref in out_refs:
        ref[...] = jnp.zeros_like(ref)

    def step(i, carry):
        for p in range(per):
            pair = i * per + p
            acc = None
            for a in range(2):
                kk = kk_ref[:, lanes_at(2 * pair + a, 2 * LANES)]
                at = pl.ds(pl.multiple_of(pair * PAIR + a * LANES, LANES), 2 * LANES)
                qs = [q_ref[g, :, at] for g in ids]
                q = qs[0] if n_groups == 1 else jnp.concatenate(qs, axis=0)
                lse = glob_ref[pl.ds(2 * pair + a, 1), :]
                e = jnp.exp2(dot_nt(kk, q) * SCALE_MAIN - lse)
                acc = e if acc is None else acc + e
            for g, at, ref in tiles:
                ref[...] += acc[at, g * rows : (g + 1) * rows]
        return carry

    lax.fori_loop(0, pairs // per, step, 0)
    for g, at, ref in tiles:
        ref[...] = jnp.where(bias_ref[at, lanes_at(ids[g], rows)] < 0, 0.0, ref[...])


def head_sums(masks, q, kk, bias, lses, parts=1):
    _, rows, width = q.shape
    heads = width // DQK
    keys = kk.shape[0]
    n = len(masks)
    return pl.pallas_call(
        functools.partial(target_kernel, len(lses), masks, 4 // n, parts),
        in_specs=[IN_VMEM] * (3 + len(lses)),
        out_specs=[IN_VMEM] * (n * parts),
        out_shape=[jax.ShapeDtypeStruct((keys // parts, rows), f32)] * (n * parts),
        scratch_shapes=[pltpu.VMEM((heads, n * rows), f32)],
        compiler_params=pltpu.CompilerParams(vmem_limit_bytes=16 * 1024 * 1024),
        cost_estimate=cost(
            heads * n * rows * keys * 512, heads * n * rows * keys // 16, heads * n * rows * keys
        ),
        name="head_sums",
    )(q, kk, bias, *lses)


def logits_kernel(per, iq_ref, ik_ref, wt_ref, bias_ref, logits_ref, lse_ref, wm_ref, w_ref):
    rows, width = iq_ref.shape
    w_ref[...] = wt_ref[...].astype(f32)
    logits_ref[...] = jnp.zeros_like(logits_ref)

    def step(i, carry):
        for p in range(per):
            first = 2 * (i * per + p)
            q = jnp.concatenate([iq_ref[:, lanes_at(first + a, ID)] for a in range(2)], axis=0)
            z = dot_nt(ik_ref[...], q)
            w = jnp.concatenate([w_ref[pl.ds(first + a, 1), :] for a in range(2)], axis=1)
            masked = jnp.where(z > 0, w, 0.0)
            wm_ref[:, lanes_at(i * per + p, 2 * rows)] = masked.astype(bf16)
            r = z * masked
            logits_ref[...] += r[:, :rows] + r[:, rows:]
        return carry

    lax.fori_loop(0, width // (2 * ID * per), step, 0)
    logits = logits_ref[...] * SCALE_INDEX
    logits_ref[...] = logits
    valid = bias_ref[:, lanes_at(lax.axis_index("head"), rows)] == 0
    s = jnp.where(valid, logits * LOG2E, NEG)
    top = jnp.max(s, axis=0, keepdims=True)
    lse_ref[...] = top + jnp.log2(jnp.sum(jnp.exp2(s - top), axis=0, keepdims=True))


def index_logits(index_query, index_key, weight_t, bias):
    rows, width = index_query.shape
    keys = index_key.shape[0]
    whole = lambda i: (0, 0)
    return pl.pallas_call(
        functools.partial(logits_kernel, 4),
        grid=(1,),
        in_specs=[
            IN_VMEM,
            pl.BlockSpec(index_key.shape, whole),
            pl.BlockSpec(weight_t.shape, whole),
            IN_VMEM,
        ],
        out_specs=[IN_VMEM] * 3,
        out_shape=[
            jax.ShapeDtypeStruct((keys, rows), f32),
            jax.ShapeDtypeStruct((1, rows), f32),
            jax.ShapeDtypeStruct((keys, (width // ID) * rows), bf16),
        ],
        scratch_shapes=[pltpu.VMEM((width // ID, rows), f32)],
        compiler_params=pltpu.CompilerParams(vmem_limit_bytes=16 * 1024 * 1024),
        cost_estimate=cost(2 * keys * rows * width, rows * width * 2 + keys * rows * width // ID * 2),
        name="index_logits",
    )(index_query, index_key, weight_t, bias)


def grad_key_kernel(n_parts, n_lse, per, *refs):
    parts = refs[:n_parts]
    lses = refs[n_parts : n_parts + n_lse]
    logits_ref, wm_ref, iq_ref, bias_ref, cot_ref, sg_ref, lo_ref, hi_ref = refs[n_parts + n_lse :]
    keys, rows = logits_ref.shape
    width = iq_ref.shape[1]

    valid = bias_ref[:, lanes_at(lax.axis_index("head"), rows)] == 0
    target = functools.reduce(jnp.add, [p[...] for p in parts]) * (1.0 / H)
    logits = logits_ref[...]
    lse2 = combine_lse([r[...] for r in lses])
    qprob = jnp.where(valid, jnp.exp2(logits * LOG2E - lse2), 0.0)
    sg_ref[:keys, :] = SCALE_INDEX * (cot_ref[...] * (qprob - target))
    live = target > 0
    terms = jnp.where(live, target * (jnp.log(jnp.where(live, target, 1.0)) - logits), 0.0)
    kl = jnp.sum(terms, axis=0, keepdims=True)
    sg_ref[keys:, :] = jnp.broadcast_to(kl, (8, rows))
    lo_ref[...] = jnp.zeros_like(lo_ref)
    hi_ref[...] = jnp.zeros_like(hi_ref)

    def step(i, carry):
        for p in range(per):
            dz = []
            qs = []
            for a in range(2):
                j = 2 * (i * per + p) + a
                wm = wm_ref[:, lanes_at(j, rows)].astype(f32)
                dz.append((sg_ref[:keys, :] * wm).astype(bf16))
                qs.append(iq_ref[:, lanes_at(j, ID)])
            g = dot_nn(jnp.concatenate(dz, axis=1), jnp.concatenate(qs, axis=0))
            lo_ref[...] += g[: keys // 2]
            hi_ref[...] += g[keys // 2 :]
        return carry

    lax.fori_loop(0, width // (2 * ID * per), step, 0)


def index_grad_key(parts, lses, logits, wm, index_query, bias, cotangent):
    rows, width = index_query.shape
    keys = logits.shape[0]
    return pl.pallas_call(
        functools.partial(grad_key_kernel, len(parts), len(lses), 8),
        grid=(1,),
        in_specs=[IN_VMEM] * (len(parts) + len(lses) + 4)
        + [pl.BlockSpec((1, rows), lambda i: (0, 0))],
        out_specs=[IN_VMEM] * 3,
        out_shape=[
            jax.ShapeDtypeStruct((keys + 8, rows), f32),
            jax.ShapeDtypeStruct((keys // 2, ID), f32),
            jax.ShapeDtypeStruct((keys // 2, ID), f32),
        ],
        compiler_params=pltpu.CompilerParams(vmem_limit_bytes=16 * 1024 * 1024),
        cost_estimate=cost(2 * keys * rows * width, rows * width * 2 + keys * rows * width // ID * 2),
        name="index_grad_key",
    )(*parts, *lses, logits, wm, index_query, bias, cotangent)


def grad_query_kernel(n_shards, first, n_lse, *refs):
    sgs = refs[:n_shards]
    iks = refs[n_shards : 2 * n_shards]
    iq_ref, w_ref = refs[2 * n_shards : 2 * n_shards + 2]
    rest = refs[2 * n_shards + 2 :]
    lses = rest[:n_lse]
    rest = rest[n_lse:]
    if first:
        gq_ref, kl_ref, ws_ref = rest
    else:
        gq_in_ref, kl_in_ref, gq_ref, kl_ref, ws_ref = rest
    rows = iq_ref.shape[0]
    heads = gq_ref.shape[1] // ID
    keys = iks[0].shape[0]
    base = lax.axis_index("key") * heads
    ws_ref[...] = w_ref[...].astype(f32)
    mine = ws_ref[pl.ds(base, heads), :]
    ws = jnp.transpose(jnp.concatenate([mine, jnp.zeros((LANES - heads, rows), f32)], axis=0))
    kl = functools.reduce(jnp.add, [s[keys : keys + 1, :] for s in sgs])
    kl = kl if first else kl_in_ref[...] + kl
    if n_lse:
        kl = kl + combine_lse([r[...] for r in lses]) * (1.0 / LOG2E)
    kl_ref[...] = kl
    unit = min(heads, 4)
    iks = [ref[...].astype(bf16) for ref in iks]
    sgts = [jnp.transpose(ref[:keys, :]) for ref in sgs]
    for start in range(0, heads, unit):
        js = range(start, start + unit)
        iq = jnp.concatenate([iq_ref[:, lanes_at(base + j, ID)] for j in js], axis=0)
        out = None
        for ik, sgt in zip(iks, sgts):
            z = dot_nt(iq, ik)
            dz = jnp.concatenate(
                [
                    jnp.where(z[i * rows : (i + 1) * rows] > 0, sgt * ws[:, j : j + 1], 0.0).astype(bf16)
                    for i, j in enumerate(js)
                ],
                axis=0,
            )
            g = dot_nn(dz, ik)
            out = g if out is None else out + g
        for i, j in enumerate(js):
            cols = slice(j * ID, (j + 1) * ID)
            g = out[i * rows : (i + 1) * rows]
            gq_ref[:, cols] = g if first else gq_in_ref[:, cols] + g


def index_grad_query(n_slots, sgs, iks, index_query, weight_t, lses, carry):
    rows, width = index_query.shape
    heads = width // ID
    mine = width // n_slots
    keys = iks[0].shape[0]
    first = carry is None
    carried = [] if first else list(carry)
    n = len(sgs)
    return pl.pallas_call(
        functools.partial(grad_query_kernel, n, first, len(lses)),
        grid=(1,),
        in_specs=[IN_VMEM] * (2 * n + 1)
        + [pl.BlockSpec(weight_t.shape, lambda i: (0, 0))]
        + [IN_VMEM] * (len(lses) + len(carried)),
        out_specs=[IN_VMEM, IN_VMEM],
        out_shape=[
            jax.ShapeDtypeStruct((rows, mine), f32),
            jax.ShapeDtypeStruct((1, rows), f32),
        ],
        scratch_shapes=[pltpu.VMEM((heads, rows), f32)],
        compiler_params=pltpu.CompilerParams(vmem_limit_bytes=20 * 1024 * 1024),
        cost_estimate=cost(4 * n * keys * rows * mine, n * (keys * ID * 8) + rows * mine * 8),
        name="index_grad_query",
    )(*sgs, *iks, index_query, weight_t, *lses, *carried)


def swap(value, axis, mask, size):
    return lax.ppermute(value, axis, [(i, i ^ mask) for i in range(size)])


def butterfly_lse(value, size):
    pair = [value]
    for bit in reversed(range(size.bit_length() - 1)):
        here = combine_lse(pair)
        pair = [here, swap(here, "key", 1 << bit, size)]
    return pair


def summed_copies(pieces, n_head, n_query):
    steps = [("head", (2 << b) - 1, n_head) for b in reversed(range(n_head.bit_length() - 1))]
    steps += [("query", 1 << b, n_query) for b in range(n_query.bit_length() - 1)]
    steps = steps[:1] + steps[2:] + steps[1:2]
    for number in range(len(steps)):
        moved = []
        for i, piece in enumerate(pieces):
            moved.append(swap(piece, *steps[(number - i) % len(steps)]))
        pieces = [piece + other for piece, other in zip(pieces, moved)]
    return jnp.concatenate(pieces, axis=0)


def in_hbm(*values):
    return tuple(pltpu.with_memory_space_constraint(v, pltpu.HBM) for v in values)


def body(n_key, n_head, n_query, main_query, key_nope, key_rope, query_pos, key_pos, key_count,
         index_query, index_key, index_weight, row_cotangent):
    groups, rows, _ = main_query.shape
    keys = key_nope.shape[0]
    main_query, key_nope, rope_t, query_pos, key_row, key_count, weight_t, cotangent, narrow = in_hbm(
        main_query, key_nope, key_rope.T, query_pos, key_pos.reshape(1, keys), key_count,
        index_weight.T, row_cotangent.reshape(1, rows), index_key,
    )

    def gathered(value):
        if n_key == 4:
            near = swap(value, "key", 1, n_key)
            far = swap(value, "key", 2, n_key)
            across = swap(far, "key", 1, n_key)
            return [value, near, far, across]
        return list(lax.all_gather(value, "key"))

    lse, q, kk, bias = main_stats(main_query, key_nope, rope_t, query_pos, key_row, key_count)
    lses = butterfly_lse(lse, n_key)
    logits, index_lse, wm = index_logits(index_query, narrow, weight_t, bias)
    index_lses = butterfly_lse(index_lse, n_key)
    iks = gathered(index_key.astype(f32))

    half = keys // 2
    if n_head == 4 and groups == 4:
        low, high = head_sums([2], q, kk, bias, lses, parts=2)
        low = swap(low, "head", 1, 4)
        high = swap(high, "head", 3, 4)
        up, down = head_sums([1, 3], q, kk, bias, lses)
        up = up + jnp.pad(high, ((half, 0), (0, 0)))
        down = down + jnp.pad(low, ((0, half), (0, 0)))
        from_up = swap(up, "head", 1, 4)
        from_down = swap(down, "head", 3, 4)
        own = head_sums([0], q, kk, bias, lses)[0]
        parts = [own, from_up, from_down]
    else:
        z = lax.axis_index("head")
        tiles = jnp.stack([head_sums([g], q, kk, bias, lses)[0] for g in range(groups)])
        tiles = tiles[jnp.bitwise_xor(jnp.arange(groups), z)]
        parts = [lax.psum_scatter(tiles, "head", scatter_dimension=0, tiled=True)[0]]

    sg, *grad_key = index_grad_key(parts, index_lses, logits, wm, index_query, bias, cotangent)
    grad_key = summed_copies(grad_key, n_head, n_query)
    sgs = gathered(sg)
    carry = None
    for lo in range(0, n_key, 2):
        last = lo + 2 >= n_key
        carry = index_grad_query(
            n_key, sgs[lo : lo + 2], iks[lo : lo + 2], index_query, weight_t,
            index_lses if last else [], carry,
        )
    grad_query, kl = carry
    return kl.reshape(rows), grad_query, grad_key


def solution(mesh):
    sizes = (mesh.shape["key"], mesh.shape["head"], mesh.shape["query"])

    def step(*args):
        return body(*sizes, *args)

    return jax.shard_map(
        step,
        mesh=mesh,
        in_specs=(
            P(None, "query", "head"),
            P("key", "head"),
            P("key", None),
            P(None, "query"),
            P("key"),
            P("key"),
            P(("head", "query"), None),
            P("key", None),
            P(("head", "query"), None),
            P(("head", "query")),
        ),
        out_specs=(P(("head", "query")), P(("head", "query"), "key"), P("key", None)),
        check_vma=False,
    )
```

```python
import functools
import math
import jax
import jax.numpy as jnp
from jax import lax
from jax.experimental import pallas as pl
from jax.experimental.pallas import tpu as pltpu
from jax.sharding import PartitionSpec as P


H = 128
DNOPE = 128
DROPE = 64
ID = 128
KBLOCK = 32
DQK = 192
LANES = 128
PAIR = 2 * DQK
NEG = -1e30
SMALL = 2.0**-90
LARGE = 2.0**100
BIG = 2**30
LOG2E = math.log2(math.e)
SCALE_MAIN = DQK ** (-0.5) * LOG2E
SCALE_INDEX = ID ** (-0.5)

f32 = jnp.float32
bf16 = jnp.bfloat16
IN_VMEM = pl.BlockSpec(memory_space=pltpu.VMEM)


def dot_nt(a, b):
    return lax.dot_general(a, b, (((1,), (1,)), ((), ())), preferred_element_type=f32)


def dot_nn(a, b):
    return lax.dot_general(a, b, (((1,), (0,)), ((), ())), preferred_element_type=f32)


def cost(flops, bytes_accessed, transcendentals=0):
    return pl.CostEstimate(
        flops=int(flops), bytes_accessed=int(bytes_accessed), transcendentals=int(transcendentals)
    )


def combine_lse(parts):
    if len(parts) == 1:
        return parts[0]
    top = functools.reduce(jnp.maximum, parts)
    return top + jnp.log2(functools.reduce(jnp.add, [jnp.exp2(p - top) for p in parts]))


def key_limit_column(count_ref, row, keys):
    lane = lax.broadcasted_iota(jnp.int32, (1, keys), 1)
    block = lane // KBLOCK
    limit = jnp.zeros((1, keys), jnp.int32)
    for b in range(keys // KBLOCK):
        limit = jnp.where(block == b, count_ref[b], limit)
    live = (lane % KBLOCK) < limit
    row = jnp.where(live, row, BIG)
    return jnp.transpose(jnp.broadcast_to(row, (8, keys)))[:, :1]


def main_keys(nope, parity, even_ref, odd_ref):
    if parity == 0:
        return jnp.concatenate([nope, even_ref[...]], axis=1)
    turned = jnp.concatenate([nope[:, DROPE:], nope[:, :DROPE]], axis=1)
    low = lax.broadcasted_iota(jnp.int32, turned.shape, 1) < DROPE
    first = jnp.where(low, jnp.zeros_like(turned), turned)
    second = jnp.where(low, turned, odd_ref[...])
    return jnp.concatenate([first, second], axis=1)


def lanes_at(index, width):
    return pl.ds(pl.multiple_of(index * width, LANES), width)


def stats_kernel(per, count_hbm, q_hbm, kn_hbm, rope_hbm, qpos_hbm, kpos_hbm,
                 lse_ref, q_ref, kk_ref, bias_ref,
                 kn_ref, rope_ref, qpos_ref, kpos_ref, even_ref, odd_ref, none_ref, bad_ref,
                 count_ref, small_sem, q_sem, kn_sem):
    keys = kn_ref.shape[0]
    groups, rows = q_ref.shape[0], q_ref.shape[1]
    pairs = q_ref.shape[2] // PAIR
    halves = [slice(2 * c * rows, (2 * c + 2) * rows) for c in range(groups // 2)]

    small = [
        pltpu.make_async_copy(src, dst, small_sem.at[i])
        for i, (src, dst) in enumerate(
            ((count_hbm, count_ref), (kpos_hbm, kpos_ref), (qpos_hbm, qpos_ref), (rope_hbm, rope_ref))
        )
    ]

    def large(i):
        q_at, k_at = lanes_at(i, PAIR), lanes_at(i, 2 * DNOPE)
        return (
            pltpu.make_async_copy(kn_hbm.at[:, k_at], kn_ref.at[:, k_at], kn_sem.at[i]),
            pltpu.make_async_copy(q_hbm.at[:, :, q_at], q_ref.at[:, :, q_at], q_sem.at[i]),
        )

    for copy in small:
        copy.start()
    for i in range(pairs):
        for copy in large(i):
            copy.start()
    for copy in small:
        copy.wait()

    rope = jnp.transpose(rope_ref[...].astype(f32)).astype(bf16)
    zero = jnp.zeros_like(rope)
    even_ref[...] = jnp.concatenate([rope, zero], axis=1)
    odd_ref[...] = jnp.concatenate([zero, rope], axis=1)
    column = key_limit_column(count_ref, kpos_ref[...], keys)
    for g in range(groups):
        valid = column <= qpos_ref[g : g + 1, :]
        bias = jnp.where(valid, 0.0, NEG)
        bias_ref[:, g * rows : (g + 1) * rows] = bias
        none_ref[:, g * rows : (g + 1) * rows] = jnp.where(
            jnp.max(bias, axis=0, keepdims=True) < 0, 1.0, 0.0
        )
    bad_ref[...] = jnp.zeros_like(bad_ref)

    def scores(kk, q3, c):
        q = q3.reshape(2 * rows, 2 * LANES)
        return dot_nt(kk, q) * SCALE_MAIN + bias_ref[:, halves[c]]

    def query(pair, a, c):
        at = pl.ds(pl.multiple_of(pair * PAIR + a * LANES, LANES), 2 * LANES)
        return q_ref[2 * c : 2 * c + 2, :, at]

    def step(i, carry):
        for p in range(per):
            pair = i * per + p
            for copy in large(pair):
                copy.wait()
        for p in range(per):
            pair = i * per + p
            for a in range(2):
                kk = main_keys(kn_ref[:, lanes_at(2 * pair + a, DNOPE)], a, even_ref, odd_ref)
                kk_ref[:, lanes_at(2 * pair + a, 2 * LANES)] = kk
                for c, cols in enumerate(halves):
                    s = scores(kk, query(pair, a, c), c)
                    total = jnp.sum(jnp.exp2(s), axis=0, keepdims=True)
                    fine = (total >= SMALL) & (total <= LARGE)
                    skip = none_ref[:, cols] > 0
                    bad_ref[:, cols] += jnp.where(fine | skip, 0.0, 1.0)
                    lse_ref[pl.ds(2 * pair + a, 1), cols] = jnp.where(skip, NEG, jnp.log2(total))
        return carry

    lax.fori_loop(0, pairs // per, step, 0)

    @pl.when(jnp.max(bad_ref[...]) > 0)
    def _():
        def again(pair, carry):
            for a in range(2):
                kk = kk_ref[:, lanes_at(2 * pair + a, 2 * LANES)]
                for c, cols in enumerate(halves):
                    s = scores(kk, query(pair, a, c), c)
                    top = jnp.max(s, axis=0, keepdims=True)
                    total = jnp.sum(jnp.exp2(s - top), axis=0, keepdims=True)
                    lse_ref[pl.ds(2 * pair + a, 1), cols] = top + jnp.log2(total)
            return carry

        lax.fori_loop(0, pairs, again, 0)


def main_stats(main_query, key_nope, rope_t, query_pos, key_pos, key_count):
    groups, rows, width = main_query.shape
    heads = width // DQK
    keys = key_nope.shape[0]
    total = groups * rows
    return pl.pallas_call(
        functools.partial(stats_kernel, 2),
        in_specs=[pl.BlockSpec(memory_space=pltpu.HBM)] * 6,
        out_specs=[IN_VMEM] * 4,
        out_shape=[
            jax.ShapeDtypeStruct((heads, total), f32),
            jax.ShapeDtypeStruct(main_query.shape, bf16),
            jax.ShapeDtypeStruct((keys, heads * 2 * LANES), bf16),
            jax.ShapeDtypeStruct((keys, total), f32),
        ],
        scratch_shapes=[
            pltpu.VMEM(key_nope.shape, bf16),
            pltpu.VMEM(rope_t.shape, bf16),
            pltpu.VMEM(query_pos.shape, jnp.int32),
            pltpu.VMEM(key_pos.shape, jnp.int32),
            pltpu.VMEM((keys, LANES), bf16),
            pltpu.VMEM((keys, LANES), bf16),
            pltpu.VMEM((1, total), f32),
            pltpu.VMEM((1, total), f32),
            pltpu.SMEM(key_count.shape, jnp.int32),
            pltpu.SemaphoreType.DMA((4,)),
            pltpu.SemaphoreType.DMA((heads // 2,)),
            pltpu.SemaphoreType.DMA((heads // 2,)),
        ],
        compiler_params=pltpu.CompilerParams(vmem_limit_bytes=16 * 1024 * 1024),
        cost_estimate=cost(
            heads * total * keys * 512, main_query.size * 2 + key_nope.size * 2, heads * total * keys
        ),
        name="main_stats",
    )(key_count, main_query, key_nope, rope_t, query_pos, key_pos)


def target_kernel(n_lse, masks, per, parts, q_ref, kk_ref, bias_ref, *refs):
    lse_refs = refs[:n_lse]
    out_refs = refs[n_lse:-1]
    glob_ref = refs[-1]
    n_groups = len(masks)
    keys = kk_ref.shape[0]
    rows = q_ref.shape[1]
    pairs = q_ref.shape[2] // PAIR
    size = keys // parts
    me = lax.axis_index("head")
    ids = [lax.bitwise_xor(me, mask) for mask in masks]
    tiles = [
        (g, slice(i * size, (i + 1) * size), out_refs[g * parts + i])
        for g in range(n_groups)
        for i in range(parts)
    ]
    for g in range(n_groups):
        at = lanes_at(ids[g], rows)
        glob_ref[:, g * rows : (g + 1) * rows] = combine_lse([r[:, at] for r in lse_refs])
    for ref in out_refs:
        ref[...] = jnp.zeros_like(ref)

    def step(i, carry):
        for p in range(per):
            pair = i * per + p
            acc = None
            for a in range(2):
                kk = kk_ref[:, lanes_at(2 * pair + a, 2 * LANES)]
                at = pl.ds(pl.multiple_of(pair * PAIR + a * LANES, LANES), 2 * LANES)
                qs = [q_ref[g, :, at] for g in ids]
                q = qs[0] if n_groups == 1 else jnp.concatenate(qs, axis=0)
                lse = glob_ref[pl.ds(2 * pair + a, 1), :]
                e = jnp.exp2(dot_nt(kk, q) * SCALE_MAIN - lse)
                acc = e if acc is None else acc + e
            for g, at, ref in tiles:
                ref[...] += acc[at, g * rows : (g + 1) * rows]
        return carry

    lax.fori_loop(0, pairs // per, step, 0)
    for g, at, ref in tiles:
        ref[...] = jnp.where(bias_ref[at, lanes_at(ids[g], rows)] < 0, 0.0, ref[...])


def head_sums(masks, q, kk, bias, lses, parts=1):
    _, rows, width = q.shape
    heads = width // DQK
    keys = kk.shape[0]
    n = len(masks)
    return pl.pallas_call(
        functools.partial(target_kernel, len(lses), masks, 4 // n, parts),
        in_specs=[IN_VMEM] * (3 + len(lses)),
        out_specs=[IN_VMEM] * (n * parts),
        out_shape=[jax.ShapeDtypeStruct((keys // parts, rows), f32)] * (n * parts),
        scratch_shapes=[pltpu.VMEM((heads, n * rows), f32)],
        compiler_params=pltpu.CompilerParams(vmem_limit_bytes=16 * 1024 * 1024),
        cost_estimate=cost(
            heads * n * rows * keys * 512, heads * n * rows * keys // 16, heads * n * rows * keys
        ),
        name="head_sums",
    )(q, kk, bias, *lses)


def logits_kernel(per, iq_ref, ik_ref, wt_ref, bias_ref, logits_ref, lse_ref, wm_ref, w_ref):
    rows, width = iq_ref.shape
    w_ref[...] = wt_ref[...].astype(f32)
    logits_ref[...] = jnp.zeros_like(logits_ref)

    def step(i, carry):
        for p in range(per):
            first = 2 * (i * per + p)
            q = jnp.concatenate([iq_ref[:, lanes_at(first + a, ID)] for a in range(2)], axis=0)
            z = dot_nt(ik_ref[...], q)
            w = jnp.concatenate([w_ref[pl.ds(first + a, 1), :] for a in range(2)], axis=1)
            masked = jnp.where(z > 0, w, 0.0)
            wm_ref[:, lanes_at(i * per + p, 2 * rows)] = masked.astype(bf16)
            r = z * masked
            logits_ref[...] += r[:, :rows] + r[:, rows:]
        return carry

    lax.fori_loop(0, width // (2 * ID * per), step, 0)
    logits = logits_ref[...] * SCALE_INDEX
    logits_ref[...] = logits
    valid = bias_ref[:, lanes_at(lax.axis_index("head"), rows)] == 0
    s = jnp.where(valid, logits * LOG2E, NEG)
    top = jnp.max(s, axis=0, keepdims=True)
    lse_ref[...] = top + jnp.log2(jnp.sum(jnp.exp2(s - top), axis=0, keepdims=True))


def index_logits(index_query, index_key, weight_t, bias):
    rows, width = index_query.shape
    keys = index_key.shape[0]
    whole = lambda i: (0, 0)
    return pl.pallas_call(
        functools.partial(logits_kernel, 4),
        grid=(1,),
        in_specs=[
            IN_VMEM,
            pl.BlockSpec(index_key.shape, whole),
            pl.BlockSpec(weight_t.shape, whole),
            IN_VMEM,
        ],
        out_specs=[IN_VMEM] * 3,
        out_shape=[
            jax.ShapeDtypeStruct((keys, rows), f32),
            jax.ShapeDtypeStruct((1, rows), f32),
            jax.ShapeDtypeStruct((keys, (width // ID) * rows), bf16),
        ],
        scratch_shapes=[pltpu.VMEM((width // ID, rows), f32)],
        compiler_params=pltpu.CompilerParams(vmem_limit_bytes=16 * 1024 * 1024),
        cost_estimate=cost(2 * keys * rows * width, rows * width * 2 + keys * rows * width // ID * 2),
        name="index_logits",
    )(index_query, index_key, weight_t, bias)


def grad_key_kernel(n_parts, n_lse, per, *refs):
    parts = refs[:n_parts]
    lses = refs[n_parts : n_parts + n_lse]
    logits_ref, wm_ref, iq_ref, bias_ref, cot_ref, sg_ref, lo_ref, hi_ref = refs[n_parts + n_lse :]
    keys, rows = logits_ref.shape
    width = iq_ref.shape[1]

    valid = bias_ref[:, lanes_at(lax.axis_index("head"), rows)] == 0
    target = functools.reduce(jnp.add, [p[...] for p in parts]) * (1.0 / H)
    logits = logits_ref[...]
    lse2 = combine_lse([r[...] for r in lses])
    qprob = jnp.where(valid, jnp.exp2(logits * LOG2E - lse2), 0.0)
    sg_ref[:keys, :] = SCALE_INDEX * (cot_ref[...] * (qprob - target))
    live = target > 0
    terms = jnp.where(live, target * (jnp.log(jnp.where(live, target, 1.0)) - logits), 0.0)
    kl = jnp.sum(terms, axis=0, keepdims=True)
    sg_ref[keys:, :] = jnp.broadcast_to(kl, (8, rows))
    lo_ref[...] = jnp.zeros_like(lo_ref)
    hi_ref[...] = jnp.zeros_like(hi_ref)

    def step(i, carry):
        for p in range(per):
            dz = []
            qs = []
            for a in range(2):
                j = 2 * (i * per + p) + a
                wm = wm_ref[:, lanes_at(j, rows)].astype(f32)
                dz.append((sg_ref[:keys, :] * wm).astype(bf16))
                qs.append(iq_ref[:, lanes_at(j, ID)])
            g = dot_nn(jnp.concatenate(dz, axis=1), jnp.concatenate(qs, axis=0))
            lo_ref[...] += g[: keys // 2]
            hi_ref[...] += g[keys // 2 :]
        return carry

    lax.fori_loop(0, width // (2 * ID * per), step, 0)


def index_grad_key(parts, lses, logits, wm, index_query, bias, cotangent):
    rows, width = index_query.shape
    keys = logits.shape[0]
    return pl.pallas_call(
        functools.partial(grad_key_kernel, len(parts), len(lses), 8),
        grid=(1,),
        in_specs=[IN_VMEM] * (len(parts) + len(lses) + 4)
        + [pl.BlockSpec((1, rows), lambda i: (0, 0))],
        out_specs=[IN_VMEM] * 3,
        out_shape=[
            jax.ShapeDtypeStruct((keys + 8, rows), f32),
            jax.ShapeDtypeStruct((keys // 2, ID), f32),
            jax.ShapeDtypeStruct((keys // 2, ID), f32),
        ],
        compiler_params=pltpu.CompilerParams(vmem_limit_bytes=16 * 1024 * 1024),
        cost_estimate=cost(2 * keys * rows * width, rows * width * 2 + keys * rows * width // ID * 2),
        name="index_grad_key",
    )(*parts, *lses, logits, wm, index_query, bias, cotangent)


def grad_query_kernel(n_shards, first, n_lse, *refs):
    sgs = refs[:n_shards]
    iks = refs[n_shards : 2 * n_shards]
    iq_ref, w_ref = refs[2 * n_shards : 2 * n_shards + 2]
    rest = refs[2 * n_shards + 2 :]
    lses = rest[:n_lse]
    rest = rest[n_lse:]
    if first:
        gq_ref, kl_ref, ws_ref = rest
    else:
        gq_in_ref, kl_in_ref, gq_ref, kl_ref, ws_ref = rest
    rows = iq_ref.shape[0]
    heads = gq_ref.shape[1] // ID
    keys = iks[0].shape[0]
    base = lax.axis_index("key") * heads
    ws_ref[...] = w_ref[...].astype(f32)
    mine = ws_ref[pl.ds(base, heads), :]
    ws = jnp.transpose(jnp.concatenate([mine, jnp.zeros((LANES - heads, rows), f32)], axis=0))
    kl = functools.reduce(jnp.add, [s[keys : keys + 1, :] for s in sgs])
    kl = kl if first else kl_in_ref[...] + kl
    if n_lse:
        kl = kl + combine_lse([r[...] for r in lses]) * (1.0 / LOG2E)
    kl_ref[...] = kl
    unit = min(heads, 4)
    iks = [ref[...].astype(bf16) for ref in iks]
    sgts = [jnp.transpose(ref[:keys, :]) for ref in sgs]
    for start in range(0, heads, unit):
        js = range(start, start + unit)
        iq = jnp.concatenate([iq_ref[:, lanes_at(base + j, ID)] for j in js], axis=0)
        out = None
        for ik, sgt in zip(iks, sgts):
            z = dot_nt(iq, ik)
            dz = jnp.concatenate(
                [
                    jnp.where(z[i * rows : (i + 1) * rows] > 0, sgt * ws[:, j : j + 1], 0.0).astype(bf16)
                    for i, j in enumerate(js)
                ],
                axis=0,
            )
            g = dot_nn(dz, ik)
            out = g if out is None else out + g
        for i, j in enumerate(js):
            cols = slice(j * ID, (j + 1) * ID)
            g = out[i * rows : (i + 1) * rows]
            gq_ref[:, cols] = g if first else gq_in_ref[:, cols] + g


def index_grad_query(n_slots, sgs, iks, index_query, weight_t, lses, carry):
    rows, width = index_query.shape
    heads = width // ID
    mine = width // n_slots
    keys = iks[0].shape[0]
    first = carry is None
    carried = [] if first else list(carry)
    n = len(sgs)
    return pl.pallas_call(
        functools.partial(grad_query_kernel, n, first, len(lses)),
        grid=(1,),
        in_specs=[IN_VMEM] * (2 * n + 1)
        + [pl.BlockSpec(weight_t.shape, lambda i: (0, 0))]
        + [IN_VMEM] * (len(lses) + len(carried)),
        out_specs=[IN_VMEM, IN_VMEM],
        out_shape=[
            jax.ShapeDtypeStruct((rows, mine), f32),
            jax.ShapeDtypeStruct((1, rows), f32),
        ],
        scratch_shapes=[pltpu.VMEM((heads, rows), f32)],
        compiler_params=pltpu.CompilerParams(vmem_limit_bytes=20 * 1024 * 1024),
        cost_estimate=cost(4 * n * keys * rows * mine, n * (keys * ID * 8) + rows * mine * 8),
        name="index_grad_query",
    )(*sgs, *iks, index_query, weight_t, *lses, *carried)


def swap(value, axis, mask, size):
    return lax.ppermute(value, axis, [(i, i ^ mask) for i in range(size)])


def butterfly_lse(value, size):
    pair = [value]
    for bit in reversed(range(size.bit_length() - 1)):
        here = combine_lse(pair)
        pair = [here, swap(here, "key", 1 << bit, size)]
    return pair


def summed_copies(pieces, n_head, n_query):
    steps = [("head", (2 << b) - 1, n_head) for b in reversed(range(n_head.bit_length() - 1))]
    steps += [("query", 1 << b, n_query) for b in range(n_query.bit_length() - 1)]
    steps = steps[:1] + steps[2:] + steps[1:2]
    for number in range(len(steps)):
        moved = []
        for i, piece in enumerate(pieces):
            moved.append(swap(piece, *steps[(number - i) % len(steps)]))
        pieces = [piece + other for piece, other in zip(pieces, moved)]
    return jnp.concatenate(pieces, axis=0)


def in_hbm(*values):
    return tuple(pltpu.with_memory_space_constraint(v, pltpu.HBM) for v in values)


def body(n_key, n_head, n_query, main_query, key_nope, key_rope, query_pos, key_pos, key_count,
         index_query, index_key, index_weight, row_cotangent):
    groups, rows, _ = main_query.shape
    keys = key_nope.shape[0]
    main_query, key_nope, rope_t, query_pos, key_row, key_count, weight_t, cotangent, narrow = in_hbm(
        main_query, key_nope, key_rope.T, query_pos, key_pos.reshape(1, keys), key_count,
        index_weight.T, row_cotangent.reshape(1, rows), index_key,
    )

    def gathered(value):
        if n_key == 4:
            near = swap(value, "key", 1, n_key)
            far = swap(value, "key", 2, n_key)
            across = swap(far, "key", 1, n_key)
            return [value, near, far, across]
        return list(lax.all_gather(value, "key"))

    lse, q, kk, bias = main_stats(main_query, key_nope, rope_t, query_pos, key_row, key_count)
    lses = butterfly_lse(lse, n_key)
    logits, index_lse, wm = index_logits(index_query, narrow, weight_t, bias)
    index_lses = butterfly_lse(index_lse, n_key)
    iks = gathered(index_key.astype(f32))

    if n_head == 4 and groups == 4:
        across = head_sums([2], q, kk, bias, lses)[0]
        from_across = swap(across, "head", 2, 4)
        up, down = head_sums([1, 3], q, kk, bias, lses)
        from_up = swap(up, "head", 1, 4)
        from_down = swap(down, "head", 3, 4)
        own = head_sums([0], q, kk, bias, lses)[0]
        parts = [own, from_up, from_down, from_across]
    else:
        z = lax.axis_index("head")
        tiles = jnp.stack([head_sums([g], q, kk, bias, lses)[0] for g in range(groups)])
        tiles = tiles[jnp.bitwise_xor(jnp.arange(groups), z)]
        parts = [lax.psum_scatter(tiles, "head", scatter_dimension=0, tiled=True)[0]]

    sg, *grad_key = index_grad_key(parts, index_lses, logits, wm, index_query, bias, cotangent)
    grad_key = summed_copies(grad_key, n_head, n_query)
    sgs = gathered(sg)
    carry = None
    for lo in range(0, n_key, 2):
        last = lo + 2 >= n_key
        carry = index_grad_query(
            n_key, sgs[lo : lo + 2], iks[lo : lo + 2], index_query, weight_t,
            index_lses if last else [], carry,
        )
    grad_query, kl = carry
    return kl.reshape(rows), grad_query, grad_key


def solution(mesh):
    sizes = (mesh.shape["key"], mesh.shape["head"], mesh.shape["query"])

    def step(*args):
        return body(*sizes, *args)

    return jax.shard_map(
        step,
        mesh=mesh,
        in_specs=(
            P(None, "query", "head"),
            P("key", "head"),
            P("key", None),
            P(None, "query"),
            P("key"),
            P("key"),
            P(("head", "query"), None),
            P("key", None),
            P(("head", "query"), None),
            P(("head", "query")),
        ),
        out_specs=(P(("head", "query")), P(("head", "query"), "key"), P("key", None)),
        check_vma=False,
    )
```

```python
import functools
import math
import jax
import jax.numpy as jnp
from jax import lax
from jax.experimental import pallas as pl
from jax.experimental.pallas import tpu as pltpu
from jax.sharding import PartitionSpec as P


H = 128
DNOPE = 128
DROPE = 64
ID = 128
KBLOCK = 32
DQK = 192
LANES = 128
PAIR = 2 * DQK
NEG = -1e30
SMALL = 2.0**-90
LARGE = 2.0**100
BIG = 2**30
LOG2E = math.log2(math.e)
SCALE_MAIN = DQK ** (-0.5) * LOG2E
SCALE_INDEX = ID ** (-0.5)

f32 = jnp.float32
bf16 = jnp.bfloat16
IN_VMEM = pl.BlockSpec(memory_space=pltpu.VMEM)


def dot_nt(a, b):
    return lax.dot_general(a, b, (((1,), (1,)), ((), ())), preferred_element_type=f32)


def dot_nn(a, b):
    return lax.dot_general(a, b, (((1,), (0,)), ((), ())), preferred_element_type=f32)


def cost(flops, bytes_accessed, transcendentals=0):
    return pl.CostEstimate(
        flops=int(flops), bytes_accessed=int(bytes_accessed), transcendentals=int(transcendentals)
    )


def combine_lse(parts):
    if len(parts) == 1:
        return parts[0]
    top = functools.reduce(jnp.maximum, parts)
    return top + jnp.log2(functools.reduce(jnp.add, [jnp.exp2(p - top) for p in parts]))


def key_limit_column(count_ref, row, keys):
    lane = lax.broadcasted_iota(jnp.int32, (1, keys), 1)
    block = lane // KBLOCK
    limit = jnp.zeros((1, keys), jnp.int32)
    for b in range(keys // KBLOCK):
        limit = jnp.where(block == b, count_ref[b], limit)
    live = (lane % KBLOCK) < limit
    row = jnp.where(live, row, BIG)
    return jnp.transpose(jnp.broadcast_to(row, (8, keys)))[:, :1]


def main_keys(nope, parity, even_ref, odd_ref):
    if parity == 0:
        return jnp.concatenate([nope, even_ref[...]], axis=1)
    turned = jnp.concatenate([nope[:, DROPE:], nope[:, :DROPE]], axis=1)
    low = lax.broadcasted_iota(jnp.int32, turned.shape, 1) < DROPE
    first = jnp.where(low, jnp.zeros_like(turned), turned)
    second = jnp.where(low, turned, odd_ref[...])
    return jnp.concatenate([first, second], axis=1)


def lanes_at(index, width):
    return pl.ds(pl.multiple_of(index * width, LANES), width)


def stats_kernel(per, count_hbm, q_hbm, kn_hbm, rope_hbm, qpos_hbm, kpos_hbm, iq_hbm,
                 lse_ref, q_ref, kk_ref, bias_ref, iq_ref,
                 kn_ref, rope_ref, qpos_ref, kpos_ref, even_ref, odd_ref, none_ref, bad_ref,
                 count_ref, small_sem, q_sem, kn_sem, iq_sem):
    keys = kn_ref.shape[0]
    groups, rows = q_ref.shape[0], q_ref.shape[1]
    pairs = q_ref.shape[2] // PAIR
    halves = [slice(2 * c * rows, (2 * c + 2) * rows) for c in range(groups // 2)]

    small = [
        pltpu.make_async_copy(src, dst, small_sem.at[i])
        for i, (src, dst) in enumerate(
            ((count_hbm, count_ref), (kpos_hbm, kpos_ref), (qpos_hbm, qpos_ref), (rope_hbm, rope_ref))
        )
    ]

    def large(i):
        q_at, k_at = lanes_at(i, PAIR), lanes_at(i, 2 * DNOPE)
        return (
            pltpu.make_async_copy(kn_hbm.at[:, k_at], kn_ref.at[:, k_at], kn_sem.at[i]),
            pltpu.make_async_copy(q_hbm.at[:, :, q_at], q_ref.at[:, :, q_at], q_sem.at[i]),
        )

    for copy in small:
        copy.start()
    for i in range(pairs):
        for copy in large(i):
            copy.start()
    index_copy = pltpu.make_async_copy(iq_hbm, iq_ref, iq_sem)
    index_copy.start()
    for copy in small:
        copy.wait()

    rope = jnp.transpose(rope_ref[...].astype(f32)).astype(bf16)
    zero = jnp.zeros_like(rope)
    even_ref[...] = jnp.concatenate([rope, zero], axis=1)
    odd_ref[...] = jnp.concatenate([zero, rope], axis=1)
    column = key_limit_column(count_ref, kpos_ref[...], keys)
    for g in range(groups):
        valid = column <= qpos_ref[g : g + 1, :]
        bias = jnp.where(valid, 0.0, NEG)
        bias_ref[:, g * rows : (g + 1) * rows] = bias
        none_ref[:, g * rows : (g + 1) * rows] = jnp.where(
            jnp.max(bias, axis=0, keepdims=True) < 0, 1.0, 0.0
        )
    bad_ref[...] = jnp.zeros_like(bad_ref)

    def scores(kk, q3, c):
        q = q3.reshape(2 * rows, 2 * LANES)
        return dot_nt(kk, q) * SCALE_MAIN + bias_ref[:, halves[c]]

    def query(pair, a, c):
        at = pl.ds(pl.multiple_of(pair * PAIR + a * LANES, LANES), 2 * LANES)
        return q_ref[2 * c : 2 * c + 2, :, at]

    def step(i, carry):
        for p in range(per):
            pair = i * per + p
            for copy in large(pair):
                copy.wait()
        for p in range(per):
            pair = i * per + p
            for a in range(2):
                kk = main_keys(kn_ref[:, lanes_at(2 * pair + a, DNOPE)], a, even_ref, odd_ref)
                kk_ref[:, lanes_at(2 * pair + a, 2 * LANES)] = kk
                for c, cols in enumerate(halves):
                    s = scores(kk, query(pair, a, c), c)
                    total = jnp.sum(jnp.exp2(s), axis=0, keepdims=True)
                    fine = (total >= SMALL) & (total <= LARGE)
                    skip = none_ref[:, cols] > 0
                    bad_ref[:, cols] += jnp.where(fine | skip, 0.0, 1.0)
                    lse_ref[pl.ds(2 * pair + a, 1), cols] = jnp.where(skip, NEG, jnp.log2(total))
        return carry

    lax.fori_loop(0, pairs // per, step, 0)
    index_copy.wait()

    @pl.when(jnp.max(bad_ref[...]) > 0)
    def _():
        def again(pair, carry):
            for a in range(2):
                kk = kk_ref[:, lanes_at(2 * pair + a, 2 * LANES)]
                for c, cols in enumerate(halves):
                    s = scores(kk, query(pair, a, c), c)
                    top = jnp.max(s, axis=0, keepdims=True)
                    total = jnp.sum(jnp.exp2(s - top), axis=0, keepdims=True)
                    lse_ref[pl.ds(2 * pair + a, 1), cols] = top + jnp.log2(total)
            return carry

        lax.fori_loop(0, pairs, again, 0)


def main_stats(main_query, key_nope, rope_t, query_pos, key_pos, key_count, index_query):
    groups, rows, width = main_query.shape
    heads = width // DQK
    keys = key_nope.shape[0]
    total = groups * rows
    return pl.pallas_call(
        functools.partial(stats_kernel, 2),
        in_specs=[pl.BlockSpec(memory_space=pltpu.HBM)] * 7,
        out_specs=[IN_VMEM] * 5,
        out_shape=[
            jax.ShapeDtypeStruct((heads, total), f32),
            jax.ShapeDtypeStruct(main_query.shape, bf16),
            jax.ShapeDtypeStruct((keys, heads * 2 * LANES), bf16),
            jax.ShapeDtypeStruct((keys, total), f32),
            jax.ShapeDtypeStruct(index_query.shape, bf16),
        ],
        scratch_shapes=[
            pltpu.VMEM(key_nope.shape, bf16),
            pltpu.VMEM(rope_t.shape, bf16),
            pltpu.VMEM(query_pos.shape, jnp.int32),
            pltpu.VMEM(key_pos.shape, jnp.int32),
            pltpu.VMEM((keys, LANES), bf16),
            pltpu.VMEM((keys, LANES), bf16),
            pltpu.VMEM((1, total), f32),
            pltpu.VMEM((1, total), f32),
            pltpu.SMEM(key_count.shape, jnp.int32),
            pltpu.SemaphoreType.DMA((4,)),
            pltpu.SemaphoreType.DMA((heads // 2,)),
            pltpu.SemaphoreType.DMA((heads // 2,)),
            pltpu.SemaphoreType.DMA,
        ],
        compiler_params=pltpu.CompilerParams(vmem_limit_bytes=16 * 1024 * 1024),
        cost_estimate=cost(
            heads * total * keys * 512, main_query.size * 2 + key_nope.size * 2, heads * total * keys
        ),
        name="main_stats",
    )(key_count, main_query, key_nope, rope_t, query_pos, key_pos, index_query)


def target_kernel(n_lse, masks, per, parts, q_ref, kk_ref, bias_ref, *refs):
    lse_refs = refs[:n_lse]
    out_refs = refs[n_lse:-1]
    glob_ref = refs[-1]
    n_groups = len(masks)
    keys = kk_ref.shape[0]
    rows = q_ref.shape[1]
    pairs = q_ref.shape[2] // PAIR
    size = keys // parts
    me = lax.axis_index("head")
    ids = [lax.bitwise_xor(me, mask) for mask in masks]
    tiles = [
        (g, slice(i * size, (i + 1) * size), out_refs[g * parts + i])
        for g in range(n_groups)
        for i in range(parts)
    ]
    for g in range(n_groups):
        at = lanes_at(ids[g], rows)
        glob_ref[:, g * rows : (g + 1) * rows] = combine_lse([r[:, at] for r in lse_refs])
    for ref in out_refs:
        ref[...] = jnp.zeros_like(ref)

    def step(i, carry):
        for p in range(per):
            pair = i * per + p
            acc = None
            for a in range(2):
                kk = kk_ref[:, lanes_at(2 * pair + a, 2 * LANES)]
                at = pl.ds(pl.multiple_of(pair * PAIR + a * LANES, LANES), 2 * LANES)
                qs = [q_ref[g, :, at] for g in ids]
                q = qs[0] if n_groups == 1 else jnp.concatenate(qs, axis=0)
                lse = glob_ref[pl.ds(2 * pair + a, 1), :]
                e = jnp.exp2(dot_nt(kk, q) * SCALE_MAIN - lse)
                acc = e if acc is None else acc + e
            for g, at, ref in tiles:
                ref[...] += acc[at, g * rows : (g + 1) * rows]
        return carry

    lax.fori_loop(0, pairs // per, step, 0)
    for g, at, ref in tiles:
        ref[...] = jnp.where(bias_ref[at, lanes_at(ids[g], rows)] < 0, 0.0, ref[...])


def head_sums(masks, q, kk, bias, lses, parts=1):
    _, rows, width = q.shape
    heads = width // DQK
    keys = kk.shape[0]
    n = len(masks)
    return pl.pallas_call(
        functools.partial(target_kernel, len(lses), masks, 4 // n, parts),
        in_specs=[IN_VMEM] * (3 + len(lses)),
        out_specs=[IN_VMEM] * (n * parts),
        out_shape=[jax.ShapeDtypeStruct((keys // parts, rows), f32)] * (n * parts),
        scratch_shapes=[pltpu.VMEM((heads, n * rows), f32)],
        compiler_params=pltpu.CompilerParams(vmem_limit_bytes=16 * 1024 * 1024),
        cost_estimate=cost(
            heads * n * rows * keys * 512, heads * n * rows * keys // 16, heads * n * rows * keys
        ),
        name="head_sums",
    )(q, kk, bias, *lses)


def logits_kernel(per, iq_ref, ik_ref, wt_ref, bias_ref, logits_ref, lse_ref, wm_ref, w_ref):
    rows, width = iq_ref.shape
    w_ref[...] = wt_ref[...].astype(f32)
    logits_ref[...] = jnp.zeros_like(logits_ref)

    def step(i, carry):
        for p in range(per):
            first = 2 * (i * per + p)
            q = jnp.concatenate([iq_ref[:, lanes_at(first + a, ID)] for a in range(2)], axis=0)
            z = dot_nt(ik_ref[...], q)
            w = jnp.concatenate([w_ref[pl.ds(first + a, 1), :] for a in range(2)], axis=1)
            masked = jnp.where(z > 0, w, 0.0)
            wm_ref[:, lanes_at(i * per + p, 2 * rows)] = masked.astype(bf16)
            r = z * masked
            logits_ref[...] += r[:, :rows] + r[:, rows:]
        return carry

    lax.fori_loop(0, width // (2 * ID * per), step, 0)
    logits = logits_ref[...] * SCALE_INDEX
    logits_ref[...] = logits
    valid = bias_ref[:, lanes_at(lax.axis_index("head"), rows)] == 0
    s = jnp.where(valid, logits * LOG2E, NEG)
    top = jnp.max(s, axis=0, keepdims=True)
    lse_ref[...] = top + jnp.log2(jnp.sum(jnp.exp2(s - top), axis=0, keepdims=True))


def index_logits(index_query, index_key, weight_t, bias):
    rows, width = index_query.shape
    keys = index_key.shape[0]
    whole = lambda i: (0, 0)
    return pl.pallas_call(
        functools.partial(logits_kernel, 4),
        grid=(1,),
        in_specs=[
            IN_VMEM,
            pl.BlockSpec(index_key.shape, whole),
            pl.BlockSpec(weight_t.shape, whole),
            IN_VMEM,
        ],
        out_specs=[IN_VMEM] * 3,
        out_shape=[
            jax.ShapeDtypeStruct((keys, rows), f32),
            jax.ShapeDtypeStruct((1, rows), f32),
            jax.ShapeDtypeStruct((keys, (width // ID) * rows), bf16),
        ],
        scratch_shapes=[pltpu.VMEM((width // ID, rows), f32)],
        compiler_params=pltpu.CompilerParams(vmem_limit_bytes=16 * 1024 * 1024),
        cost_estimate=cost(2 * keys * rows * width, rows * width * 2 + keys * rows * width // ID * 2),
        name="index_logits",
    )(index_query, index_key, weight_t, bias)


def grad_key_kernel(n_parts, n_lse, per, *refs):
    parts = refs[:n_parts]
    lses = refs[n_parts : n_parts + n_lse]
    logits_ref, wm_ref, iq_ref, bias_ref, cot_ref, sg_ref, lo_ref, hi_ref = refs[n_parts + n_lse :]
    keys, rows = logits_ref.shape
    width = iq_ref.shape[1]

    valid = bias_ref[:, lanes_at(lax.axis_index("head"), rows)] == 0
    target = functools.reduce(jnp.add, [p[...] for p in parts]) * (1.0 / H)
    logits = logits_ref[...]
    lse2 = combine_lse([r[...] for r in lses])
    qprob = jnp.where(valid, jnp.exp2(logits * LOG2E - lse2), 0.0)
    sg_ref[:keys, :] = SCALE_INDEX * (cot_ref[...] * (qprob - target))
    live = target > 0
    terms = jnp.where(live, target * (jnp.log(jnp.where(live, target, 1.0)) - logits), 0.0)
    kl = jnp.sum(terms, axis=0, keepdims=True)
    sg_ref[keys:, :] = jnp.broadcast_to(kl, (8, rows))
    lo_ref[...] = jnp.zeros_like(lo_ref)
    hi_ref[...] = jnp.zeros_like(hi_ref)

    def step(i, carry):
        for p in range(per):
            dz = []
            qs = []
            for a in range(2):
                j = 2 * (i * per + p) + a
                wm = wm_ref[:, lanes_at(j, rows)].astype(f32)
                dz.append((sg_ref[:keys, :] * wm).astype(bf16))
                qs.append(iq_ref[:, lanes_at(j, ID)])
            g = dot_nn(jnp.concatenate(dz, axis=1), jnp.concatenate(qs, axis=0))
            lo_ref[...] += g[: keys // 2]
            hi_ref[...] += g[keys // 2 :]
        return carry

    lax.fori_loop(0, width // (2 * ID * per), step, 0)


def index_grad_key(parts, lses, logits, wm, index_query, bias, cotangent):
    rows, width = index_query.shape
    keys = logits.shape[0]
    return pl.pallas_call(
        functools.partial(grad_key_kernel, len(parts), len(lses), 8),
        grid=(1,),
        in_specs=[IN_VMEM] * (len(parts) + len(lses) + 4)
        + [pl.BlockSpec((1, rows), lambda i: (0, 0))],
        out_specs=[IN_VMEM] * 3,
        out_shape=[
            jax.ShapeDtypeStruct((keys + 8, rows), f32),
            jax.ShapeDtypeStruct((keys // 2, ID), f32),
            jax.ShapeDtypeStruct((keys // 2, ID), f32),
        ],
        compiler_params=pltpu.CompilerParams(vmem_limit_bytes=16 * 1024 * 1024),
        cost_estimate=cost(2 * keys * rows * width, rows * width * 2 + keys * rows * width // ID * 2),
        name="index_grad_key",
    )(*parts, *lses, logits, wm, index_query, bias, cotangent)


def grad_query_kernel(n_shards, first, n_lse, *refs):
    sgs = refs[:n_shards]
    iks = refs[n_shards : 2 * n_shards]
    iq_ref, w_ref = refs[2 * n_shards : 2 * n_shards + 2]
    rest = refs[2 * n_shards + 2 :]
    lses = rest[:n_lse]
    rest = rest[n_lse:]
    if first:
        gq_ref, kl_ref, ws_ref = rest
    else:
        gq_in_ref, kl_in_ref, gq_ref, kl_ref, ws_ref = rest
    rows = iq_ref.shape[0]
    heads = gq_ref.shape[1] // ID
    keys = iks[0].shape[0]
    base = lax.axis_index("key") * heads
    ws_ref[...] = w_ref[...].astype(f32)
    mine = ws_ref[pl.ds(base, heads), :]
    ws = jnp.transpose(jnp.concatenate([mine, jnp.zeros((LANES - heads, rows), f32)], axis=0))
    kl = functools.reduce(jnp.add, [s[keys : keys + 1, :] for s in sgs])
    kl = kl if first else kl_in_ref[...] + kl
    if n_lse:
        kl = kl + combine_lse([r[...] for r in lses]) * (1.0 / LOG2E)
    kl_ref[...] = kl
    unit = min(heads, 4)
    iks = [ref[...].astype(bf16) for ref in iks]
    sgts = [jnp.transpose(ref[:keys, :]) for ref in sgs]
    for start in range(0, heads, unit):
        js = range(start, start + unit)
        iq = jnp.concatenate([iq_ref[:, lanes_at(base + j, ID)] for j in js], axis=0)
        out = None
        for ik, sgt in zip(iks, sgts):
            z = dot_nt(iq, ik)
            dz = jnp.concatenate(
                [
                    jnp.where(z[i * rows : (i + 1) * rows] > 0, sgt * ws[:, j : j + 1], 0.0).astype(bf16)
                    for i, j in enumerate(js)
                ],
                axis=0,
            )
            g = dot_nn(dz, ik)
            out = g if out is None else out + g
        for i, j in enumerate(js):
            cols = slice(j * ID, (j + 1) * ID)
            g = out[i * rows : (i + 1) * rows]
            gq_ref[:, cols] = g if first else gq_in_ref[:, cols] + g


def index_grad_query(n_slots, sgs, iks, index_query, weight_t, lses, carry):
    rows, width = index_query.shape
    heads = width // ID
    mine = width // n_slots
    keys = iks[0].shape[0]
    first = carry is None
    carried = [] if first else list(carry)
    n = len(sgs)
    return pl.pallas_call(
        functools.partial(grad_query_kernel, n, first, len(lses)),
        grid=(1,),
        in_specs=[IN_VMEM] * (2 * n + 1)
        + [pl.BlockSpec(weight_t.shape, lambda i: (0, 0))]
        + [IN_VMEM] * (len(lses) + len(carried)),
        out_specs=[IN_VMEM, IN_VMEM],
        out_shape=[
            jax.ShapeDtypeStruct((rows, mine), f32),
            jax.ShapeDtypeStruct((1, rows), f32),
        ],
        scratch_shapes=[pltpu.VMEM((heads, rows), f32)],
        compiler_params=pltpu.CompilerParams(vmem_limit_bytes=20 * 1024 * 1024),
        cost_estimate=cost(4 * n * keys * rows * mine, n * (keys * ID * 8) + rows * mine * 8),
        name="index_grad_query",
    )(*sgs, *iks, index_query, weight_t, *lses, *carried)


def swap(value, axis, mask, size):
    return lax.ppermute(value, axis, [(i, i ^ mask) for i in range(size)])


def butterfly_lse(value, size):
    pair = [value]
    for bit in reversed(range(size.bit_length() - 1)):
        here = combine_lse(pair)
        pair = [here, swap(here, "key", 1 << bit, size)]
    return pair


def summed_copies(pieces, n_head, n_query):
    steps = [("head", (2 << b) - 1, n_head) for b in reversed(range(n_head.bit_length() - 1))]
    steps += [("query", 1 << b, n_query) for b in range(n_query.bit_length() - 1)]
    steps = steps[:1] + steps[2:] + steps[1:2]
    for number in range(len(steps)):
        moved = []
        for i, piece in enumerate(pieces):
            moved.append(swap(piece, *steps[(number - i) % len(steps)]))
        pieces = [piece + other for piece, other in zip(pieces, moved)]
    return jnp.concatenate(pieces, axis=0)


def in_hbm(*values):
    return tuple(pltpu.with_memory_space_constraint(v, pltpu.HBM) for v in values)


def body(n_key, n_head, n_query, main_query, key_nope, key_rope, query_pos, key_pos, key_count,
         index_query, index_key, index_weight, row_cotangent):
    groups, rows, _ = main_query.shape
    keys = key_nope.shape[0]
    (main_query, key_nope, rope_t, query_pos, key_row, key_count, weight_t, cotangent, narrow,
     index_query) = in_hbm(
        main_query, key_nope, key_rope.T, query_pos, key_pos.reshape(1, keys), key_count,
        index_weight.T, row_cotangent.reshape(1, rows), index_key, index_query,
    )

    def gathered(value):
        if n_key == 4:
            near = swap(value, "key", 1, n_key)
            far = swap(value, "key", 2, n_key)
            across = swap(far, "key", 1, n_key)
            return [value, near, far, across]
        return list(lax.all_gather(value, "key"))

    lse, q, kk, bias, iq = main_stats(
        main_query, key_nope, rope_t, query_pos, key_row, key_count, index_query
    )
    lses = butterfly_lse(lse, n_key)
    logits, index_lse, wm = index_logits(iq, narrow, weight_t, bias)
    index_lses = butterfly_lse(index_lse, n_key)
    iks = gathered(index_key.astype(f32))

    half = keys // 2
    if n_head == 4 and groups == 4:
        low, high = head_sums([2], q, kk, bias, lses, parts=2)
        low = swap(low, "head", 1, 4)
        high = swap(high, "head", 3, 4)
        up, down = head_sums([1, 3], q, kk, bias, lses)
        up = up + jnp.pad(high, ((half, 0), (0, 0)))
        down = down + jnp.pad(low, ((0, half), (0, 0)))
        from_up = swap(up, "head", 1, 4)
        from_down = swap(down, "head", 3, 4)
        own = head_sums([0], q, kk, bias, lses)[0]
        parts = [own, from_up, from_down]
    else:
        z = lax.axis_index("head")
        tiles = jnp.stack([head_sums([g], q, kk, bias, lses)[0] for g in range(groups)])
        tiles = tiles[jnp.bitwise_xor(jnp.arange(groups), z)]
        parts = [lax.psum_scatter(tiles, "head", scatter_dimension=0, tiled=True)[0]]

    sg, *grad_key = index_grad_key(parts, index_lses, logits, wm, iq, bias, cotangent)
    grad_key = summed_copies(grad_key, n_head, n_query)
    sgs = gathered(sg)
    carry = None
    for lo in range(0, n_key, 2):
        last = lo + 2 >= n_key
        carry = index_grad_query(
            n_key, sgs[lo : lo + 2], iks[lo : lo + 2], iq, weight_t,
            index_lses if last else [], carry,
        )
    grad_query, kl = carry
    return kl.reshape(rows), grad_query, grad_key


def solution(mesh):
    sizes = (mesh.shape["key"], mesh.shape["head"], mesh.shape["query"])

    def step(*args):
        return body(*sizes, *args)

    return jax.shard_map(
        step,
        mesh=mesh,
        in_specs=(
            P(None, "query", "head"),
            P("key", "head"),
            P("key", None),
            P(None, "query"),
            P("key"),
            P("key"),
            P(("head", "query"), None),
            P("key", None),
            P(("head", "query"), None),
            P(("head", "query")),
        ),
        out_specs=(P(("head", "query")), P(("head", "query"), "key"), P("key", None)),
        check_vma=False,
    )
```

```python
import functools
import math
import jax
import jax.numpy as jnp
from jax import lax
from jax.experimental import pallas as pl
from jax.experimental.pallas import tpu as pltpu
from jax.sharding import PartitionSpec as P


H = 128
DNOPE = 128
DROPE = 64
ID = 128
KBLOCK = 32
DQK = 192
LANES = 128
PAIR = 2 * DQK
NEG = -1e30
SMALL = 2.0**-90
LARGE = 2.0**100
BIG = 2**30
LOG2E = math.log2(math.e)
SCALE_MAIN = DQK ** (-0.5) * LOG2E
SCALE_INDEX = ID ** (-0.5)

f32 = jnp.float32
bf16 = jnp.bfloat16
IN_VMEM = pl.BlockSpec(memory_space=pltpu.VMEM)


def dot_nt(a, b):
    return lax.dot_general(a, b, (((1,), (1,)), ((), ())), preferred_element_type=f32)


def dot_nn(a, b):
    return lax.dot_general(a, b, (((1,), (0,)), ((), ())), preferred_element_type=f32)


def cost(flops, bytes_accessed, transcendentals=0):
    return pl.CostEstimate(
        flops=int(flops), bytes_accessed=int(bytes_accessed), transcendentals=int(transcendentals)
    )


def combine_lse(parts):
    if len(parts) == 1:
        return parts[0]
    top = functools.reduce(jnp.maximum, parts)
    return top + jnp.log2(functools.reduce(jnp.add, [jnp.exp2(p - top) for p in parts]))


def packed_sizes(keys):
    return [keys * part // 32 for part in (18, 20, 22, 32)]


def for_packed(live, keys, run):
    below = 0
    for size in packed_sizes(keys):
        pl.when((live > below) & (live <= size))(functools.partial(run, size))
        below = size


def packing(count_ref, keys):
    lane = lax.broadcasted_iota(jnp.int32, (1, keys), 1)
    block, place = lane // KBLOCK, lane % KBLOCK
    rank = jnp.full((1, keys), -1, jnp.int32)
    base = jnp.int32(0)
    for b in range(keys // KBLOCK):
        here = count_ref[b]
        rank = jnp.where((block == b) & (place < here), base + place, rank)
        base = base + here
    return rank, base


def main_keys(nope, parity, even_ref, odd_ref):
    count = nope.shape[0]
    if parity == 0:
        return jnp.concatenate([nope, even_ref[:count, :]], axis=1)
    turned = jnp.concatenate([nope[:, DROPE:], nope[:, :DROPE]], axis=1)
    low = lax.broadcasted_iota(jnp.int32, turned.shape, 1) < DROPE
    first = jnp.where(low, jnp.zeros_like(turned), turned)
    second = jnp.where(low, turned, odd_ref[:count, :])
    return jnp.concatenate([first, second], axis=1)


def lanes_at(index, width):
    return pl.ds(pl.multiple_of(index * width, LANES), width)


def stats_kernel(per, count_hbm, q_hbm, kn_hbm, rope_hbm, qpos_hbm, kpos_hbm, iq_hbm, ik_hbm,
                 lse_ref, q_ref, kk_ref, bias_ref, iq_ref, ik_ref, spread_ref, live_ref,
                 kn_ref, rope_ref, qpos_ref, kpos_ref, even_ref, odd_ref, none_ref, bad_ref,
                 pack_ref, raw_ref, count_ref, small_sem, q_sem, kn_sem, iq_sem):
    keys = kn_ref.shape[0]
    groups, rows = q_ref.shape[0], q_ref.shape[1]
    pairs = q_ref.shape[2] // PAIR
    halves = [slice(2 * c * rows, (2 * c + 2) * rows) for c in range(groups // 2)]

    small = [
        pltpu.make_async_copy(src, dst, small_sem.at[i])
        for i, (src, dst) in enumerate(
            ((count_hbm, count_ref), (kpos_hbm, kpos_ref), (qpos_hbm, qpos_ref), (rope_hbm, rope_ref),
             (ik_hbm, raw_ref))
        )
    ]

    def large(i):
        q_at, k_at = lanes_at(i, PAIR), lanes_at(i, 2 * DNOPE)
        return (
            pltpu.make_async_copy(kn_hbm.at[:, k_at], kn_ref.at[:, k_at], kn_sem.at[i]),
            pltpu.make_async_copy(q_hbm.at[:, :, q_at], q_ref.at[:, :, q_at], q_sem.at[i]),
        )

    for copy in small:
        copy.start()
    for i in range(pairs):
        for copy in large(i):
            copy.start()
    index_copy = pltpu.make_async_copy(iq_hbm, iq_ref, iq_sem)
    index_copy.start()
    for copy in small:
        copy.wait()

    rank, live = packing(count_ref, keys)
    row = lax.broadcasted_iota(jnp.int32, (keys, keys), 0)
    chosen = row == rank
    pack_ref[...] = jnp.where(chosen, 1.0, 0.0).astype(bf16)
    position = jnp.sum(jnp.where(chosen, kpos_ref[...].astype(f32), 0.0), axis=1, keepdims=True)
    column = jnp.where(row[:, :1] < live, position.astype(jnp.int32), BIG)
    rank_column = jnp.transpose(jnp.broadcast_to(rank, (8, keys)))[:, :1]
    lane = lax.broadcasted_iota(jnp.int32, (keys, keys), 1)
    spread_ref[...] = jnp.where(lane == rank_column, 1.0, 0.0).astype(bf16)
    live_ref[...] = jnp.broadcast_to(live, live_ref.shape)
    ik_ref[...] = dot_nn(pack_ref[...], raw_ref[...])
    rope = dot_nt(pack_ref[...], rope_ref[...]).astype(bf16)
    zero = jnp.zeros_like(rope)
    even_ref[...] = jnp.concatenate([rope, zero], axis=1)
    odd_ref[...] = jnp.concatenate([zero, rope], axis=1)
    for g in range(groups):
        valid = column <= qpos_ref[g : g + 1, :]
        bias = jnp.where(valid, 0.0, NEG)
        bias_ref[:, g * rows : (g + 1) * rows] = bias
        none_ref[:, g * rows : (g + 1) * rows] = jnp.where(
            jnp.max(bias, axis=0, keepdims=True) < 0, 1.0, 0.0
        )
    bad_ref[...] = jnp.zeros_like(bad_ref)

    def scores(kk, q3, c):
        q = q3.reshape(2 * rows, 2 * LANES)
        return dot_nt(kk, q) * SCALE_MAIN + bias_ref[: kk.shape[0], halves[c]]

    def query(pair, a, c):
        at = pl.ds(pl.multiple_of(pair * PAIR + a * LANES, LANES), 2 * LANES)
        return q_ref[2 * c : 2 * c + 2, :, at]

    def step(size, i, carry):
        for p in range(per):
            pair = i * per + p
            for copy in large(pair):
                copy.wait()
        for p in range(per):
            pair = i * per + p
            both = dot_nn(pack_ref[:size, :], kn_ref[:, lanes_at(pair, 2 * DNOPE)]).astype(bf16)
            for a in range(2):
                kk = main_keys(both[:, a * DNOPE : (a + 1) * DNOPE], a, even_ref, odd_ref)
                kk_ref[:size, lanes_at(2 * pair + a, 2 * LANES)] = kk
                for c, cols in enumerate(halves):
                    s = scores(kk, query(pair, a, c), c)
                    total = jnp.sum(jnp.exp2(s), axis=0, keepdims=True)
                    fine = (total >= SMALL) & (total <= LARGE)
                    skip = none_ref[:, cols] > 0
                    bad_ref[:, cols] += jnp.where(fine | skip, 0.0, 1.0)
                    lse_ref[pl.ds(2 * pair + a, 1), cols] = jnp.where(skip, NEG, jnp.log2(total))
        return carry

    def run(size):
        lax.fori_loop(0, pairs // per, functools.partial(step, size), 0)

    for_packed(live, keys, run)
    index_copy.wait()

    @pl.when(jnp.max(bad_ref[...]) > 0)
    def _():
        def again(pair, carry):
            for a in range(2):
                kk = kk_ref[:, lanes_at(2 * pair + a, 2 * LANES)]
                for c, cols in enumerate(halves):
                    s = jnp.where(bias_ref[:, cols] < 0, NEG, scores(kk, query(pair, a, c), c))
                    top = jnp.max(s, axis=0, keepdims=True)
                    total = jnp.sum(jnp.exp2(s - top), axis=0, keepdims=True)
                    lse_ref[pl.ds(2 * pair + a, 1), cols] = top + jnp.log2(total)
            return carry

        lax.fori_loop(0, pairs, again, 0)


def main_stats(main_query, key_nope, rope_t, query_pos, key_pos, key_count, index_query, index_key):
    groups, rows, width = main_query.shape
    heads = width // DQK
    keys = key_nope.shape[0]
    total = groups * rows
    return pl.pallas_call(
        functools.partial(stats_kernel, 2),
        in_specs=[pl.BlockSpec(memory_space=pltpu.HBM)] * 8,
        out_specs=[IN_VMEM] * 8,
        out_shape=[
            jax.ShapeDtypeStruct((heads, total), f32),
            jax.ShapeDtypeStruct(main_query.shape, bf16),
            jax.ShapeDtypeStruct((keys, heads * 2 * LANES), bf16),
            jax.ShapeDtypeStruct((keys, total), f32),
            jax.ShapeDtypeStruct(index_query.shape, bf16),
            jax.ShapeDtypeStruct(index_key.shape, f32),
            jax.ShapeDtypeStruct((keys, keys), bf16),
            jax.ShapeDtypeStruct((8, LANES), jnp.int32),
        ],
        scratch_shapes=[
            pltpu.VMEM(key_nope.shape, bf16),
            pltpu.VMEM(rope_t.shape, bf16),
            pltpu.VMEM(query_pos.shape, jnp.int32),
            pltpu.VMEM(key_pos.shape, jnp.int32),
            pltpu.VMEM((keys, LANES), bf16),
            pltpu.VMEM((keys, LANES), bf16),
            pltpu.VMEM((1, total), f32),
            pltpu.VMEM((1, total), f32),
            pltpu.VMEM((keys, keys), bf16),
            pltpu.VMEM(index_key.shape, bf16),
            pltpu.SMEM(key_count.shape, jnp.int32),
            pltpu.SemaphoreType.DMA((5,)),
            pltpu.SemaphoreType.DMA((heads // 2,)),
            pltpu.SemaphoreType.DMA((heads // 2,)),
            pltpu.SemaphoreType.DMA,
        ],
        compiler_params=pltpu.CompilerParams(vmem_limit_bytes=16 * 1024 * 1024),
        cost_estimate=cost(
            heads * total * keys * 512, main_query.size * 2 + key_nope.size * 2, heads * total * keys
        ),
        name="main_stats",
    )(key_count, main_query, key_nope, rope_t, query_pos, key_pos, index_query, index_key)


def target_kernel(n_lse, masks, per, parts, q_ref, kk_ref, bias_ref, live_ref, *refs):
    lse_refs = refs[:n_lse]
    out_refs = refs[n_lse:-1]
    glob_ref = refs[-1]
    n_groups = len(masks)
    keys = kk_ref.shape[0]
    rows = q_ref.shape[1]
    pairs = q_ref.shape[2] // PAIR
    size = keys // parts
    me = lax.axis_index("head")
    ids = [lax.bitwise_xor(me, mask) for mask in masks]
    tiles = [
        (g, slice(i * size, (i + 1) * size), out_refs[g * parts + i])
        for g in range(n_groups)
        for i in range(parts)
    ]
    for g in range(n_groups):
        at = lanes_at(ids[g], rows)
        glob_ref[:, g * rows : (g + 1) * rows] = combine_lse([r[:, at] for r in lse_refs])
    for ref in out_refs:
        ref[...] = jnp.zeros_like(ref)

    def step(rows_kept, i, carry):
        for p in range(per):
            pair = i * per + p
            acc = None
            for a in range(2):
                kk = kk_ref[:rows_kept, lanes_at(2 * pair + a, 2 * LANES)]
                at = pl.ds(pl.multiple_of(pair * PAIR + a * LANES, LANES), 2 * LANES)
                qs = [q_ref[g, :, at] for g in ids]
                q = qs[0] if n_groups == 1 else jnp.concatenate(qs, axis=0)
                lse = glob_ref[pl.ds(2 * pair + a, 1), :]
                e = jnp.exp2(dot_nt(kk, q) * SCALE_MAIN - lse)
                acc = e if acc is None else acc + e
            for g, at, ref in tiles:
                some = acc[at, g * rows : (g + 1) * rows]
                if some.shape[0]:
                    ref[: some.shape[0], :] += some
        return carry

    def run(rows_kept):
        lax.fori_loop(0, pairs // per, functools.partial(step, rows_kept), 0)

    for_packed(jnp.max(live_ref[...]), keys, run)
    for g, at, ref in tiles:
        ref[...] = jnp.where(bias_ref[at, lanes_at(ids[g], rows)] < 0, 0.0, ref[...])


def head_sums(masks, q, kk, bias, live, lses, parts=1):
    _, rows, width = q.shape
    heads = width // DQK
    keys = kk.shape[0]
    n = len(masks)
    return pl.pallas_call(
        functools.partial(target_kernel, len(lses), masks, 4 // n, parts),
        in_specs=[IN_VMEM] * (4 + len(lses)),
        out_specs=[IN_VMEM] * (n * parts),
        out_shape=[jax.ShapeDtypeStruct((keys // parts, rows), f32)] * (n * parts),
        scratch_shapes=[pltpu.VMEM((heads, n * rows), f32)],
        compiler_params=pltpu.CompilerParams(vmem_limit_bytes=16 * 1024 * 1024),
        cost_estimate=cost(
            heads * n * rows * keys * 512, heads * n * rows * keys // 16, heads * n * rows * keys
        ),
        name="head_sums",
    )(q, kk, bias, live, *lses)


def logits_kernel(per, iq_ref, wide_ref, wt_ref, bias_ref, live_ref,
                  logits_ref, lse_ref, wm_ref, w_ref, ik_ref):
    keys = wide_ref.shape[0]
    rows, width = iq_ref.shape
    w_ref[...] = wt_ref[...].astype(f32)
    ik_ref[...] = wide_ref[...].astype(bf16)
    logits_ref[...] = jnp.zeros_like(logits_ref)

    def step(size, i, carry):
        for p in range(per):
            first = 2 * (i * per + p)
            q = jnp.concatenate([iq_ref[:, lanes_at(first + a, ID)] for a in range(2)], axis=0)
            z = dot_nt(ik_ref[:size, :], q)
            w = jnp.concatenate([w_ref[pl.ds(first + a, 1), :] for a in range(2)], axis=1)
            masked = jnp.where(z > 0, w, 0.0)
            wm_ref[:size, lanes_at(i * per + p, 2 * rows)] = masked.astype(bf16)
            r = z * masked
            logits_ref[:size, :] += r[:, :rows] + r[:, rows:]
        return carry

    def run(size):
        lax.fori_loop(0, width // (2 * ID * per), functools.partial(step, size), 0)

    for_packed(jnp.max(live_ref[...]), keys, run)
    logits = logits_ref[...] * SCALE_INDEX
    logits_ref[...] = logits
    valid = bias_ref[:, lanes_at(lax.axis_index("head"), rows)] == 0
    s = jnp.where(valid, logits * LOG2E, NEG)
    top = jnp.max(s, axis=0, keepdims=True)
    lse_ref[...] = top + jnp.log2(jnp.sum(jnp.exp2(s - top), axis=0, keepdims=True))


def index_logits(index_query, index_key, weight_t, bias, live):
    rows, width = index_query.shape
    keys = index_key.shape[0]
    whole = lambda i: (0, 0)
    return pl.pallas_call(
        functools.partial(logits_kernel, 4),
        grid=(1,),
        in_specs=[
            IN_VMEM,
            IN_VMEM,
            pl.BlockSpec(weight_t.shape, whole),
            IN_VMEM,
            IN_VMEM,
        ],
        out_specs=[IN_VMEM] * 3,
        out_shape=[
            jax.ShapeDtypeStruct((keys, rows), f32),
            jax.ShapeDtypeStruct((1, rows), f32),
            jax.ShapeDtypeStruct((keys, (width // ID) * rows), bf16),
        ],
        scratch_shapes=[
            pltpu.VMEM((width // ID, rows), f32),
            pltpu.VMEM(index_key.shape, bf16),
        ],
        compiler_params=pltpu.CompilerParams(vmem_limit_bytes=16 * 1024 * 1024),
        cost_estimate=cost(2 * keys * rows * width, rows * width * 2 + keys * rows * width // ID * 2),
        name="index_logits",
    )(index_query, index_key, weight_t, bias, live)


def grad_key_kernel(n_parts, n_lse, per, *refs):
    parts = refs[:n_parts]
    lses = refs[n_parts : n_parts + n_lse]
    (logits_ref, wm_ref, iq_ref, bias_ref, live_ref, spread_ref, cot_ref,
     sg_ref, lo_ref, hi_ref, sum_ref) = refs[n_parts + n_lse :]
    keys, rows = logits_ref.shape
    width = iq_ref.shape[1]

    valid = bias_ref[:, lanes_at(lax.axis_index("head"), rows)] == 0
    target = functools.reduce(jnp.add, [p[...] for p in parts]) * (1.0 / H)
    logits = logits_ref[...]
    lse2 = combine_lse([r[...] for r in lses])
    qprob = jnp.where(valid, jnp.exp2(logits * LOG2E - lse2), 0.0)
    sg_ref[:keys, :] = SCALE_INDEX * (cot_ref[...] * (qprob - target))
    live = target > 0
    terms = jnp.where(live, target * (jnp.log(jnp.where(live, target, 1.0)) - logits), 0.0)
    kl = jnp.sum(terms, axis=0, keepdims=True)
    sg_ref[keys:, :] = jnp.broadcast_to(kl, (8, rows))
    sum_ref[...] = jnp.zeros_like(sum_ref)

    def step(size, i, carry):
        for p in range(per):
            dz = []
            qs = []
            for a in range(2):
                j = 2 * (i * per + p) + a
                wm = wm_ref[:size, lanes_at(j, rows)].astype(f32)
                dz.append((sg_ref[:size, :] * wm).astype(bf16))
                qs.append(iq_ref[:, lanes_at(j, ID)])
            sum_ref[:size, :] += dot_nn(jnp.concatenate(dz, axis=1), jnp.concatenate(qs, axis=0))
        return carry

    def run(size):
        lax.fori_loop(0, width // (2 * ID * per), functools.partial(step, size), 0)

    for_packed(jnp.max(live_ref[...]), keys, run)
    rest = sum_ref[...]
    pieces = []
    for _ in range(3):
        piece = rest.astype(bf16)
        pieces.append(piece)
        rest = rest - piece.astype(f32)
    placed = dot_nn(spread_ref[...], jnp.concatenate(pieces, axis=1))
    placed = placed[:, :ID] + placed[:, ID : 2 * ID] + placed[:, 2 * ID :]
    lo_ref[...] = placed[: keys // 2]
    hi_ref[...] = placed[keys // 2 :]


def index_grad_key(parts, lses, logits, wm, index_query, bias, live, spread, cotangent):
    rows, width = index_query.shape
    keys = logits.shape[0]
    return pl.pallas_call(
        functools.partial(grad_key_kernel, len(parts), len(lses), 4),
        grid=(1,),
        in_specs=[IN_VMEM] * (len(parts) + len(lses) + 6)
        + [pl.BlockSpec((1, rows), lambda i: (0, 0))],
        out_specs=[IN_VMEM] * 3,
        out_shape=[
            jax.ShapeDtypeStruct((keys + 8, rows), f32),
            jax.ShapeDtypeStruct((keys // 2, ID), f32),
            jax.ShapeDtypeStruct((keys // 2, ID), f32),
        ],
        scratch_shapes=[pltpu.VMEM((keys, ID), f32)],
        compiler_params=pltpu.CompilerParams(vmem_limit_bytes=16 * 1024 * 1024),
        cost_estimate=cost(2 * keys * rows * width, rows * width * 2 + keys * rows * width // ID * 2),
        name="index_grad_key",
    )(*parts, *lses, logits, wm, index_query, bias, live, spread, cotangent)


def grad_query_kernel(n_shards, first, n_lse, *refs):
    sgs = refs[:n_shards]
    iks = refs[n_shards : 2 * n_shards]
    iq_ref, w_ref = refs[2 * n_shards : 2 * n_shards + 2]
    rest = refs[2 * n_shards + 2 :]
    lses = rest[:n_lse]
    rest = rest[n_lse:]
    if first:
        gq_ref, kl_ref, ws_ref = rest
    else:
        gq_in_ref, kl_in_ref, gq_ref, kl_ref, ws_ref = rest
    rows = iq_ref.shape[0]
    heads = gq_ref.shape[1] // ID
    keys = iks[0].shape[0]
    base = lax.axis_index("key") * heads
    ws_ref[...] = w_ref[...].astype(f32)
    mine = ws_ref[pl.ds(base, heads), :]
    ws = jnp.transpose(jnp.concatenate([mine, jnp.zeros((LANES - heads, rows), f32)], axis=0))
    kl = functools.reduce(jnp.add, [s[keys : keys + 1, :] for s in sgs])
    kl = kl if first else kl_in_ref[...] + kl
    if n_lse:
        kl = kl + combine_lse([r[...] for r in lses]) * (1.0 / LOG2E)
    kl_ref[...] = kl
    unit = min(heads, 4)
    iks = [ref[...].astype(bf16) for ref in iks]
    sgts = [jnp.transpose(ref[:keys, :]) for ref in sgs]
    for start in range(0, heads, unit):
        js = range(start, start + unit)
        iq = jnp.concatenate([iq_ref[:, lanes_at(base + j, ID)] for j in js], axis=0)
        out = None
        for ik, sgt in zip(iks, sgts):
            z = dot_nt(iq, ik)
            dz = jnp.concatenate(
                [
                    jnp.where(z[i * rows : (i + 1) * rows] > 0, sgt * ws[:, j : j + 1], 0.0).astype(bf16)
                    for i, j in enumerate(js)
                ],
                axis=0,
            )
            g = dot_nn(dz, ik)
            out = g if out is None else out + g
        for i, j in enumerate(js):
            cols = slice(j * ID, (j + 1) * ID)
            g = out[i * rows : (i + 1) * rows]
            gq_ref[:, cols] = g if first else gq_in_ref[:, cols] + g


def index_grad_query(n_slots, sgs, iks, index_query, weight_t, lses, carry):
    rows, width = index_query.shape
    heads = width // ID
    mine = width // n_slots
    keys = iks[0].shape[0]
    first = carry is None
    carried = [] if first else list(carry)
    n = len(sgs)
    return pl.pallas_call(
        functools.partial(grad_query_kernel, n, first, len(lses)),
        grid=(1,),
        in_specs=[IN_VMEM] * (2 * n + 1)
        + [pl.BlockSpec(weight_t.shape, lambda i: (0, 0))]
        + [IN_VMEM] * (len(lses) + len(carried)),
        out_specs=[IN_VMEM, IN_VMEM],
        out_shape=[
            jax.ShapeDtypeStruct((rows, mine), f32),
            jax.ShapeDtypeStruct((1, rows), f32),
        ],
        scratch_shapes=[pltpu.VMEM((heads, rows), f32)],
        compiler_params=pltpu.CompilerParams(vmem_limit_bytes=20 * 1024 * 1024),
        cost_estimate=cost(4 * n * keys * rows * mine, n * (keys * ID * 8) + rows * mine * 8),
        name="index_grad_query",
    )(*sgs, *iks, index_query, weight_t, *lses, *carried)


def swap(value, axis, mask, size):
    return lax.ppermute(value, axis, [(i, i ^ mask) for i in range(size)])


def butterfly_lse(value, size):
    pair = [value]
    for bit in reversed(range(size.bit_length() - 1)):
        here = combine_lse(pair)
        pair = [here, swap(here, "key", 1 << bit, size)]
    return pair


def summed_copies(pieces, n_head, n_query):
    steps = [("head", (2 << b) - 1, n_head) for b in reversed(range(n_head.bit_length() - 1))]
    steps += [("query", 1 << b, n_query) for b in range(n_query.bit_length() - 1)]
    steps = steps[:1] + steps[2:] + steps[1:2]
    for number in range(len(steps)):
        moved = []
        for i, piece in enumerate(pieces):
            moved.append(swap(piece, *steps[(number - i) % len(steps)]))
        pieces = [piece + other for piece, other in zip(pieces, moved)]
    return jnp.concatenate(pieces, axis=0)


def in_hbm(*values):
    return tuple(pltpu.with_memory_space_constraint(v, pltpu.HBM) for v in values)


def body(n_key, n_head, n_query, main_query, key_nope, key_rope, query_pos, key_pos, key_count,
         index_query, index_key, index_weight, row_cotangent):
    groups, rows, _ = main_query.shape
    keys = key_nope.shape[0]
    (main_query, key_nope, rope_t, query_pos, key_row, key_count, weight_t, cotangent, narrow,
     index_query) = in_hbm(
        main_query, key_nope, key_rope.T, query_pos, key_pos.reshape(1, keys), key_count,
        index_weight.T, row_cotangent.reshape(1, rows), index_key, index_query,
    )

    def gathered(value):
        if n_key == 4:
            near = swap(value, "key", 1, n_key)
            far = swap(value, "key", 2, n_key)
            across = swap(far, "key", 1, n_key)
            return [value, near, far, across]
        return list(lax.all_gather(value, "key"))

    lse, q, kk, bias, iq, wide, spread, live = main_stats(
        main_query, key_nope, rope_t, query_pos, key_row, key_count, index_query, narrow
    )
    lses = butterfly_lse(lse, n_key)
    logits, index_lse, wm = index_logits(iq, wide, weight_t, bias, live)
    index_lses = butterfly_lse(index_lse, n_key)
    iks = gathered(wide)

    half = keys // 2
    if n_head == 4 and groups == 4:
        low, high = head_sums([2], q, kk, bias, live, lses, parts=2)
        low = swap(low, "head", 1, 4)
        high = swap(high, "head", 3, 4)
        up, down = head_sums([1, 3], q, kk, bias, live, lses)
        up = up + jnp.pad(high, ((half, 0), (0, 0)))
        down = down + jnp.pad(low, ((0, half), (0, 0)))
        from_up = swap(up, "head", 1, 4)
        from_down = swap(down, "head", 3, 4)
        own = head_sums([0], q, kk, bias, live, lses)[0]
        parts = [own, from_up, from_down]
    else:
        z = lax.axis_index("head")
        tiles = jnp.stack([head_sums([g], q, kk, bias, live, lses)[0] for g in range(groups)])
        tiles = tiles[jnp.bitwise_xor(jnp.arange(groups), z)]
        parts = [lax.psum_scatter(tiles, "head", scatter_dimension=0, tiled=True)[0]]

    sg, *grad_key = index_grad_key(
        parts, index_lses, logits, wm, iq, bias, live, spread, cotangent
    )
    grad_key = summed_copies(grad_key, n_head, n_query)
    sgs = gathered(sg)
    carry = None
    for lo in range(0, n_key, 2):
        last = lo + 2 >= n_key
        carry = index_grad_query(
            n_key, sgs[lo : lo + 2], iks[lo : lo + 2], iq, weight_t,
            index_lses if last else [], carry,
        )
    grad_query, kl = carry
    return kl.reshape(rows), grad_query, grad_key


def solution(mesh):
    sizes = (mesh.shape["key"], mesh.shape["head"], mesh.shape["query"])

    def step(*args):
        return body(*sizes, *args)

    return jax.shard_map(
        step,
        mesh=mesh,
        in_specs=(
            P(None, "query", "head"),
            P("key", "head"),
            P("key", None),
            P(None, "query"),
            P("key"),
            P("key"),
            P(("head", "query"), None),
            P("key", None),
            P(("head", "query"), None),
            P(("head", "query")),
        ),
        out_specs=(P(("head", "query")), P(("head", "query"), "key"), P("key", None)),
        check_vma=False,
    )
```

```python
import functools
import math
import jax
import jax.numpy as jnp
from jax import lax
from jax.experimental import pallas as pl
from jax.experimental.pallas import tpu as pltpu
from jax.sharding import PartitionSpec as P


H = 128
DNOPE = 128
DROPE = 64
ID = 128
KBLOCK = 32
DQK = 192
LANES = 128
PAIR = 2 * DQK
NEG = -1e30
SMALL = 2.0**-90
LARGE = 2.0**100
BIG = 2**30
LOG2E = math.log2(math.e)
SCALE_MAIN = DQK ** (-0.5) * LOG2E
SCALE_INDEX = ID ** (-0.5)

f32 = jnp.float32
bf16 = jnp.bfloat16
IN_VMEM = pl.BlockSpec(memory_space=pltpu.VMEM)


def dot_nt(a, b):
    return lax.dot_general(a, b, (((1,), (1,)), ((), ())), preferred_element_type=f32)


def dot_nn(a, b):
    return lax.dot_general(a, b, (((1,), (0,)), ((), ())), preferred_element_type=f32)


def cost(flops, bytes_accessed, transcendentals=0):
    return pl.CostEstimate(
        flops=int(flops), bytes_accessed=int(bytes_accessed), transcendentals=int(transcendentals)
    )


def combine_lse(parts):
    if len(parts) == 1:
        return parts[0]
    top = functools.reduce(jnp.maximum, parts)
    return top + jnp.log2(functools.reduce(jnp.add, [jnp.exp2(p - top) for p in parts]))


def packed_sizes(keys):
    return [keys * part // 32 for part in (18, 20, 22, 32)]


def for_packed(live, keys, run):
    below = 0
    for size in packed_sizes(keys):
        pl.when((live > below) & (live <= size))(functools.partial(run, size))
        below = size


def packing(count_ref, keys):
    lane = lax.broadcasted_iota(jnp.int32, (1, keys), 1)
    block, place = lane // KBLOCK, lane % KBLOCK
    rank = jnp.full((1, keys), -1, jnp.int32)
    base = jnp.int32(0)
    for b in range(keys // KBLOCK):
        here = count_ref[b]
        rank = jnp.where((block == b) & (place < here), base + place, rank)
        base = base + here
    return rank, base


def main_keys(nope, parity, even_ref, odd_ref):
    count = nope.shape[0]
    if parity == 0:
        return jnp.concatenate([nope, even_ref[:count, :]], axis=1)
    turned = jnp.concatenate([nope[:, DROPE:], nope[:, :DROPE]], axis=1)
    low = lax.broadcasted_iota(jnp.int32, turned.shape, 1) < DROPE
    first = jnp.where(low, jnp.zeros_like(turned), turned)
    second = jnp.where(low, turned, odd_ref[:count, :])
    return jnp.concatenate([first, second], axis=1)


def lanes_at(index, width):
    return pl.ds(pl.multiple_of(index * width, LANES), width)


def stats_kernel(per, count_hbm, q_hbm, kn_hbm, rope_hbm, qpos_hbm, kpos_hbm, iq_hbm, ik_hbm,
                 lse_ref, q_ref, kk_ref, bias_ref, iq_ref, ik_ref, rank_ref, live_ref,
                 kn_ref, rope_ref, qpos_ref, kpos_ref, even_ref, odd_ref, none_ref, bad_ref,
                 pack_ref, raw_ref, one_ref, two_ref, count_ref, small_sem, q_sem, kn_sem, iq_sem):
    keys = kn_ref.shape[0]
    groups, rows = q_ref.shape[0], q_ref.shape[1]
    pairs = q_ref.shape[2] // PAIR
    halves = [slice(2 * c * rows, (2 * c + 2) * rows) for c in range(groups // 2)]

    small = [
        pltpu.make_async_copy(src, dst, small_sem.at[i])
        for i, (src, dst) in enumerate(
            ((count_hbm, count_ref), (kpos_hbm, kpos_ref), (qpos_hbm, qpos_ref), (rope_hbm, rope_ref),
             (ik_hbm, raw_ref))
        )
    ]

    def large(i):
        q_at, k_at = lanes_at(i, PAIR), lanes_at(i, 2 * DNOPE)
        return (
            pltpu.make_async_copy(kn_hbm.at[:, k_at], kn_ref.at[:, k_at], kn_sem.at[i]),
            pltpu.make_async_copy(q_hbm.at[:, :, q_at], q_ref.at[:, :, q_at], q_sem.at[i]),
        )

    for copy in small:
        copy.start()
    for i in range(pairs):
        for copy in large(i):
            copy.start()
    index_copy = pltpu.make_async_copy(iq_hbm, iq_ref, iq_sem)
    index_copy.start()
    for copy in small:
        copy.wait()

    rank, live = packing(count_ref, keys)
    row = lax.broadcasted_iota(jnp.int32, (keys, keys), 0)
    chosen = row == rank
    pack_ref[...] = jnp.where(chosen, 1.0, 0.0).astype(bf16)
    rank_ref[...] = jnp.broadcast_to(rank, rank_ref.shape)
    live_ref[...] = jnp.broadcast_to(live, live_ref.shape)
    position = kpos_ref[...].astype(f32)
    digits = [rope_ref[...].astype(f32)]
    for unit in (2048.0, 32.0, 1.0):
        digit = jnp.floor(position / unit)
        position = position - digit * unit
        digits.append(digit)
    digits.append(jnp.zeros((LANES - DROPE - 3, keys), f32))
    packed = dot_nt(pack_ref[...], jnp.concatenate(digits, axis=0).astype(bf16))
    position = (
        packed[:, DROPE : DROPE + 1] * 2048.0
        + packed[:, DROPE + 1 : DROPE + 2] * 32.0
        + packed[:, DROPE + 2 : DROPE + 3]
    )
    column = jnp.where(row[:, :1] < live, position.astype(jnp.int32), BIG)
    rope = packed[:, :DROPE].astype(bf16)
    zero = jnp.zeros_like(rope)
    even_ref[...] = jnp.concatenate([rope, zero], axis=1)
    odd_ref[...] = jnp.concatenate([zero, rope], axis=1)
    for g in range(groups):
        valid = column <= qpos_ref[g : g + 1, :]
        bias = jnp.where(valid, 0.0, NEG)
        bias_ref[:, g * rows : (g + 1) * rows] = bias
        none_ref[:, g * rows : (g + 1) * rows] = jnp.where(
            jnp.max(bias, axis=0, keepdims=True) < 0, 1.0, 0.0
        )
    bad_ref[...] = jnp.zeros_like(bad_ref)

    def scores(kk, q3, c):
        q = q3.reshape(2 * rows, 2 * LANES)
        return dot_nt(kk, q) * SCALE_MAIN + bias_ref[: kk.shape[0], halves[c]]

    def query(pair, a, c):
        at = pl.ds(pl.multiple_of(pair * PAIR + a * LANES, LANES), 2 * LANES)
        return q_ref[2 * c : 2 * c + 2, :, at]

    steps = pairs // per

    def arrive(i):
        for p in range(per):
            for copy in large(i * per + p):
                copy.wait()

    def build(size, buf, i):
        for p in range(per):
            pair = i * per + p
            both = dot_nn(pack_ref[:size, :], kn_ref[:, lanes_at(pair, 2 * DNOPE)]).astype(bf16)
            for a in range(2):
                kk = main_keys(both[:, a * DNOPE : (a + 1) * DNOPE], a, even_ref, odd_ref)
                kk_ref[:size, lanes_at(2 * pair + a, 2 * LANES)] = kk
                at = (2 * p + a) * 2 * LANES
                buf[:size, at : at + 2 * LANES] = kk

    def process(size, buf, i):
        for p in range(per):
            pair = i * per + p
            for a in range(2):
                at = (2 * p + a) * 2 * LANES
                kk = buf[:size, at : at + 2 * LANES]
                for c, cols in enumerate(halves):
                    s = scores(kk, query(pair, a, c), c)
                    total = jnp.sum(jnp.exp2(s), axis=0, keepdims=True)
                    fine = (total >= SMALL) & (total <= LARGE)
                    skip = none_ref[:, cols] > 0
                    bad_ref[:, cols] += jnp.where(fine | skip, 0.0, 1.0)
                    lse_ref[pl.ds(2 * pair + a, 1), cols] = jnp.where(skip, NEG, jnp.log2(total))

    def step(size, i, carry):
        arrive(2 * i + 1)
        pl.when(2 * i + 2 < steps)(lambda: arrive(2 * i + 2))
        process(size, one_ref, 2 * i)
        build(size, two_ref, 2 * i + 1)
        process(size, two_ref, 2 * i + 1)
        build(size, one_ref, jnp.minimum(2 * i + 2, steps - 1))
        return carry

    def run(size):
        build(size, one_ref, 0)
        lax.fori_loop(0, steps // 2, functools.partial(step, size), 0)

    arrive(0)
    for_packed(live, keys, run)
    ik_ref[...] = dot_nn(pack_ref[...], raw_ref[...])
    index_copy.wait()

    @pl.when(jnp.max(bad_ref[...]) > 0)
    def _():
        def again(pair, carry):
            for a in range(2):
                kk = kk_ref[:, lanes_at(2 * pair + a, 2 * LANES)]
                for c, cols in enumerate(halves):
                    s = jnp.where(bias_ref[:, cols] < 0, NEG, scores(kk, query(pair, a, c), c))
                    top = jnp.max(s, axis=0, keepdims=True)
                    total = jnp.sum(jnp.exp2(s - top), axis=0, keepdims=True)
                    lse_ref[pl.ds(2 * pair + a, 1), cols] = top + jnp.log2(total)
            return carry

        lax.fori_loop(0, pairs, again, 0)


def main_stats(main_query, key_nope, rope_t, query_pos, key_pos, key_count, index_query, index_key):
    groups, rows, width = main_query.shape
    heads = width // DQK
    keys = key_nope.shape[0]
    total = groups * rows
    return pl.pallas_call(
        functools.partial(stats_kernel, 2),
        in_specs=[pl.BlockSpec(memory_space=pltpu.HBM)] * 8,
        out_specs=[IN_VMEM] * 8,
        out_shape=[
            jax.ShapeDtypeStruct((heads, total), f32),
            jax.ShapeDtypeStruct(main_query.shape, bf16),
            jax.ShapeDtypeStruct((keys, heads * 2 * LANES), bf16),
            jax.ShapeDtypeStruct((keys, total), f32),
            jax.ShapeDtypeStruct(index_query.shape, bf16),
            jax.ShapeDtypeStruct(index_key.shape, f32),
            jax.ShapeDtypeStruct((8, keys), jnp.int32),
            jax.ShapeDtypeStruct((8, LANES), jnp.int32),
        ],
        scratch_shapes=[
            pltpu.VMEM(key_nope.shape, bf16),
            pltpu.VMEM(rope_t.shape, bf16),
            pltpu.VMEM(query_pos.shape, jnp.int32),
            pltpu.VMEM(key_pos.shape, jnp.int32),
            pltpu.VMEM((keys, LANES), bf16),
            pltpu.VMEM((keys, LANES), bf16),
            pltpu.VMEM((1, total), f32),
            pltpu.VMEM((1, total), f32),
            pltpu.VMEM((keys, keys), bf16),
            pltpu.VMEM(index_key.shape, bf16),
            pltpu.VMEM((keys, 8 * LANES), bf16),
            pltpu.VMEM((keys, 8 * LANES), bf16),
            pltpu.SMEM(key_count.shape, jnp.int32),
            pltpu.SemaphoreType.DMA((5,)),
            pltpu.SemaphoreType.DMA((heads // 2,)),
            pltpu.SemaphoreType.DMA((heads // 2,)),
            pltpu.SemaphoreType.DMA,
        ],
        compiler_params=pltpu.CompilerParams(vmem_limit_bytes=16 * 1024 * 1024),
        cost_estimate=cost(
            heads * total * keys * 512, main_query.size * 2 + key_nope.size * 2, heads * total * keys
        ),
        name="main_stats",
    )(key_count, main_query, key_nope, rope_t, query_pos, key_pos, index_query, index_key)


def spread_kernel(rank_ref, spread_ref):
    keys = rank_ref.shape[1]
    column = jnp.transpose(rank_ref[...])[:, :1]
    lane = lax.broadcasted_iota(jnp.int32, (keys, keys), 1)
    spread_ref[...] = jnp.where(lane == column, 1.0, 0.0).astype(bf16)


def spread_matrix(rank):
    keys = rank.shape[1]
    return pl.pallas_call(
        spread_kernel,
        in_specs=[IN_VMEM],
        out_specs=IN_VMEM,
        out_shape=jax.ShapeDtypeStruct((keys, keys), bf16),
        compiler_params=pltpu.CompilerParams(vmem_limit_bytes=8 * 1024 * 1024),
        cost_estimate=cost(keys * keys * 4, keys * keys * 2),
        name="spread_matrix",
    )(rank)


def target_kernel(n_lse, masks, per, parts, q_ref, kk_ref, bias_ref, live_ref, *refs):
    lse_refs = refs[:n_lse]
    out_refs = refs[n_lse:-1]
    glob_ref = refs[-1]
    n_groups = len(masks)
    keys = kk_ref.shape[0]
    rows = q_ref.shape[1]
    pairs = q_ref.shape[2] // PAIR
    size = keys // parts
    me = lax.axis_index("head")
    ids = [lax.bitwise_xor(me, mask) for mask in masks]
    tiles = [
        (g, slice(i * size, (i + 1) * size), out_refs[g * parts + i])
        for g in range(n_groups)
        for i in range(parts)
    ]
    for g in range(n_groups):
        at = lanes_at(ids[g], rows)
        glob_ref[:, g * rows : (g + 1) * rows] = combine_lse([r[:, at] for r in lse_refs])
    for ref in out_refs:
        ref[...] = jnp.zeros_like(ref)

    def step(rows_kept, i, carry):
        for p in range(per):
            pair = i * per + p
            acc = None
            for a in range(2):
                kk = kk_ref[:rows_kept, lanes_at(2 * pair + a, 2 * LANES)]
                at = pl.ds(pl.multiple_of(pair * PAIR + a * LANES, LANES), 2 * LANES)
                qs = [q_ref[g, :, at] for g in ids]
                q = qs[0] if n_groups == 1 else jnp.concatenate(qs, axis=0)
                lse = glob_ref[pl.ds(2 * pair + a, 1), :]
                e = jnp.exp2(dot_nt(kk, q) * SCALE_MAIN - lse)
                acc = e if acc is None else acc + e
            for g, at, ref in tiles:
                some = acc[at, g * rows : (g + 1) * rows]
                if some.shape[0]:
                    ref[: some.shape[0], :] += some
        return carry

    def run(rows_kept):
        lax.fori_loop(0, pairs // per, functools.partial(step, rows_kept), 0)

    for_packed(jnp.max(live_ref[...]), keys, run)
    for g, at, ref in tiles:
        ref[...] = jnp.where(bias_ref[at, lanes_at(ids[g], rows)] < 0, 0.0, ref[...])


def head_sums(masks, q, kk, bias, live, lses, parts=1):
    _, rows, width = q.shape
    heads = width // DQK
    keys = kk.shape[0]
    n = len(masks)
    return pl.pallas_call(
        functools.partial(target_kernel, len(lses), masks, 4 // n, parts),
        in_specs=[IN_VMEM] * (4 + len(lses)),
        out_specs=[IN_VMEM] * (n * parts),
        out_shape=[jax.ShapeDtypeStruct((keys // parts, rows), f32)] * (n * parts),
        scratch_shapes=[pltpu.VMEM((heads, n * rows), f32)],
        compiler_params=pltpu.CompilerParams(vmem_limit_bytes=16 * 1024 * 1024),
        cost_estimate=cost(
            heads * n * rows * keys * 512, heads * n * rows * keys // 16, heads * n * rows * keys
        ),
        name="head_sums",
    )(q, kk, bias, live, *lses)


def logits_kernel(per, iq_ref, wide_ref, wt_ref, bias_ref, live_ref,
                  logits_ref, lse_ref, wm_ref, w_ref, ik_ref):
    keys = wide_ref.shape[0]
    rows, width = iq_ref.shape
    w_ref[...] = wt_ref[...].astype(f32)
    ik_ref[...] = wide_ref[...].astype(bf16)
    logits_ref[...] = jnp.zeros_like(logits_ref)

    def step(size, i, carry):
        for p in range(per):
            first = 2 * (i * per + p)
            q = jnp.concatenate([iq_ref[:, lanes_at(first + a, ID)] for a in range(2)], axis=0)
            z = dot_nt(ik_ref[:size, :], q)
            w = jnp.concatenate([w_ref[pl.ds(first + a, 1), :] for a in range(2)], axis=1)
            masked = jnp.where(z > 0, w, 0.0)
            wm_ref[:size, lanes_at(i * per + p, 2 * rows)] = masked.astype(bf16)
            r = z * masked
            logits_ref[:size, :] += r[:, :rows] + r[:, rows:]
        return carry

    def run(size):
        lax.fori_loop(0, width // (2 * ID * per), functools.partial(step, size), 0)

    for_packed(jnp.max(live_ref[...]), keys, run)
    logits = logits_ref[...] * SCALE_INDEX
    logits_ref[...] = logits
    valid = bias_ref[:, lanes_at(lax.axis_index("head"), rows)] == 0
    s = jnp.where(valid, logits * LOG2E, NEG)
    top = jnp.max(s, axis=0, keepdims=True)
    lse_ref[...] = top + jnp.log2(jnp.sum(jnp.exp2(s - top), axis=0, keepdims=True))


def index_logits(index_query, index_key, weight_t, bias, live):
    rows, width = index_query.shape
    keys = index_key.shape[0]
    whole = lambda i: (0, 0)
    return pl.pallas_call(
        functools.partial(logits_kernel, 4),
        grid=(1,),
        in_specs=[
            IN_VMEM,
            IN_VMEM,
            pl.BlockSpec(weight_t.shape, whole),
            IN_VMEM,
            IN_VMEM,
        ],
        out_specs=[IN_VMEM] * 3,
        out_shape=[
            jax.ShapeDtypeStruct((keys, rows), f32),
            jax.ShapeDtypeStruct((1, rows), f32),
            jax.ShapeDtypeStruct((keys, (width // ID) * rows), bf16),
        ],
        scratch_shapes=[
            pltpu.VMEM((width // ID, rows), f32),
            pltpu.VMEM(index_key.shape, bf16),
        ],
        compiler_params=pltpu.CompilerParams(vmem_limit_bytes=16 * 1024 * 1024),
        cost_estimate=cost(2 * keys * rows * width, rows * width * 2 + keys * rows * width // ID * 2),
        name="index_logits",
    )(index_query, index_key, weight_t, bias, live)


def grad_key_kernel(n_parts, n_lse, per, *refs):
    parts = refs[:n_parts]
    lses = refs[n_parts : n_parts + n_lse]
    (logits_ref, wm_ref, iq_ref, bias_ref, live_ref, spread_ref, cot_ref,
     sg_ref, lo_ref, hi_ref, sum_ref) = refs[n_parts + n_lse :]
    keys, rows = logits_ref.shape
    width = iq_ref.shape[1]

    valid = bias_ref[:, lanes_at(lax.axis_index("head"), rows)] == 0
    target = functools.reduce(jnp.add, [p[...] for p in parts]) * (1.0 / H)
    logits = logits_ref[...]
    lse2 = combine_lse([r[...] for r in lses])
    qprob = jnp.where(valid, jnp.exp2(logits * LOG2E - lse2), 0.0)
    sg_ref[:keys, :] = SCALE_INDEX * (cot_ref[...] * (qprob - target))
    live = target > 0
    terms = jnp.where(live, target * (jnp.log(jnp.where(live, target, 1.0)) - logits), 0.0)
    kl = jnp.sum(terms, axis=0, keepdims=True)
    sg_ref[keys:, :] = jnp.broadcast_to(kl, (8, rows))
    sum_ref[...] = jnp.zeros_like(sum_ref)

    def step(size, i, carry):
        for p in range(per):
            dz = []
            qs = []
            for a in range(2):
                j = 2 * (i * per + p) + a
                wm = wm_ref[:size, lanes_at(j, rows)].astype(f32)
                dz.append((sg_ref[:size, :] * wm).astype(bf16))
                qs.append(iq_ref[:, lanes_at(j, ID)])
            sum_ref[:size, :] += dot_nn(jnp.concatenate(dz, axis=1), jnp.concatenate(qs, axis=0))
        return carry

    def run(size):
        lax.fori_loop(0, width // (2 * ID * per), functools.partial(step, size), 0)

    for_packed(jnp.max(live_ref[...]), keys, run)
    rest = sum_ref[...]
    pieces = []
    for _ in range(3):
        piece = rest.astype(bf16)
        pieces.append(piece)
        rest = rest - piece.astype(f32)
    placed = dot_nn(spread_ref[...], jnp.concatenate(pieces, axis=1))
    placed = placed[:, :ID] + placed[:, ID : 2 * ID] + placed[:, 2 * ID :]
    lo_ref[...] = placed[: keys // 2]
    hi_ref[...] = placed[keys // 2 :]


def index_grad_key(parts, lses, logits, wm, index_query, bias, live, spread, cotangent):
    rows, width = index_query.shape
    keys = logits.shape[0]
    return pl.pallas_call(
        functools.partial(grad_key_kernel, len(parts), len(lses), 8),
        grid=(1,),
        in_specs=[IN_VMEM] * (len(parts) + len(lses) + 6)
        + [pl.BlockSpec((1, rows), lambda i: (0, 0))],
        out_specs=[IN_VMEM] * 3,
        out_shape=[
            jax.ShapeDtypeStruct((keys + 8, rows), f32),
            jax.ShapeDtypeStruct((keys // 2, ID), f32),
            jax.ShapeDtypeStruct((keys // 2, ID), f32),
        ],
        scratch_shapes=[pltpu.VMEM((keys, ID), f32)],
        compiler_params=pltpu.CompilerParams(vmem_limit_bytes=16 * 1024 * 1024),
        cost_estimate=cost(2 * keys * rows * width, rows * width * 2 + keys * rows * width // ID * 2),
        name="index_grad_key",
    )(*parts, *lses, logits, wm, index_query, bias, live, spread, cotangent)


def grad_query_kernel(n_shards, first, n_lse, *refs):
    sgs = refs[:n_shards]
    iks = refs[n_shards : 2 * n_shards]
    iq_ref, w_ref = refs[2 * n_shards : 2 * n_shards + 2]
    rest = refs[2 * n_shards + 2 :]
    lses = rest[:n_lse]
    rest = rest[n_lse:]
    if first:
        gq_ref, kl_ref, ws_ref = rest
    else:
        gq_in_ref, kl_in_ref, gq_ref, kl_ref, ws_ref = rest
    rows = iq_ref.shape[0]
    heads = gq_ref.shape[1] // ID
    keys = iks[0].shape[0]
    base = lax.axis_index("key") * heads
    ws_ref[...] = w_ref[...].astype(f32)
    mine = ws_ref[pl.ds(base, heads), :]
    ws = jnp.transpose(jnp.concatenate([mine, jnp.zeros((LANES - heads, rows), f32)], axis=0))
    kl = functools.reduce(jnp.add, [s[keys : keys + 1, :] for s in sgs])
    kl = kl if first else kl_in_ref[...] + kl
    if n_lse:
        kl = kl + combine_lse([r[...] for r in lses]) * (1.0 / LOG2E)
    kl_ref[...] = kl
    unit = min(heads, 4)
    iks = [ref[...].astype(bf16) for ref in iks]
    sgts = [jnp.transpose(ref[:keys, :]) for ref in sgs]
    for start in range(0, heads, unit):
        js = range(start, start + unit)
        iq = jnp.concatenate([iq_ref[:, lanes_at(base + j, ID)] for j in js], axis=0)
        out = None
        for ik, sgt in zip(iks, sgts):
            z = dot_nt(iq, ik)
            dz = jnp.concatenate(
                [
                    jnp.where(z[i * rows : (i + 1) * rows] > 0, sgt * ws[:, j : j + 1], 0.0).astype(bf16)
                    for i, j in enumerate(js)
                ],
                axis=0,
            )
            g = dot_nn(dz, ik)
            out = g if out is None else out + g
        for i, j in enumerate(js):
            cols = slice(j * ID, (j + 1) * ID)
            g = out[i * rows : (i + 1) * rows]
            gq_ref[:, cols] = g if first else gq_in_ref[:, cols] + g


def index_grad_query(n_slots, sgs, iks, index_query, weight_t, lses, carry):
    rows, width = index_query.shape
    heads = width // ID
    mine = width // n_slots
    keys = iks[0].shape[0]
    first = carry is None
    carried = [] if first else list(carry)
    n = len(sgs)
    return pl.pallas_call(
        functools.partial(grad_query_kernel, n, first, len(lses)),
        grid=(1,),
        in_specs=[IN_VMEM] * (2 * n + 1)
        + [pl.BlockSpec(weight_t.shape, lambda i: (0, 0))]
        + [IN_VMEM] * (len(lses) + len(carried)),
        out_specs=[IN_VMEM, IN_VMEM],
        out_shape=[
            jax.ShapeDtypeStruct((rows, mine), f32),
            jax.ShapeDtypeStruct((1, rows), f32),
        ],
        scratch_shapes=[pltpu.VMEM((heads, rows), f32)],
        compiler_params=pltpu.CompilerParams(vmem_limit_bytes=20 * 1024 * 1024),
        cost_estimate=cost(4 * n * keys * rows * mine, n * (keys * ID * 8) + rows * mine * 8),
        name="index_grad_query",
    )(*sgs, *iks, index_query, weight_t, *lses, *carried)


def swap(value, axis, mask, size):
    return lax.ppermute(value, axis, [(i, i ^ mask) for i in range(size)])


def butterfly_lse(value, size):
    pair = [value]
    for bit in reversed(range(size.bit_length() - 1)):
        here = combine_lse(pair)
        pair = [here, swap(here, "key", 1 << bit, size)]
    return pair


def summed_copies(pieces, n_head, n_query):
    steps = [("head", (2 << b) - 1, n_head) for b in reversed(range(n_head.bit_length() - 1))]
    steps += [("query", 1 << b, n_query) for b in range(n_query.bit_length() - 1)]
    steps = steps[:1] + steps[2:] + steps[1:2]
    for number in range(len(steps)):
        moved = []
        for i, piece in enumerate(pieces):
            moved.append(swap(piece, *steps[(number - i) % len(steps)]))
        pieces = [piece + other for piece, other in zip(pieces, moved)]
    return jnp.concatenate(pieces, axis=0)


def in_hbm(*values):
    return tuple(pltpu.with_memory_space_constraint(v, pltpu.HBM) for v in values)


def body(n_key, n_head, n_query, main_query, key_nope, key_rope, query_pos, key_pos, key_count,
         index_query, index_key, index_weight, row_cotangent):
    groups, rows, _ = main_query.shape
    keys = key_nope.shape[0]
    (main_query, key_nope, rope_t, query_pos, key_row, key_count, weight_t, cotangent, narrow,
     index_query) = in_hbm(
        main_query, key_nope, key_rope.T, query_pos, key_pos.reshape(1, keys), key_count,
        index_weight.T, row_cotangent.reshape(1, rows), index_key, index_query,
    )

    def gathered(value):
        if n_key == 4:
            near = swap(value, "key", 1, n_key)
            far = swap(value, "key", 2, n_key)
            across = swap(far, "key", 1, n_key)
            return [value, near, far, across]
        return list(lax.all_gather(value, "key"))

    lse, q, kk, bias, iq, wide, rank, live = main_stats(
        main_query, key_nope, rope_t, query_pos, key_row, key_count, index_query, narrow
    )
    lses = butterfly_lse(lse, n_key)
    logits, index_lse, wm = index_logits(iq, wide, weight_t, bias, live)
    index_lses = butterfly_lse(index_lse, n_key)
    iks = gathered(wide)

    half = keys // 2
    if n_head == 4 and groups == 4:
        low, high = head_sums([2], q, kk, bias, live, lses, parts=2)
        low = swap(low, "head", 1, 4)
        high = swap(high, "head", 3, 4)
        up, down = head_sums([1, 3], q, kk, bias, live, lses)
        up = up + jnp.pad(high, ((half, 0), (0, 0)))
        down = down + jnp.pad(low, ((0, half), (0, 0)))
        from_up = swap(up, "head", 1, 4)
        from_down = swap(down, "head", 3, 4)
        own = head_sums([0], q, kk, bias, live, lses)[0]
        parts = [own, from_up, from_down]
    else:
        z = lax.axis_index("head")
        tiles = jnp.stack([head_sums([g], q, kk, bias, live, lses)[0] for g in range(groups)])
        tiles = tiles[jnp.bitwise_xor(jnp.arange(groups), z)]
        parts = [lax.psum_scatter(tiles, "head", scatter_dimension=0, tiled=True)[0]]

    spread = spread_matrix(rank)
    sg, *grad_key = index_grad_key(
        parts, index_lses, logits, wm, iq, bias, live, spread, cotangent
    )
    grad_key = summed_copies(grad_key, n_head, n_query)
    sgs = gathered(sg)
    carry = None
    for lo in range(0, n_key, 2):
        last = lo + 2 >= n_key
        carry = index_grad_query(
            n_key, sgs[lo : lo + 2], iks[lo : lo + 2], iq, weight_t,
            index_lses if last else [], carry,
        )
    grad_query, kl = carry
    return kl.reshape(rows), grad_query, grad_key


def solution(mesh):
    sizes = (mesh.shape["key"], mesh.shape["head"], mesh.shape["query"])

    def step(*args):
        return body(*sizes, *args)

    return jax.shard_map(
        step,
        mesh=mesh,
        in_specs=(
            P(None, "query", "head"),
            P("key", "head"),
            P("key", None),
            P(None, "query"),
            P("key"),
            P("key"),
            P(("head", "query"), None),
            P("key", None),
            P(("head", "query"), None),
            P(("head", "query")),
        ),
        out_specs=(P(("head", "query")), P(("head", "query"), "key"), P("key", None)),
        check_vma=False,
    )
```

```python
import functools
import math
import jax
import jax.numpy as jnp
from jax import lax
from jax.experimental import pallas as pl
from jax.experimental.pallas import tpu as pltpu
from jax.sharding import PartitionSpec as P


H = 128
DNOPE = 128
DROPE = 64
ID = 128
KBLOCK = 32
DQK = 192
LANES = 128
PAIR = 2 * DQK
NEG = -1e30
SMALL = 2.0**-90
LARGE = 2.0**100
BIG = 2**30
LOG2E = math.log2(math.e)
SCALE_MAIN = DQK ** (-0.5) * LOG2E
SCALE_INDEX = ID ** (-0.5)

f32 = jnp.float32
bf16 = jnp.bfloat16
IN_VMEM = pl.BlockSpec(memory_space=pltpu.VMEM)


def dot_nt(a, b):
    return lax.dot_general(a, b, (((1,), (1,)), ((), ())), preferred_element_type=f32)


def dot_nn(a, b):
    return lax.dot_general(a, b, (((1,), (0,)), ((), ())), preferred_element_type=f32)


def cost(flops, bytes_accessed, transcendentals=0):
    return pl.CostEstimate(
        flops=int(flops), bytes_accessed=int(bytes_accessed), transcendentals=int(transcendentals)
    )


def combine_lse(parts):
    if len(parts) == 1:
        return parts[0]
    top = functools.reduce(jnp.maximum, parts)
    return top + jnp.log2(functools.reduce(jnp.add, [jnp.exp2(p - top) for p in parts]))


def packed_sizes(keys):
    return [keys * part // 32 for part in (18, 20, 22, 32)]


def for_packed(live, keys, run):
    below = 0
    for size in packed_sizes(keys):
        pl.when((live > below) & (live <= size))(functools.partial(run, size))
        below = size


def packing(count_ref, keys):
    lane = lax.broadcasted_iota(jnp.int32, (1, keys), 1)
    block, place = lane // KBLOCK, lane % KBLOCK
    rank = jnp.full((1, keys), -1, jnp.int32)
    base = jnp.int32(0)
    for b in range(keys // KBLOCK):
        here = count_ref[b]
        rank = jnp.where((block == b) & (place < here), base + place, rank)
        base = base + here
    return rank, base


def main_keys(nope, parity, even_ref, odd_ref):
    count = nope.shape[0]
    if parity == 0:
        return jnp.concatenate([nope, even_ref[:count, :]], axis=1)
    turned = jnp.concatenate([nope[:, DROPE:], nope[:, :DROPE]], axis=1)
    low = lax.broadcasted_iota(jnp.int32, turned.shape, 1) < DROPE
    first = jnp.where(low, jnp.zeros_like(turned), turned)
    second = jnp.where(low, turned, odd_ref[:count, :])
    return jnp.concatenate([first, second], axis=1)


def lanes_at(index, width):
    return pl.ds(pl.multiple_of(index * width, LANES), width)


def stats_kernel(per, count_hbm, q_hbm, kn_hbm, rope_hbm, qpos_hbm, kpos_hbm, iq_hbm, ik_hbm,
                 lse_ref, q_ref, kk_ref, bias_ref, iq_ref, ik_ref, rank_ref, live_ref,
                 kn_ref, rope_ref, qpos_ref, kpos_ref, even_ref, odd_ref, none_ref, bad_ref,
                 pack_ref, raw_ref, one_ref, two_ref, count_ref, small_sem, q_sem, kn_sem, iq_sem):
    keys = kn_ref.shape[0]
    groups, rows = q_ref.shape[0], q_ref.shape[1]
    pairs = q_ref.shape[2] // PAIR
    halves = [slice(2 * c * rows, (2 * c + 2) * rows) for c in range(groups // 2)]

    small = [
        pltpu.make_async_copy(src, dst, small_sem.at[i])
        for i, (src, dst) in enumerate(
            ((count_hbm, count_ref), (kpos_hbm, kpos_ref), (qpos_hbm, qpos_ref), (rope_hbm, rope_ref),
             (ik_hbm, raw_ref))
        )
    ]

    def large(i):
        q_at, k_at = lanes_at(i, PAIR), lanes_at(i, 2 * DNOPE)
        return (
            pltpu.make_async_copy(kn_hbm.at[:, k_at], kn_ref.at[:, k_at], kn_sem.at[i]),
            pltpu.make_async_copy(q_hbm.at[:, :, q_at], q_ref.at[:, :, q_at], q_sem.at[i]),
        )

    for copy in small:
        copy.start()
    for i in range(pairs):
        for copy in large(i):
            copy.start()
    index_copy = pltpu.make_async_copy(iq_hbm, iq_ref, iq_sem)
    index_copy.start()
    for copy in small:
        copy.wait()

    rank, live = packing(count_ref, keys)
    row = lax.broadcasted_iota(jnp.int32, (keys, keys), 0)
    chosen = row == rank
    pack_ref[...] = jnp.where(chosen, 1.0, 0.0).astype(bf16)
    rank_ref[...] = jnp.broadcast_to(rank, rank_ref.shape)
    live_ref[...] = jnp.broadcast_to(live, live_ref.shape)
    position = kpos_ref[...].astype(f32)
    digits = [rope_ref[...].astype(f32)]
    for unit in (2048.0, 32.0, 1.0):
        digit = jnp.floor(position / unit)
        position = position - digit * unit
        digits.append(digit)
    digits.append(jnp.zeros((LANES - DROPE - 3, keys), f32))
    packed = dot_nt(pack_ref[...], jnp.concatenate(digits, axis=0).astype(bf16))
    position = (
        packed[:, DROPE : DROPE + 1] * 2048.0
        + packed[:, DROPE + 1 : DROPE + 2] * 32.0
        + packed[:, DROPE + 2 : DROPE + 3]
    )
    column = jnp.where(row[:, :1] < live, position.astype(jnp.int32), BIG)
    rope = packed[:, :DROPE].astype(bf16)
    zero = jnp.zeros_like(rope)
    even_ref[...] = jnp.concatenate([rope, zero], axis=1)
    odd_ref[...] = jnp.concatenate([zero, rope], axis=1)
    for g in range(groups):
        valid = column <= qpos_ref[g : g + 1, :]
        bias = jnp.where(valid, 0.0, NEG)
        bias_ref[:, g * rows : (g + 1) * rows] = bias
        none_ref[:, g * rows : (g + 1) * rows] = jnp.where(
            jnp.max(bias, axis=0, keepdims=True) < 0, 1.0, 0.0
        )
    bad_ref[...] = jnp.zeros_like(bad_ref)

    def scores(kk, q3, c):
        q = q3.reshape(2 * rows, 2 * LANES)
        return dot_nt(kk, q) * SCALE_MAIN + bias_ref[: kk.shape[0], halves[c]]

    def query(pair, a, c):
        at = pl.ds(pl.multiple_of(pair * PAIR + a * LANES, LANES), 2 * LANES)
        return q_ref[2 * c : 2 * c + 2, :, at]

    steps = pairs // per

    def arrive(i):
        for p in range(per):
            for copy in large(i * per + p):
                copy.wait()

    def build(size, buf, i):
        for p in range(per):
            pair = i * per + p
            both = dot_nn(pack_ref[:size, :], kn_ref[:, lanes_at(pair, 2 * DNOPE)]).astype(bf16)
            for a in range(2):
                kk = main_keys(both[:, a * DNOPE : (a + 1) * DNOPE], a, even_ref, odd_ref)
                kk_ref[:size, lanes_at(2 * pair + a, 2 * LANES)] = kk
                at = (2 * p + a) * 2 * LANES
                buf[:size, at : at + 2 * LANES] = kk

    def process(size, buf, i):
        for p in range(per):
            pair = i * per + p
            for a in range(2):
                at = (2 * p + a) * 2 * LANES
                kk = buf[:size, at : at + 2 * LANES]
                for c, cols in enumerate(halves):
                    s = scores(kk, query(pair, a, c), c)
                    total = jnp.sum(jnp.exp2(s), axis=0, keepdims=True)
                    fine = (total >= SMALL) & (total <= LARGE)
                    skip = none_ref[:, cols] > 0
                    bad_ref[:, cols] += jnp.where(fine | skip, 0.0, 1.0)
                    lse_ref[pl.ds(2 * pair + a, 1), cols] = jnp.where(skip, NEG, jnp.log2(total))

    def step(size, i, carry):
        arrive(2 * i + 1)
        pl.when(2 * i + 2 < steps)(lambda: arrive(2 * i + 2))
        process(size, one_ref, 2 * i)
        build(size, two_ref, 2 * i + 1)
        process(size, two_ref, 2 * i + 1)
        build(size, one_ref, jnp.minimum(2 * i + 2, steps - 1))
        return carry

    def run(size):
        build(size, one_ref, 0)
        lax.fori_loop(0, steps // 2, functools.partial(step, size), 0)

    arrive(0)
    for_packed(live, keys, run)
    ik_ref[...] = dot_nn(pack_ref[...], raw_ref[...])
    index_copy.wait()

    @pl.when(jnp.max(bad_ref[...]) > 0)
    def _():
        def again(pair, carry):
            for a in range(2):
                kk = kk_ref[:, lanes_at(2 * pair + a, 2 * LANES)]
                for c, cols in enumerate(halves):
                    s = jnp.where(bias_ref[:, cols] < 0, NEG, scores(kk, query(pair, a, c), c))
                    top = jnp.max(s, axis=0, keepdims=True)
                    total = jnp.sum(jnp.exp2(s - top), axis=0, keepdims=True)
                    lse_ref[pl.ds(2 * pair + a, 1), cols] = top + jnp.log2(total)
            return carry

        lax.fori_loop(0, pairs, again, 0)


def main_stats(main_query, key_nope, rope_t, query_pos, key_pos, key_count, index_query, index_key):
    groups, rows, width = main_query.shape
    heads = width // DQK
    keys = key_nope.shape[0]
    total = groups * rows
    return pl.pallas_call(
        functools.partial(stats_kernel, 2),
        in_specs=[pl.BlockSpec(memory_space=pltpu.HBM)] * 8,
        out_specs=[IN_VMEM] * 8,
        out_shape=[
            jax.ShapeDtypeStruct((heads, total), f32),
            jax.ShapeDtypeStruct(main_query.shape, bf16),
            jax.ShapeDtypeStruct((keys, heads * 2 * LANES), bf16),
            jax.ShapeDtypeStruct((keys, total), f32),
            jax.ShapeDtypeStruct(index_query.shape, bf16),
            jax.ShapeDtypeStruct(index_key.shape, f32),
            jax.ShapeDtypeStruct((8, keys), jnp.int32),
            jax.ShapeDtypeStruct((8, LANES), jnp.int32),
        ],
        scratch_shapes=[
            pltpu.VMEM(key_nope.shape, bf16),
            pltpu.VMEM(rope_t.shape, bf16),
            pltpu.VMEM(query_pos.shape, jnp.int32),
            pltpu.VMEM(key_pos.shape, jnp.int32),
            pltpu.VMEM((keys, LANES), bf16),
            pltpu.VMEM((keys, LANES), bf16),
            pltpu.VMEM((1, total), f32),
            pltpu.VMEM((1, total), f32),
            pltpu.VMEM((keys, keys), bf16),
            pltpu.VMEM(index_key.shape, bf16),
            pltpu.VMEM((keys, 8 * LANES), bf16),
            pltpu.VMEM((keys, 8 * LANES), bf16),
            pltpu.SMEM(key_count.shape, jnp.int32),
            pltpu.SemaphoreType.DMA((5,)),
            pltpu.SemaphoreType.DMA((heads // 2,)),
            pltpu.SemaphoreType.DMA((heads // 2,)),
            pltpu.SemaphoreType.DMA,
        ],
        compiler_params=pltpu.CompilerParams(vmem_limit_bytes=16 * 1024 * 1024),
        cost_estimate=cost(
            heads * total * keys * 512, main_query.size * 2 + key_nope.size * 2, heads * total * keys
        ),
        name="main_stats",
    )(key_count, main_query, key_nope, rope_t, query_pos, key_pos, index_query, index_key)


def spread_kernel(rank_ref, spread_ref):
    keys = rank_ref.shape[1]
    column = jnp.transpose(rank_ref[...])[:, :1]
    lane = lax.broadcasted_iota(jnp.int32, (keys, keys), 1)
    spread_ref[...] = jnp.where(lane == column, 1.0, 0.0).astype(bf16)


def spread_matrix(rank):
    keys = rank.shape[1]
    return pl.pallas_call(
        spread_kernel,
        in_specs=[IN_VMEM],
        out_specs=IN_VMEM,
        out_shape=jax.ShapeDtypeStruct((keys, keys), bf16),
        compiler_params=pltpu.CompilerParams(vmem_limit_bytes=8 * 1024 * 1024),
        cost_estimate=cost(keys * keys * 4, keys * keys * 2),
        name="spread_matrix",
    )(rank)


def target_kernel(n_lse, masks, per, parts, q_ref, kk_ref, bias_ref, live_ref, *refs):
    lse_refs = refs[:n_lse]
    out_refs = refs[n_lse:-1]
    glob_ref = refs[-1]
    n_groups = len(masks)
    keys = kk_ref.shape[0]
    rows = q_ref.shape[1]
    pairs = q_ref.shape[2] // PAIR
    size = keys // parts
    me = lax.axis_index("head")
    ids = [lax.bitwise_xor(me, mask) for mask in masks]
    tiles = [
        (g, slice(i * size, (i + 1) * size), out_refs[g * parts + i])
        for g in range(n_groups)
        for i in range(parts)
    ]
    for g in range(n_groups):
        at = lanes_at(ids[g], rows)
        glob_ref[:, g * rows : (g + 1) * rows] = combine_lse([r[:, at] for r in lse_refs])
    for ref in out_refs:
        ref[...] = jnp.zeros_like(ref)

    def step(rows_kept, i, carry):
        for p in range(per):
            pair = i * per + p
            acc = None
            for a in range(2):
                kk = kk_ref[:rows_kept, lanes_at(2 * pair + a, 2 * LANES)]
                at = pl.ds(pl.multiple_of(pair * PAIR + a * LANES, LANES), 2 * LANES)
                qs = [q_ref[g, :, at] for g in ids]
                q = qs[0] if n_groups == 1 else jnp.concatenate(qs, axis=0)
                lse = glob_ref[pl.ds(2 * pair + a, 1), :]
                e = jnp.exp2(dot_nt(kk, q) * SCALE_MAIN - lse)
                acc = e if acc is None else acc + e
            for g, at, ref in tiles:
                some = acc[at, g * rows : (g + 1) * rows]
                if some.shape[0]:
                    ref[: some.shape[0], :] += some
        return carry

    def run(rows_kept):
        lax.fori_loop(0, pairs // per, functools.partial(step, rows_kept), 0)

    for_packed(jnp.max(live_ref[...]), keys, run)
    for g, at, ref in tiles:
        ref[...] = jnp.where(bias_ref[at, lanes_at(ids[g], rows)] < 0, 0.0, ref[...])


def head_sums(masks, q, kk, bias, live, lses, parts=1):
    _, rows, width = q.shape
    heads = width // DQK
    keys = kk.shape[0]
    n = len(masks)
    return pl.pallas_call(
        functools.partial(target_kernel, len(lses), masks, 4 // n, parts),
        in_specs=[IN_VMEM] * (4 + len(lses)),
        out_specs=[IN_VMEM] * (n * parts),
        out_shape=[jax.ShapeDtypeStruct((keys // parts, rows), f32)] * (n * parts),
        scratch_shapes=[pltpu.VMEM((heads, n * rows), f32)],
        compiler_params=pltpu.CompilerParams(vmem_limit_bytes=16 * 1024 * 1024),
        cost_estimate=cost(
            heads * n * rows * keys * 512, heads * n * rows * keys // 16, heads * n * rows * keys
        ),
        name="head_sums",
    )(q, kk, bias, live, *lses)


def logits_kernel(per, iq_ref, wide_ref, wt_ref, bias_ref, live_ref,
                  logits_ref, lse_ref, wm_ref, w_ref, ik_ref):
    keys = wide_ref.shape[0]
    rows, width = iq_ref.shape
    w_ref[...] = wt_ref[...].astype(f32)
    ik_ref[...] = wide_ref[...].astype(bf16)
    logits_ref[...] = jnp.zeros_like(logits_ref)

    def step(size, i, carry):
        for p in range(per):
            first = 2 * (i * per + p)
            q = jnp.concatenate([iq_ref[:, lanes_at(first + a, ID)] for a in range(2)], axis=0)
            z = dot_nt(ik_ref[:size, :], q)
            w = jnp.concatenate([w_ref[pl.ds(first + a, 1), :] for a in range(2)], axis=1)
            masked = jnp.where(z > 0, w, 0.0)
            wm_ref[:size, lanes_at(i * per + p, 2 * rows)] = masked.astype(bf16)
            r = z * masked
            logits_ref[:size, :] += r[:, :rows] + r[:, rows:]
        return carry

    def run(size):
        lax.fori_loop(0, width // (2 * ID * per), functools.partial(step, size), 0)

    for_packed(jnp.max(live_ref[...]), keys, run)
    logits = logits_ref[...] * SCALE_INDEX
    logits_ref[...] = logits
    valid = bias_ref[:, lanes_at(lax.axis_index("head"), rows)] == 0
    s = jnp.where(valid, logits * LOG2E, NEG)
    top = jnp.max(s, axis=0, keepdims=True)
    lse_ref[...] = top + jnp.log2(jnp.sum(jnp.exp2(s - top), axis=0, keepdims=True))


def index_logits(index_query, index_key, weight_t, bias, live):
    rows, width = index_query.shape
    keys = index_key.shape[0]
    whole = lambda i: (0, 0)
    return pl.pallas_call(
        functools.partial(logits_kernel, 4),
        grid=(1,),
        in_specs=[
            IN_VMEM,
            IN_VMEM,
            pl.BlockSpec(weight_t.shape, whole),
            IN_VMEM,
            IN_VMEM,
        ],
        out_specs=[IN_VMEM] * 3,
        out_shape=[
            jax.ShapeDtypeStruct((keys, rows), f32),
            jax.ShapeDtypeStruct((1, rows), f32),
            jax.ShapeDtypeStruct((keys, (width // ID) * rows), bf16),
        ],
        scratch_shapes=[
            pltpu.VMEM((width // ID, rows), f32),
            pltpu.VMEM(index_key.shape, bf16),
        ],
        compiler_params=pltpu.CompilerParams(vmem_limit_bytes=16 * 1024 * 1024),
        cost_estimate=cost(2 * keys * rows * width, rows * width * 2 + keys * rows * width // ID * 2),
        name="index_logits",
    )(index_query, index_key, weight_t, bias, live)


def grad_key_kernel(n_parts, n_lse, per, *refs):
    parts = refs[:n_parts]
    lses = refs[n_parts : n_parts + n_lse]
    (logits_ref, wm_ref, iq_ref, bias_ref, live_ref, spread_ref, cot_ref,
     sg_ref, lo_ref, hi_ref, sum_ref) = refs[n_parts + n_lse :]
    keys, rows = logits_ref.shape
    width = iq_ref.shape[1]

    valid = bias_ref[:, lanes_at(lax.axis_index("head"), rows)] == 0
    target = parts[0][...]
    for i in range(1, n_parts, 2):
        target = target + jnp.concatenate([p[...] for p in parts[i : i + 2]], axis=0)
    target = target * (1.0 / H)
    logits = logits_ref[...]
    lse2 = combine_lse([r[...] for r in lses])
    qprob = jnp.where(valid, jnp.exp2(logits * LOG2E - lse2), 0.0)
    sg_ref[:keys, :] = SCALE_INDEX * (cot_ref[...] * (qprob - target))
    live = target > 0
    terms = jnp.where(live, target * (jnp.log(jnp.where(live, target, 1.0)) - logits), 0.0)
    kl = jnp.sum(terms, axis=0, keepdims=True)
    sg_ref[keys:, :] = jnp.broadcast_to(kl, (8, rows))
    sum_ref[...] = jnp.zeros_like(sum_ref)

    def step(size, i, carry):
        for p in range(per):
            dz = []
            qs = []
            for a in range(2):
                j = 2 * (i * per + p) + a
                wm = wm_ref[:size, lanes_at(j, rows)].astype(f32)
                dz.append((sg_ref[:size, :] * wm).astype(bf16))
                qs.append(iq_ref[:, lanes_at(j, ID)])
            sum_ref[:size, :] += dot_nn(jnp.concatenate(dz, axis=1), jnp.concatenate(qs, axis=0))
        return carry

    def run(size):
        lax.fori_loop(0, width // (2 * ID * per), functools.partial(step, size), 0)

    for_packed(jnp.max(live_ref[...]), keys, run)
    rest = sum_ref[...]
    pieces = []
    for _ in range(3):
        piece = rest.astype(bf16)
        pieces.append(piece)
        rest = rest - piece.astype(f32)
    placed = dot_nn(spread_ref[...], jnp.concatenate(pieces, axis=1))
    placed = placed[:, :ID] + placed[:, ID : 2 * ID] + placed[:, 2 * ID :]
    lo_ref[...] = placed[: keys // 2]
    hi_ref[...] = placed[keys // 2 :]


def index_grad_key(parts, lses, logits, wm, index_query, bias, live, spread, cotangent):
    rows, width = index_query.shape
    keys = logits.shape[0]
    return pl.pallas_call(
        functools.partial(grad_key_kernel, len(parts), len(lses), 8),
        grid=(1,),
        in_specs=[IN_VMEM] * (len(parts) + len(lses) + 6)
        + [pl.BlockSpec((1, rows), lambda i: (0, 0))],
        out_specs=[IN_VMEM] * 3,
        out_shape=[
            jax.ShapeDtypeStruct((keys + 8, rows), f32),
            jax.ShapeDtypeStruct((keys // 2, ID), f32),
            jax.ShapeDtypeStruct((keys // 2, ID), f32),
        ],
        scratch_shapes=[pltpu.VMEM((keys, ID), f32)],
        compiler_params=pltpu.CompilerParams(vmem_limit_bytes=16 * 1024 * 1024),
        cost_estimate=cost(2 * keys * rows * width, rows * width * 2 + keys * rows * width // ID * 2),
        name="index_grad_key",
    )(*parts, *lses, logits, wm, index_query, bias, live, spread, cotangent)


def grad_query_kernel(n_shards, first, n_lse, *refs):
    sgs = refs[:n_shards]
    iks = refs[n_shards : 2 * n_shards]
    iq_ref, w_ref = refs[2 * n_shards : 2 * n_shards + 2]
    rest = refs[2 * n_shards + 2 :]
    lses = rest[:n_lse]
    rest = rest[n_lse:]
    if first:
        gq_ref, kl_ref, ws_ref = rest
    else:
        gq_in_ref, kl_in_ref, gq_ref, kl_ref, ws_ref = rest
    rows = iq_ref.shape[0]
    heads = gq_ref.shape[1] // ID
    keys = iks[0].shape[0]
    base = lax.axis_index("key") * heads
    ws_ref[...] = w_ref[...].astype(f32)
    mine = ws_ref[pl.ds(base, heads), :]
    ws = jnp.transpose(jnp.concatenate([mine, jnp.zeros((LANES - heads, rows), f32)], axis=0))
    kl = functools.reduce(jnp.add, [s[keys : keys + 1, :] for s in sgs])
    kl = kl if first else kl_in_ref[...] + kl
    if n_lse:
        kl = kl + combine_lse([r[...] for r in lses]) * (1.0 / LOG2E)
    kl_ref[...] = kl
    unit = min(heads, 4)
    iks = [ref[...].astype(bf16) for ref in iks]
    sgts = [jnp.transpose(ref[:keys, :]) for ref in sgs]
    for start in range(0, heads, unit):
        js = range(start, start + unit)
        iq = jnp.concatenate([iq_ref[:, lanes_at(base + j, ID)] for j in js], axis=0)
        out = None
        for ik, sgt in zip(iks, sgts):
            z = dot_nt(iq, ik)
            dz = jnp.concatenate(
                [
                    jnp.where(z[i * rows : (i + 1) * rows] > 0, sgt * ws[:, j : j + 1], 0.0).astype(bf16)
                    for i, j in enumerate(js)
                ],
                axis=0,
            )
            g = dot_nn(dz, ik)
            out = g if out is None else out + g
        for i, j in enumerate(js):
            cols = slice(j * ID, (j + 1) * ID)
            g = out[i * rows : (i + 1) * rows]
            gq_ref[:, cols] = g if first else gq_in_ref[:, cols] + g


def index_grad_query(n_slots, sgs, iks, index_query, weight_t, lses, carry):
    rows, width = index_query.shape
    heads = width // ID
    mine = width // n_slots
    keys = iks[0].shape[0]
    first = carry is None
    carried = [] if first else list(carry)
    n = len(sgs)
    return pl.pallas_call(
        functools.partial(grad_query_kernel, n, first, len(lses)),
        grid=(1,),
        in_specs=[IN_VMEM] * (2 * n + 1)
        + [pl.BlockSpec(weight_t.shape, lambda i: (0, 0))]
        + [IN_VMEM] * (len(lses) + len(carried)),
        out_specs=[IN_VMEM, IN_VMEM],
        out_shape=[
            jax.ShapeDtypeStruct((rows, mine), f32),
            jax.ShapeDtypeStruct((1, rows), f32),
        ],
        scratch_shapes=[pltpu.VMEM((heads, rows), f32)],
        compiler_params=pltpu.CompilerParams(vmem_limit_bytes=20 * 1024 * 1024),
        cost_estimate=cost(4 * n * keys * rows * mine, n * (keys * ID * 8) + rows * mine * 8),
        name="index_grad_query",
    )(*sgs, *iks, index_query, weight_t, *lses, *carried)


def swap(value, axis, mask, size):
    return lax.ppermute(value, axis, [(i, i ^ mask) for i in range(size)])


def butterfly_lse(value, size):
    pair = [value]
    for bit in reversed(range(size.bit_length() - 1)):
        here = combine_lse(pair)
        pair = [here, swap(here, "key", 1 << bit, size)]
    return pair


def summed_copies(pieces, n_head, n_query):
    steps = [("head", (2 << b) - 1, n_head) for b in reversed(range(n_head.bit_length() - 1))]
    steps += [("query", 1 << b, n_query) for b in range(n_query.bit_length() - 1)]
    steps = steps[:1] + steps[2:] + steps[1:2]
    for number in range(len(steps)):
        moved = []
        for i, piece in enumerate(pieces):
            moved.append(swap(piece, *steps[(number - i) % len(steps)]))
        pieces = [piece + other for piece, other in zip(pieces, moved)]
    return jnp.concatenate(pieces, axis=0)


def in_hbm(*values):
    return tuple(pltpu.with_memory_space_constraint(v, pltpu.HBM) for v in values)


def body(n_key, n_head, n_query, main_query, key_nope, key_rope, query_pos, key_pos, key_count,
         index_query, index_key, index_weight, row_cotangent):
    groups, rows, _ = main_query.shape
    keys = key_nope.shape[0]
    (main_query, key_nope, rope_t, query_pos, key_row, key_count, weight_t, cotangent, narrow,
     index_query) = in_hbm(
        main_query, key_nope, key_rope.T, query_pos, key_pos.reshape(1, keys), key_count,
        index_weight.T, row_cotangent.reshape(1, rows), index_key, index_query,
    )

    def gathered(value):
        if n_key == 4:
            near = swap(value, "key", 1, n_key)
            far = swap(value, "key", 2, n_key)
            across = swap(far, "key", 1, n_key)
            return [value, near, far, across]
        return list(lax.all_gather(value, "key"))

    lse, q, kk, bias, iq, wide, rank, live = main_stats(
        main_query, key_nope, rope_t, query_pos, key_row, key_count, index_query, narrow
    )
    lses = butterfly_lse(lse, n_key)
    logits, index_lse, wm = index_logits(iq, wide, weight_t, bias, live)
    index_lses = butterfly_lse(index_lse, n_key)
    iks = gathered(wide)

    if n_head == 4 and groups == 4:
        low, high = head_sums([2], q, kk, bias, live, lses, parts=2)
        low = swap(low, "head", 1, 4)
        high = swap(high, "head", 3, 4)
        up_lo, up_hi, down_lo, down_hi = head_sums([1, 3], q, kk, bias, live, lses, parts=2)
        up_lo = swap(up_lo, "head", 1, 4)
        down_hi = swap(down_hi, "head", 3, 4)
        up_hi = swap(up_hi + high, "head", 1, 4)
        down_lo = swap(down_lo + low, "head", 3, 4)
        own = head_sums([0], q, kk, bias, live, lses)[0]
        parts = [own, up_lo, up_hi, down_lo, down_hi]
    else:
        z = lax.axis_index("head")
        tiles = jnp.stack([head_sums([g], q, kk, bias, live, lses)[0] for g in range(groups)])
        tiles = tiles[jnp.bitwise_xor(jnp.arange(groups), z)]
        parts = [lax.psum_scatter(tiles, "head", scatter_dimension=0, tiled=True)[0]]

    spread = spread_matrix(rank)
    sg, *grad_key = index_grad_key(
        parts, index_lses, logits, wm, iq, bias, live, spread, cotangent
    )
    grad_key = summed_copies(grad_key, n_head, n_query)
    sgs = gathered(sg)
    carry = None
    for lo in range(0, n_key, 2):
        last = lo + 2 >= n_key
        carry = index_grad_query(
            n_key, sgs[lo : lo + 2], iks[lo : lo + 2], iq, weight_t,
            index_lses if last else [], carry,
        )
    grad_query, kl = carry
    return kl.reshape(rows), grad_query, grad_key


def solution(mesh):
    sizes = (mesh.shape["key"], mesh.shape["head"], mesh.shape["query"])

    def step(*args):
        return body(*sizes, *args)

    return jax.shard_map(
        step,
        mesh=mesh,
        in_specs=(
            P(None, "query", "head"),
            P("key", "head"),
            P("key", None),
            P(None, "query"),
            P("key"),
            P("key"),
            P(("head", "query"), None),
            P("key", None),
            P(("head", "query"), None),
            P(("head", "query")),
        ),
        out_specs=(P(("head", "query")), P(("head", "query"), "key"), P("key", None)),
        check_vma=False,
    )
```
